128 devices in a mesh: pair: 2 (over core), batch: 4 (over y), vocab: 16 (over x, z).
Axes of the slice: x: 4, y: 4, z: 4, core: 2. Of those that a mesh axis runs over, the one named last changes fastest.
Arguments:
- hidden: bfloat16 [2, 512, 8192], P('pair', 'batch', 'vocab'), may hold values from -120 to 120
- norm_gain: bfloat16 [8192], P('vocab'), may hold values from 0.099609375 to 1.8984375
- head_weight: bfloat16 [8192, 65536], P(('pair', 'batch'), 'vocab'), may hold values from -1 to 1
Outputs:
- guided_logprobs: float32 [512, 65536], P(('pair', 'batch'), 'vocab')
- cond_logprobs: float32 [512, 65536], P(('pair', 'batch'), 'vocab')
The draws below stay inside these ranges and needn't reach their ends.
All inputs are finite; a program needn't handle non-finite values.
Results may differ from the reference program's by a relative error of at most 0.007.
Values may be sent and summed in bfloat16 or wider, within the bound.
A program may use at most 128 MiB of HBM per device.

```python
import math
import jax
import jax.numpy as jnp
from jax import lax

D = 8192
B = 512
V = 65536


def shared_pattern(key):
    return jnp.clip(jax.random.normal(jax.random.fold_in(key, 4242), (D,), jnp.float32), -4.0, 4.0)


def draw_hidden(key, part):
    first, second, third = jax.random.split(jax.random.fold_in(key, 11), 3)
    base = jnp.clip(jax.random.normal(first, (2, B, D), jnp.float32), -4.0, 4.0)
    top_ramp = 3.0
    row_scale = jnp.exp(jax.random.uniform(second, (2, B, 1), jnp.float32, math.log(0.3), math.log(3.0)))
    ramp = jnp.exp(math.log(top_ramp) * jnp.arange(D, dtype=jnp.float32) / (D - 1))
    col_scale = ramp * jnp.exp(jax.random.uniform(third, (D,), jnp.float32, 0.0, math.log(3.3)))
    values = base * row_scale * col_scale
    pattern = shared_pattern(key)
    chosen = jnp.array([0, B // 3, 2 * B // 3], jnp.int32)
    values = values.at[0, chosen, :].set(jnp.broadcast_to(2.0 * pattern, (3, D)))
    return values.astype(jnp.bfloat16)


def draw_head_weight(key, part):
    scale = 3.0 / math.sqrt(D)
    first = jax.random.fold_in(key, 23)
    values = jnp.clip(jax.random.normal(first, (D, V), jnp.float32), -4.0, 4.0) * scale
    pattern = shared_pattern(key) * (80.0 / D)
    strengths = [2.5, 1.8, 1.3]
    for place in range(3):
        column = place * (V // 3) + 5
        values = values.at[:, column].set(strengths[place] * pattern)
        values = values.at[:, column + 1].set((strengths[place] - 0.02) * pattern)
    return values.astype(jnp.bfloat16)


def setup_inputs(seed: int = 0) -> dict:
    keys = jax.random.split(jax.random.key(seed), 4)
    return {
        "hidden": draw_hidden(jax.random.fold_in(keys[3], 71), 0),
        "norm_gain": jnp.clip(1.0 + 0.18 * jax.random.normal(keys[1], (D,), jnp.float32), 0.099609375, 1.8984375).astype(jnp.bfloat16),
        "head_weight": draw_head_weight(jax.random.fold_in(keys[3], 71), 0),
    }


EPS = 1e-05
GUIDE = 1.5

def normalized(scores):
    peak = lax.optimization_barrier(jnp.max(scores, axis=1, keepdims=True))
    total = lax.optimization_barrier(jnp.sum(jnp.exp(scores - peak), axis=1, keepdims=True))
    return scores - (peak + jnp.log(total))

def reference(hidden, norm_gain, head_weight):
    wide = hidden.astype(jnp.float32)
    meansq = lax.optimization_barrier(jnp.mean(wide * wide, axis=2, keepdims=True))
    features = (wide * lax.rsqrt(meansq + EPS) * norm_gain.astype(jnp.float32)).astype(jnp.bfloat16)
    cond = jnp.dot(features[0], head_weight, preferred_element_type=jnp.float32)
    uncond = jnp.dot(features[1], head_weight, preferred_element_type=jnp.float32)
    guided = GUIDE * cond + (1.0 - GUIDE) * uncond
    return (normalized(guided), normalized(cond))
```

```python
import jax
import jax.numpy as jnp
from jax import lax
from jax.sharding import PartitionSpec as P

D = 8192


EPS = 1e-05
GUIDE = 1.5


def on_device(hidden, norm_gain, head_weight):
    rows = lax.all_gather(hidden[0], "vocab", axis=1, tiled=True)
    gain = lax.all_gather(norm_gain, "vocab", axis=0, tiled=True)
    wide = rows.astype(jnp.float32)
    total_sq = jnp.sum(wide * wide, axis=1)
    scaled = wide * lax.rsqrt(total_sq / D + EPS)[:, None] * gain.astype(jnp.float32)[None, :]
    features = scaled.astype(jnp.bfloat16)
    blocks = lax.all_to_all(features, ("pair", "batch"), split_axis=1, concat_axis=0, tiled=True)
    groups = lax.axis_size("pair") * lax.axis_size("batch")
    width = blocks.shape[1]
    out_rows = blocks.shape[0] // (2 * groups)
    ordered = blocks.reshape(2, groups, out_rows, width).transpose(1, 0, 2, 3).reshape(-1, width)
    logits = lax.psum_scatter(
        jnp.dot(ordered, head_weight, preferred_element_type=jnp.float32),
        ("pair", "batch"),
        scatter_dimension=0,
        tiled=True,
    )
    cond = logits[:out_rows]
    uncond = logits[out_rows:]
    guided = GUIDE * cond + (1.0 - GUIDE) * uncond
    peak_c = jnp.max(cond, axis=1)
    peak_g = jnp.max(guided, axis=1)
    local_c = jnp.sum(jnp.exp(cond - peak_c[:, None]), axis=1)
    local_g = jnp.sum(jnp.exp(guided - peak_g[:, None]), axis=1)
    stats = jnp.stack([peak_c, local_c, peak_g, local_g])
    every = lax.all_gather(stats, "vocab", axis=0)
    top_c = jnp.max(every[:, 0], axis=0)
    top_g = jnp.max(every[:, 2], axis=0)
    total_c = jnp.sum(every[:, 1] * jnp.exp(every[:, 0] - top_c[None, :]), axis=0)
    total_g = jnp.sum(every[:, 3] * jnp.exp(every[:, 2] - top_g[None, :]), axis=0)
    cond_out = cond - (top_c + jnp.log(total_c))[:, None]
    guided_out = guided - (top_g + jnp.log(total_g))[:, None]
    return (guided_out, cond_out)


def solution(mesh):
    in_specs = (P("pair", "batch", "vocab"), P("vocab"), P(("pair", "batch"), "vocab"))
    out_specs = (P(("pair", "batch"), "vocab"), P(("pair", "batch"), "vocab"))
    return jax.shard_map(
        on_device, mesh=mesh, in_specs=in_specs, out_specs=out_specs, check_vma=False
    )
```

```python
import jax
import jax.numpy as jnp
from jax import lax
from jax.sharding import PartitionSpec as P

D = 8192


EPS = 1e-05
GUIDE = 1.5


def on_device(hidden, norm_gain, head_weight):
    local_rows = hidden.shape[1]
    packed = jnp.concatenate([hidden[0], norm_gain[None, :]], axis=0)
    gathered = lax.all_gather(packed, "vocab", axis=1, tiled=True)
    wide = gathered[:local_rows].astype(jnp.float32)
    gain = gathered[local_rows]
    total_sq = jnp.sum(wide * wide, axis=1)
    scaled = wide * lax.rsqrt(total_sq / D + EPS)[:, None] * gain.astype(jnp.float32)[None, :]
    features = scaled.astype(jnp.bfloat16)
    blocks = lax.all_to_all(features, ("pair", "batch"), split_axis=1, concat_axis=0, tiled=True)
    groups = lax.axis_size("pair") * lax.axis_size("batch")
    width = blocks.shape[1]
    out_rows = blocks.shape[0] // (2 * groups)
    ordered = blocks.reshape(2, groups, out_rows, width).transpose(1, 0, 2, 3).reshape(-1, width)
    partial = jnp.dot(ordered, head_weight, preferred_element_type=jnp.float32)
    half = lax.psum_scatter(partial, "pair", scatter_dimension=0, tiled=True)
    logits = lax.psum_scatter(half, "batch", scatter_dimension=0, tiled=True)
    cond = logits[:out_rows]
    uncond = logits[out_rows:]
    guided = GUIDE * cond + (1.0 - GUIDE) * uncond
    peak_c = jnp.max(cond, axis=1)
    peak_g = jnp.max(guided, axis=1)
    local_c = jnp.sum(jnp.exp(cond - peak_c[:, None]), axis=1)
    local_g = jnp.sum(jnp.exp(guided - peak_g[:, None]), axis=1)
    stats = jnp.stack([peak_c, local_c, peak_g, local_g])
    every = lax.all_gather(stats, "vocab", axis=0)
    top_c = jnp.max(every[:, 0], axis=0)
    top_g = jnp.max(every[:, 2], axis=0)
    total_c = jnp.sum(every[:, 1] * jnp.exp(every[:, 0] - top_c[None, :]), axis=0)
    total_g = jnp.sum(every[:, 3] * jnp.exp(every[:, 2] - top_g[None, :]), axis=0)
    cond_out = cond - (top_c + jnp.log(total_c))[:, None]
    guided_out = guided - (top_g + jnp.log(total_g))[:, None]
    return (guided_out, cond_out)


def solution(mesh):
    in_specs = (P("pair", "batch", "vocab"), P("vocab"), P(("pair", "batch"), "vocab"))
    out_specs = (P(("pair", "batch"), "vocab"), P(("pair", "batch"), "vocab"))
    return jax.shard_map(
        on_device, mesh=mesh, in_specs=in_specs, out_specs=out_specs, check_vma=False
    )
```

```python
import jax
import jax.numpy as jnp
from jax import lax
from jax.sharding import PartitionSpec as P

D = 8192


EPS = 1e-05
GUIDE = 1.5
CHUNKS = 2


def on_device(hidden, norm_gain, head_weight):
    local_rows = hidden.shape[1]
    pad = jnp.zeros((15, norm_gain.shape[0]), hidden.dtype)
    packed = jnp.concatenate([hidden[0], norm_gain[None, :], pad], axis=0)
    gathered = lax.all_gather(packed, "vocab", axis=1, tiled=True)
    wide = gathered[:local_rows].astype(jnp.float32)
    gain = gathered[local_rows]
    total_sq = jnp.sum(wide * wide, axis=1)
    scaled = wide * lax.rsqrt(total_sq / D + EPS)[:, None] * gain.astype(jnp.float32)[None, :]
    features = scaled.astype(jnp.bfloat16)
    blocks = lax.all_to_all(features, ("pair", "batch"), split_axis=1, concat_axis=0, tiled=True)
    groups = lax.axis_size("pair") * lax.axis_size("batch")
    width = blocks.shape[1]
    out_rows = blocks.shape[0] // (2 * groups)
    ordered = blocks.reshape(2, groups, out_rows, width).transpose(1, 0, 2, 3).reshape(-1, width)
    half_rows = ordered.shape[0] // 2
    me = lax.axis_index("pair")
    mine = lax.dynamic_slice_in_dim(ordered, me * half_rows, half_rows, axis=0)
    theirs = lax.dynamic_slice_in_dim(ordered, (1 - me) * half_rows, half_rows, axis=0)
    cols = head_weight.shape[1]
    step = cols // CHUNKS
    pieces = []
    for j in range(CHUNKS):
        w = head_weight[:, j * step:(j + 1) * step]
        sent = jnp.dot(theirs, w, preferred_element_type=jnp.float32)
        got = lax.ppermute(sent, "pair", [(0, 1), (1, 0)])
        kept = jnp.dot(mine, w, preferred_element_type=jnp.float32)
        pieces.append(lax.psum_scatter(kept + got, "batch", scatter_dimension=0, tiled=True))
    logits = jnp.concatenate(pieces, axis=1)
    cond = logits[:out_rows]
    uncond = logits[out_rows:]
    guided = GUIDE * cond + (1.0 - GUIDE) * uncond
    peak_c = jnp.max(cond, axis=1)
    peak_g = jnp.max(guided, axis=1)
    local_c = jnp.sum(jnp.exp(cond - peak_c[:, None]), axis=1)
    local_g = jnp.sum(jnp.exp(guided - peak_g[:, None]), axis=1)
    stats = jnp.stack([peak_c, local_c, peak_g, local_g])
    every = lax.all_gather(stats, "vocab", axis=0)
    top_c = jnp.max(every[:, 0], axis=0)
    top_g = jnp.max(every[:, 2], axis=0)
    total_c = jnp.sum(every[:, 1] * jnp.exp(every[:, 0] - top_c[None, :]), axis=0)
    total_g = jnp.sum(every[:, 3] * jnp.exp(every[:, 2] - top_g[None, :]), axis=0)
    cond_out = cond - (top_c + jnp.log(total_c))[:, None]
    guided_out = guided - (top_g + jnp.log(total_g))[:, None]
    return (guided_out, cond_out)


def solution(mesh):
    in_specs = (P("pair", "batch", "vocab"), P("vocab"), P(("pair", "batch"), "vocab"))
    out_specs = (P(("pair", "batch"), "vocab"), P(("pair", "batch"), "vocab"))
    return jax.shard_map(
        on_device, mesh=mesh, in_specs=in_specs, out_specs=out_specs, check_vma=False
    )
```

```python
import functools

import jax
import jax.numpy as jnp
from jax import lax
from jax.experimental import pallas as pl
from jax.experimental.pallas import tpu as pltpu
from jax.sharding import PartitionSpec as P

MESH = pl.DeviceIdType.MESH

EPS = 1e-05
GUIDE = 1.5
CHUNKS = 2
SPARE = 16


def dispatch_kernel(npair, nb, nv, span, src_ref, out_ref, send_sems, recv_sems):
    beta = lax.axis_index("pair")
    b = lax.axis_index("batch")
    v = lax.axis_index("vocab")
    groups = npair * nb
    mine = beta * nb + b
    q = v // span
    tp = q // nb
    tb = q % nb
    slot = mine * span + v % span
    d = q - mine
    own = 1 - (d * d + groups * groups - 1) // (groups * groups)

    def sources(s):
        bs = s // (nb * span)
        bbs = (s // span) % nb
        sv = mine * span + s % span
        return bs, bbs, sv

    barrier = pltpu.get_barrier_semaphore()
    for w in range(nv):
        @pl.when(jnp.logical_not((tp == beta) & (tb == b) & (v == w)))
        def _():
            pl.semaphore_signal(barrier, inc=1, device_id=(tp, tb, w), device_id_type=MESH)
    for s in range(nv):
        bs, bbs, sv = sources(s)

        @pl.when(jnp.logical_not((bs == beta) & (bbs == b) & (sv == v)))
        def _():
            pl.semaphore_signal(barrier, inc=1, device_id=(bs, bbs, sv), device_id_type=MESH)
    pl.semaphore_wait(barrier, 2 * (nv - own))

    def remote(w):
        return pltpu.make_async_remote_copy(
            src_ref=src_ref,
            dst_ref=out_ref.at[slot],
            send_sem=send_sems.at[w],
            recv_sem=recv_sems.at[slot],
            device_id=(tp, tb, w),
            device_id_type=MESH,
        )

    for w in range(nv):
        here = (tp == beta) & (tb == b) & (v == w)

        @pl.when(jnp.logical_not(here))
        def _():
            remote(w).start()

        @pl.when(here)
        def _():
            pltpu.make_async_copy(src_ref, out_ref.at[slot], recv_sems.at[slot]).start()

    for w in range(nv):
        here = (tp == beta) & (tb == b) & (v == w)

        @pl.when(jnp.logical_not(here))
        def _():
            remote(w).wait_send()

    for s in range(nv):
        bs, bbs, sv = sources(s)
        here = (bs == beta) & (bbs == b) & (sv == v)

        @pl.when(jnp.logical_not(here))
        def _():
            pltpu.make_async_remote_copy(
                src_ref=src_ref,
                dst_ref=out_ref.at[s],
                send_sem=send_sems.at[0],
                recv_sem=recv_sems.at[s],
                device_id=(bs, bbs, sv),
                device_id_type=MESH,
            ).wait_recv()

        @pl.when(here)
        def _():
            pltpu.make_async_copy(src_ref, out_ref.at[s], recv_sems.at[s]).wait()


def dispatch(block, npair, nb, nv):
    span = nv // (npair * nb)
    size = block.size * block.dtype.itemsize
    return pl.pallas_call(
        functools.partial(dispatch_kernel, npair, nb, nv, span),
        out_shape=jax.ShapeDtypeStruct((nv,) + block.shape, block.dtype),
        in_specs=[pl.BlockSpec(memory_space=pltpu.VMEM)],
        out_specs=pl.BlockSpec(memory_space=pltpu.VMEM),
        scratch_shapes=[pltpu.SemaphoreType.DMA((nv,)), pltpu.SemaphoreType.DMA((nv,))],
        compiler_params=pltpu.CompilerParams(collective_id=0, has_side_effects=True),
        cost_estimate=pl.CostEstimate(flops=0, transcendentals=0, bytes_accessed=2 * nv * size),
    )(block)


def on_device(npair, nb, nv, hidden, norm_gain, head_weight):
    groups = npair * nb
    span = nv // groups
    local_rows, width = hidden.shape[1], hidden.shape[2]
    total_d = width * nv
    pad = jnp.zeros((SPARE - 1, width), hidden.dtype)
    block = jnp.concatenate([hidden[0], norm_gain[None, :], pad], axis=0)
    got = dispatch(block, npair, nb, nv)
    raw = got[:, :local_rows, :].reshape(npair, nb, span, local_rows, width)
    raw = raw.transpose(0, 1, 3, 2, 4).reshape(npair * nb * local_rows, span * width)
    gain = got[:span, local_rows, :].reshape(span * width)
    wide = raw.astype(jnp.float32)
    sq = jnp.sum(wide * wide, axis=1)
    feats = (wide * gain.astype(jnp.float32)[None, :]).astype(jnp.bfloat16)
    rows_all = feats.shape[0] // npair
    out_rows = rows_all // groups
    ordered = feats.reshape(npair, groups, out_rows, -1).transpose(1, 0, 2, 3).reshape(npair * rows_all, -1)
    sq_ordered = sq.reshape(npair, groups, out_rows).transpose(1, 0, 2).reshape(npair * rows_all)
    half_rows = ordered.shape[0] // 2
    me = lax.axis_index("pair")
    mine = lax.dynamic_slice_in_dim(ordered, me * half_rows, half_rows, axis=0)
    theirs = lax.dynamic_slice_in_dim(ordered, (1 - me) * half_rows, half_rows, axis=0)
    sq_mine = lax.dynamic_slice_in_dim(sq_ordered, me * half_rows, half_rows, axis=0)
    sq_theirs = lax.dynamic_slice_in_dim(sq_ordered, (1 - me) * half_rows, half_rows, axis=0)
    lanes = 128
    extra_mine = jnp.zeros((half_rows, lanes), jnp.float32).at[:, 0].set(sq_mine)
    extra_theirs = jnp.zeros((half_rows, lanes), jnp.float32).at[:, 0].set(sq_theirs)
    cols = head_weight.shape[1]
    step = cols // CHUNKS
    pieces = []
    for j in range(CHUNKS):
        w = head_weight[:, j * step:(j + 1) * step]
        sent = jnp.dot(theirs, w, preferred_element_type=jnp.float32)
        kept = jnp.dot(mine, w, preferred_element_type=jnp.float32)
        if j == 0:
            sent = jnp.concatenate([sent, extra_theirs], axis=1)
            kept = jnp.concatenate([kept, extra_mine], axis=1)
        got_half = lax.ppermute(sent, "pair", [(0, 1), (1, 0)])
        pieces.append(lax.psum_scatter(kept + got_half, "batch", scatter_dimension=0, tiled=True))
    total_sq = pieces[0][:, step]
    pieces[0] = pieces[0][:, :step]
    scale = lax.rsqrt(total_sq / total_d + EPS)
    logits = jnp.concatenate(pieces, axis=1) * scale[:, None]
    cond = logits[:out_rows]
    uncond = logits[out_rows:]
    guided = GUIDE * cond + (1.0 - GUIDE) * uncond
    peak_c = jnp.max(cond, axis=1)
    peak_g = jnp.max(guided, axis=1)
    local_c = jnp.sum(jnp.exp(cond - peak_c[:, None]), axis=1)
    local_g = jnp.sum(jnp.exp(guided - peak_g[:, None]), axis=1)
    stats = jnp.stack([peak_c, local_c, peak_g, local_g])
    every = lax.all_gather(stats, "vocab", axis=0)
    top_c = jnp.max(every[:, 0], axis=0)
    top_g = jnp.max(every[:, 2], axis=0)
    total_c = jnp.sum(every[:, 1] * jnp.exp(every[:, 0] - top_c[None, :]), axis=0)
    total_g = jnp.sum(every[:, 3] * jnp.exp(every[:, 2] - top_g[None, :]), axis=0)
    cond_out = cond - (top_c + jnp.log(total_c))[:, None]
    guided_out = guided - (top_g + jnp.log(total_g))[:, None]
    return (guided_out, cond_out)


def solution(mesh):
    npair, nb, nv = mesh.shape["pair"], mesh.shape["batch"], mesh.shape["vocab"]
    in_specs = (P("pair", "batch", "vocab"), P("vocab"), P(("pair", "batch"), "vocab"))
    out_specs = (P(("pair", "batch"), "vocab"), P(("pair", "batch"), "vocab"))
    return jax.shard_map(
        functools.partial(on_device, npair, nb, nv),
        mesh=mesh, in_specs=in_specs, out_specs=out_specs, check_vma=False,
    )
```

```python
import functools

import jax
import jax.numpy as jnp
from jax import lax
from jax.experimental import pallas as pl
from jax.experimental.pallas import tpu as pltpu
from jax.sharding import PartitionSpec as P

MESH = pl.DeviceIdType.MESH

EPS = 1e-05
GUIDE = 1.5
CHUNKS = 2
SPARE = 16


def dispatch_kernel(npair, nb, nv, span, src_ref, out_ref, send_sems, recv_sems):
    beta = lax.axis_index("pair")
    b = lax.axis_index("batch")
    v = lax.axis_index("vocab")
    groups = npair * nb
    mine = beta * nb + b
    q = v // span
    tp = q // nb
    tb = q % nb
    slot = mine * span + v % span
    d = q - mine
    own = 1 - (d * d + groups * groups - 1) // (groups * groups)

    def sources(s):
        bs = s // (nb * span)
        bbs = (s // span) % nb
        sv = mine * span + s % span
        return bs, bbs, sv

    barrier = pltpu.get_barrier_semaphore()
    for w in range(nv):
        @pl.when(jnp.logical_not((tp == beta) & (tb == b) & (v == w)))
        def _():
            pl.semaphore_signal(barrier, inc=1, device_id=(tp, tb, w), device_id_type=MESH)
    for s in range(nv):
        bs, bbs, sv = sources(s)

        @pl.when(jnp.logical_not((bs == beta) & (bbs == b) & (sv == v)))
        def _():
            pl.semaphore_signal(barrier, inc=1, device_id=(bs, bbs, sv), device_id_type=MESH)
    pl.semaphore_wait(barrier, 2 * (nv - own))

    def remote(w):
        return pltpu.make_async_remote_copy(
            src_ref=src_ref,
            dst_ref=out_ref.at[slot],
            send_sem=send_sems.at[w],
            recv_sem=recv_sems.at[slot],
            device_id=(tp, tb, w),
            device_id_type=MESH,
        )

    for w in range(nv):
        here = (tp == beta) & (tb == b) & (v == w)

        @pl.when(jnp.logical_not(here))
        def _():
            remote(w).start()

        @pl.when(here)
        def _():
            pltpu.make_async_copy(src_ref, out_ref.at[slot], recv_sems.at[slot]).start()

    for w in range(nv):
        here = (tp == beta) & (tb == b) & (v == w)

        @pl.when(jnp.logical_not(here))
        def _():
            remote(w).wait_send()

    for s in range(nv):
        bs, bbs, sv = sources(s)
        here = (bs == beta) & (bbs == b) & (sv == v)

        @pl.when(jnp.logical_not(here))
        def _():
            pltpu.make_async_remote_copy(
                src_ref=src_ref,
                dst_ref=out_ref.at[s],
                send_sem=send_sems.at[0],
                recv_sem=recv_sems.at[s],
                device_id=(bs, bbs, sv),
                device_id_type=MESH,
            ).wait_recv()

        @pl.when(here)
        def _():
            pltpu.make_async_copy(src_ref, out_ref.at[s], recv_sems.at[s]).wait()


def dispatch(block, npair, nb, nv):
    span = nv // (npair * nb)
    size = block.size * block.dtype.itemsize
    return pl.pallas_call(
        functools.partial(dispatch_kernel, npair, nb, nv, span),
        out_shape=jax.ShapeDtypeStruct((nv,) + block.shape, block.dtype),
        in_specs=[pl.BlockSpec(memory_space=pltpu.VMEM)],
        out_specs=pl.BlockSpec(memory_space=pltpu.VMEM),
        scratch_shapes=[pltpu.SemaphoreType.DMA((nv,)), pltpu.SemaphoreType.DMA((nv,))],
        compiler_params=pltpu.CompilerParams(collective_id=0, has_side_effects=True),
        cost_estimate=pl.CostEstimate(flops=0, transcendentals=0, bytes_accessed=2 * nv * size),
    )(block)


def on_device(npair, nb, nv, hidden, norm_gain, head_weight):
    groups = npair * nb
    span = nv // groups
    local_rows, width = hidden.shape[1], hidden.shape[2]
    total_d = width * nv
    pad = jnp.zeros((SPARE - 1, width), hidden.dtype)
    block = jnp.concatenate([hidden[0], norm_gain[None, :], pad], axis=0)
    got = dispatch(block, npair, nb, nv)
    half = local_rows // 2
    raw = got[:, :local_rows, :].reshape(npair, nb, span, 2, half, width)
    raw = raw.transpose(1, 3, 0, 4, 2, 5)
    gain = got[:span, local_rows, :].reshape(span, width)
    wide = raw.astype(jnp.float32)
    sq = jnp.sum(wide * wide, axis=(4, 5)).reshape(groups, npair * half)
    feats = (wide * gain.astype(jnp.float32)).astype(jnp.bfloat16)
    ordered = feats.reshape(groups * npair * half, span * width)
    out_rows = half
    me = lax.axis_index("pair")
    sq_mine = lax.dynamic_slice_in_dim(sq, me * nb, nb, axis=0)
    sq_theirs = lax.dynamic_slice_in_dim(sq, (1 - me) * nb, nb, axis=0)
    sq_half = sq_mine + lax.ppermute(sq_theirs, "pair", [(0, 1), (1, 0)])
    total_sq = lax.psum_scatter(sq_half, "batch", scatter_dimension=0, tiled=True).reshape(npair * half)
    half_rows = ordered.shape[0] // 2
    mine = lax.dynamic_slice_in_dim(ordered, me * half_rows, half_rows, axis=0)
    theirs = lax.dynamic_slice_in_dim(ordered, (1 - me) * half_rows, half_rows, axis=0)
    cols = head_weight.shape[1]
    step = cols // CHUNKS
    pieces = []
    for j in range(CHUNKS):
        w = head_weight[:, j * step:(j + 1) * step]
        sent = jnp.dot(theirs, w, preferred_element_type=jnp.float32)
        kept = jnp.dot(mine, w, preferred_element_type=jnp.float32)
        got_half = lax.ppermute(sent, "pair", [(0, 1), (1, 0)])
        pieces.append(lax.psum_scatter(kept + got_half, "batch", scatter_dimension=0, tiled=True))
    scale = lax.rsqrt(total_sq / total_d + EPS)
    logits = jnp.concatenate(pieces, axis=1) * scale[:, None]
    cond = logits[:out_rows]
    uncond = logits[out_rows:]
    guided = GUIDE * cond + (1.0 - GUIDE) * uncond
    peak_c = jnp.max(cond, axis=1)
    peak_g = jnp.max(guided, axis=1)
    local_c = jnp.sum(jnp.exp(cond - peak_c[:, None]), axis=1)
    local_g = jnp.sum(jnp.exp(guided - peak_g[:, None]), axis=1)
    stats = jnp.stack([peak_c, local_c, peak_g, local_g])
    every = lax.all_gather(stats, "vocab", axis=0)
    top_c = jnp.max(every[:, 0], axis=0)
    top_g = jnp.max(every[:, 2], axis=0)
    total_c = jnp.sum(every[:, 1] * jnp.exp(every[:, 0] - top_c[None, :]), axis=0)
    total_g = jnp.sum(every[:, 3] * jnp.exp(every[:, 2] - top_g[None, :]), axis=0)
    cond_out = cond - (top_c + jnp.log(total_c))[:, None]
    guided_out = guided - (top_g + jnp.log(total_g))[:, None]
    return (guided_out, cond_out)


def solution(mesh):
    npair, nb, nv = mesh.shape["pair"], mesh.shape["batch"], mesh.shape["vocab"]
    in_specs = (P("pair", "batch", "vocab"), P("vocab"), P(("pair", "batch"), "vocab"))
    out_specs = (P(("pair", "batch"), "vocab"), P(("pair", "batch"), "vocab"))
    return jax.shard_map(
        functools.partial(on_device, npair, nb, nv),
        mesh=mesh, in_specs=in_specs, out_specs=out_specs, check_vma=False,
    )
```

```python
import functools

import jax
import jax.numpy as jnp
from jax import lax
from jax.experimental import pallas as pl
from jax.experimental.pallas import tpu as pltpu
from jax.sharding import PartitionSpec as P

MESH = pl.DeviceIdType.MESH

EPS = 1e-05
GUIDE = 1.5
CHUNKS = 2


def dispatch_kernel(npair, nb, nv, span, src_ref, out_ref, send_sems, recv_sems):
    beta = lax.axis_index("pair")
    b = lax.axis_index("batch")
    v = lax.axis_index("vocab")
    groups = npair * nb
    mine = beta * nb + b
    q = v // span
    tp = q // nb
    tb = q % nb
    slot = mine * span + v % span
    d = q - mine
    own = 1 - (d * d + groups * groups - 1) // (groups * groups)

    def sources(s):
        bs = s // (nb * span)
        bbs = (s // span) % nb
        sv = mine * span + s % span
        return bs, bbs, sv

    barrier = pltpu.get_barrier_semaphore()
    for w in range(nv):
        @pl.when(jnp.logical_not((tp == beta) & (tb == b) & (v == w)))
        def _():
            pl.semaphore_signal(barrier, inc=1, device_id=(tp, tb, w), device_id_type=MESH)
    for s in range(nv):
        bs, bbs, sv = sources(s)

        @pl.when(jnp.logical_not((bs == beta) & (bbs == b) & (sv == v)))
        def _():
            pl.semaphore_signal(barrier, inc=1, device_id=(bs, bbs, sv), device_id_type=MESH)
    pl.semaphore_wait(barrier, 2 * (nv - own))

    def remote(w):
        return pltpu.make_async_remote_copy(
            src_ref=src_ref,
            dst_ref=out_ref.at[slot],
            send_sem=send_sems.at[w],
            recv_sem=recv_sems.at[slot],
            device_id=(tp, tb, w),
            device_id_type=MESH,
        )

    for w in range(nv):
        here = (tp == beta) & (tb == b) & (v == w)

        @pl.when(jnp.logical_not(here))
        def _():
            remote(w).start()

        @pl.when(here)
        def _():
            pltpu.make_async_copy(src_ref, out_ref.at[slot], recv_sems.at[slot]).start()

    for w in range(nv):
        here = (tp == beta) & (tb == b) & (v == w)

        @pl.when(jnp.logical_not(here))
        def _():
            remote(w).wait_send()

    for s in range(nv):
        bs, bbs, sv = sources(s)
        here = (bs == beta) & (bbs == b) & (sv == v)

        @pl.when(jnp.logical_not(here))
        def _():
            pltpu.make_async_remote_copy(
                src_ref=src_ref,
                dst_ref=out_ref.at[s],
                send_sem=send_sems.at[0],
                recv_sem=recv_sems.at[s],
                device_id=(bs, bbs, sv),
                device_id_type=MESH,
            ).wait_recv()

        @pl.when(here)
        def _():
            pltpu.make_async_copy(src_ref, out_ref.at[s], recv_sems.at[s]).wait()


def dispatch(block, npair, nb, nv):
    span = nv // (npair * nb)
    size = block.size * block.dtype.itemsize
    return pl.pallas_call(
        functools.partial(dispatch_kernel, npair, nb, nv, span),
        out_shape=jax.ShapeDtypeStruct((nv,) + block.shape, block.dtype),
        in_specs=[pl.BlockSpec(memory_space=pltpu.VMEM)],
        out_specs=pl.BlockSpec(memory_space=pltpu.VMEM),
        scratch_shapes=[pltpu.SemaphoreType.DMA((nv,)), pltpu.SemaphoreType.DMA((nv,))],
        compiler_params=pltpu.CompilerParams(collective_id=0, has_side_effects=True),
        cost_estimate=pl.CostEstimate(flops=0, transcendentals=0, bytes_accessed=2 * nv * size),
    )(block)


def gather_kernel(nv, src_ref, out_ref, send_sems, recv_sems):
    beta = lax.axis_index("pair")
    b = lax.axis_index("batch")
    v = lax.axis_index("vocab")
    barrier = pltpu.get_barrier_semaphore()
    for w in range(nv):
        @pl.when(v != w)
        def _():
            pl.semaphore_signal(barrier, inc=1, device_id=(beta, b, w), device_id_type=MESH)
    pl.semaphore_wait(barrier, nv - 1)

    def remote(w, s):
        return pltpu.make_async_remote_copy(
            src_ref=src_ref,
            dst_ref=out_ref.at[s],
            send_sem=send_sems.at[w],
            recv_sem=recv_sems.at[s],
            device_id=(beta, b, w),
            device_id_type=MESH,
        )

    for w in range(nv):
        @pl.when(v != w)
        def _():
            remote(w, v).start()

    pltpu.make_async_copy(src_ref, out_ref.at[v], recv_sems.at[v]).start()
    for w in range(nv):
        @pl.when(v != w)
        def _():
            remote(w, v).wait_send()
    for s in range(nv):
        @pl.when(v != s)
        def _():
            remote(s, s).wait_recv()
    pltpu.make_async_copy(src_ref, out_ref.at[v], recv_sems.at[v]).wait()


def vocab_gather(block, nv, cid):
    size = block.size * block.dtype.itemsize
    return pl.pallas_call(
        functools.partial(gather_kernel, nv),
        out_shape=jax.ShapeDtypeStruct((nv,) + block.shape, block.dtype),
        in_specs=[pl.BlockSpec(memory_space=pltpu.VMEM)],
        out_specs=pl.BlockSpec(memory_space=pltpu.VMEM),
        scratch_shapes=[pltpu.SemaphoreType.DMA((nv,)), pltpu.SemaphoreType.DMA((nv,))],
        compiler_params=pltpu.CompilerParams(collective_id=cid, has_side_effects=True),
        cost_estimate=pl.CostEstimate(flops=0, transcendentals=0, bytes_accessed=2 * nv * size),
    )(block)


def on_device(npair, nb, nv, hidden, norm_gain, head_weight):
    groups = npair * nb
    span = nv // groups
    local_rows, width = hidden.shape[1], hidden.shape[2]
    total_d = width * nv
    wide = hidden[0].astype(jnp.float32)
    part = jnp.sum(wide * wide, axis=1)
    lanes = 128
    part_block = jnp.zeros((8, local_rows), jnp.float32).at[0].set(part)
    parts = vocab_gather(part_block, nv, 1)
    meansq = jnp.sum(parts[:, 0, :], axis=0) / total_d
    scaled = wide * lax.rsqrt(meansq + EPS)[:, None] * norm_gain.astype(jnp.float32)[None, :]
    features = scaled.astype(jnp.bfloat16)
    got = dispatch(features, npair, nb, nv)
    half = local_rows // 2
    raw = got.reshape(npair, nb, span, 2, half, width).transpose(1, 3, 0, 4, 2, 5)
    ordered = raw.reshape(groups * npair * half, span * width)
    out_rows = half
    me = lax.axis_index("pair")
    half_rows = ordered.shape[0] // 2
    mine = lax.dynamic_slice_in_dim(ordered, me * half_rows, half_rows, axis=0)
    theirs = lax.dynamic_slice_in_dim(ordered, (1 - me) * half_rows, half_rows, axis=0)
    cols = head_weight.shape[1]
    step = cols // CHUNKS
    pieces = []
    for j in range(CHUNKS):
        w = head_weight[:, j * step:(j + 1) * step]
        sent = jnp.dot(theirs, w, preferred_element_type=jnp.float32)
        kept = jnp.dot(mine, w, preferred_element_type=jnp.float32)
        got_half = lax.ppermute(sent, "pair", [(0, 1), (1, 0)])
        pieces.append(lax.psum_scatter(kept + got_half, "batch", scatter_dimension=0, tiled=True))
    logits = jnp.concatenate(pieces, axis=1)
    cond = logits[:out_rows]
    uncond = logits[out_rows:]
    guided = GUIDE * cond + (1.0 - GUIDE) * uncond
    peak_c = jnp.max(cond, axis=1)
    peak_g = jnp.max(guided, axis=1)
    local_c = jnp.sum(jnp.exp(cond - peak_c[:, None]), axis=1)
    local_g = jnp.sum(jnp.exp(guided - peak_g[:, None]), axis=1)
    stats = jnp.zeros((8, lanes), jnp.float32).at[:4, :out_rows].set(
        jnp.stack([peak_c, local_c, peak_g, local_g]))
    every = vocab_gather(stats, nv, 2)[:, :4, :out_rows]
    top_c = jnp.max(every[:, 0], axis=0)
    top_g = jnp.max(every[:, 2], axis=0)
    total_c = jnp.sum(every[:, 1] * jnp.exp(every[:, 0] - top_c[None, :]), axis=0)
    total_g = jnp.sum(every[:, 3] * jnp.exp(every[:, 2] - top_g[None, :]), axis=0)
    cond_out = cond - (top_c + jnp.log(total_c))[:, None]
    guided_out = guided - (top_g + jnp.log(total_g))[:, None]
    return (guided_out, cond_out)


def solution(mesh):
    npair, nb, nv = mesh.shape["pair"], mesh.shape["batch"], mesh.shape["vocab"]
    in_specs = (P("pair", "batch", "vocab"), P("vocab"), P(("pair", "batch"), "vocab"))
    out_specs = (P(("pair", "batch"), "vocab"), P(("pair", "batch"), "vocab"))
    return jax.shard_map(
        functools.partial(on_device, npair, nb, nv),
        mesh=mesh, in_specs=in_specs, out_specs=out_specs, check_vma=False,
    )
```

```python
import functools

import jax
import jax.numpy as jnp
from jax import lax
from jax.experimental import pallas as pl
from jax.experimental.pallas import tpu as pltpu
from jax.sharding import PartitionSpec as P

MESH = pl.DeviceIdType.MESH

EPS = 1e-05
GUIDE = 1.5
CHUNKS = 2


def dispatch_kernel(npair, nb, nv, span, src_ref, out_ref, send_sems, recv_sems):
    beta = lax.axis_index("pair")
    b = lax.axis_index("batch")
    v = lax.axis_index("vocab")
    groups = npair * nb
    mine = beta * nb + b
    q = v // span
    tp = q // nb
    tb = q % nb
    slot = mine * span + v % span
    d = q - mine
    own = 1 - (d * d + groups * groups - 1) // (groups * groups)

    def sources(s):
        bs = s // (nb * span)
        bbs = (s // span) % nb
        sv = mine * span + s % span
        return bs, bbs, sv

    barrier = pltpu.get_barrier_semaphore()
    for w in range(nv):
        @pl.when(jnp.logical_not((tp == beta) & (tb == b) & (v == w)))
        def _():
            pl.semaphore_signal(barrier, inc=1, device_id=(tp, tb, w), device_id_type=MESH)
    for s in range(nv):
        bs, bbs, sv = sources(s)

        @pl.when(jnp.logical_not((bs == beta) & (bbs == b) & (sv == v)))
        def _():
            pl.semaphore_signal(barrier, inc=1, device_id=(bs, bbs, sv), device_id_type=MESH)
    pl.semaphore_wait(barrier, 2 * (nv - own))

    def remote(k):
        return pltpu.make_async_remote_copy(
            src_ref=src_ref,
            dst_ref=out_ref.at[slot],
            send_sem=send_sems.at[k],
            recv_sem=recv_sems.at[slot],
            device_id=(tp, tb, (k + slot) % nv),
            device_id_type=MESH,
        )

    for k in range(nv):
        here = (tp == beta) & (tb == b) & (v == (k + slot) % nv)

        @pl.when(jnp.logical_not(here))
        def _():
            remote(k).start()

        @pl.when(here)
        def _():
            pltpu.make_async_copy(src_ref, out_ref.at[slot], recv_sems.at[slot]).start()

    for k in range(nv):
        here = (tp == beta) & (tb == b) & (v == (k + slot) % nv)

        @pl.when(jnp.logical_not(here))
        def _():
            remote(k).wait_send()

    for s in range(nv):
        bs, bbs, sv = sources(s)
        here = (bs == beta) & (bbs == b) & (sv == v)

        @pl.when(jnp.logical_not(here))
        def _():
            pltpu.make_async_remote_copy(
                src_ref=src_ref,
                dst_ref=out_ref.at[s],
                send_sem=send_sems.at[0],
                recv_sem=recv_sems.at[s],
                device_id=(bs, bbs, sv),
                device_id_type=MESH,
            ).wait_recv()

        @pl.when(here)
        def _():
            pltpu.make_async_copy(src_ref, out_ref.at[s], recv_sems.at[s]).wait()


def dispatch(block, npair, nb, nv):
    span = nv // (npair * nb)
    size = block.size * block.dtype.itemsize
    return pl.pallas_call(
        functools.partial(dispatch_kernel, npair, nb, nv, span),
        out_shape=jax.ShapeDtypeStruct((nv,) + block.shape, block.dtype),
        in_specs=[pl.BlockSpec(memory_space=pltpu.VMEM)],
        out_specs=pl.BlockSpec(memory_space=pltpu.VMEM),
        scratch_shapes=[pltpu.SemaphoreType.DMA((nv,)), pltpu.SemaphoreType.DMA((nv,))],
        compiler_params=pltpu.CompilerParams(collective_id=0, has_side_effects=True),
        cost_estimate=pl.CostEstimate(flops=0, transcendentals=0, bytes_accessed=2 * nv * size),
    )(block)


def gather_kernel(nv, src_ref, out_ref, send_sems, recv_sems):
    beta = lax.axis_index("pair")
    b = lax.axis_index("batch")
    v = lax.axis_index("vocab")
    barrier = pltpu.get_barrier_semaphore()
    for w in range(nv):
        @pl.when(v != w)
        def _():
            pl.semaphore_signal(barrier, inc=1, device_id=(beta, b, w), device_id_type=MESH)
    pl.semaphore_wait(barrier, nv - 1)

    def remote(w, s):
        return pltpu.make_async_remote_copy(
            src_ref=src_ref,
            dst_ref=out_ref.at[s],
            send_sem=send_sems.at[w],
            recv_sem=recv_sems.at[s],
            device_id=(beta, b, w),
            device_id_type=MESH,
        )

    for w in range(nv):
        @pl.when(v != w)
        def _():
            remote(w, v).start()

    pltpu.make_async_copy(src_ref, out_ref.at[v], recv_sems.at[v]).start()
    for w in range(nv):
        @pl.when(v != w)
        def _():
            remote(w, v).wait_send()
    for s in range(nv):
        @pl.when(v != s)
        def _():
            remote(s, s).wait_recv()
    pltpu.make_async_copy(src_ref, out_ref.at[v], recv_sems.at[v]).wait()


def vocab_gather(block, nv, cid):
    size = block.size * block.dtype.itemsize
    return pl.pallas_call(
        functools.partial(gather_kernel, nv),
        out_shape=jax.ShapeDtypeStruct((nv,) + block.shape, block.dtype),
        in_specs=[pl.BlockSpec(memory_space=pltpu.VMEM)],
        out_specs=pl.BlockSpec(memory_space=pltpu.VMEM),
        scratch_shapes=[pltpu.SemaphoreType.DMA((nv,)), pltpu.SemaphoreType.DMA((nv,))],
        compiler_params=pltpu.CompilerParams(collective_id=cid, has_side_effects=True),
        cost_estimate=pl.CostEstimate(flops=0, transcendentals=0, bytes_accessed=2 * nv * size),
    )(block)


def on_device(npair, nb, nv, hidden, norm_gain, head_weight):
    groups = npair * nb
    span = nv // groups
    local_rows, width = hidden.shape[1], hidden.shape[2]
    total_d = width * nv
    wide = hidden[0].astype(jnp.float32)
    part = jnp.sum(wide * wide, axis=1)
    lanes = 128
    part_block = jnp.zeros((8, local_rows), jnp.float32).at[0].set(part)
    parts = vocab_gather(part_block, nv, 1)
    meansq = jnp.sum(parts[:, 0, :], axis=0) / total_d
    scaled = wide * lax.rsqrt(meansq + EPS)[:, None] * norm_gain.astype(jnp.float32)[None, :]
    features = scaled.astype(jnp.bfloat16)
    got = dispatch(features, npair, nb, nv)
    half = local_rows // 2
    raw = got.reshape(npair, nb, span, 2, half, width).transpose(1, 3, 0, 4, 2, 5)
    ordered = raw.reshape(groups * npair * half, span * width)
    out_rows = half
    me = lax.axis_index("pair")
    half_rows = ordered.shape[0] // 2
    mine = lax.dynamic_slice_in_dim(ordered, me * half_rows, half_rows, axis=0)
    theirs = lax.dynamic_slice_in_dim(ordered, (1 - me) * half_rows, half_rows, axis=0)
    cols = head_weight.shape[1]
    step = cols // CHUNKS
    pieces = []
    for j in range(CHUNKS):
        w = head_weight[:, j * step:(j + 1) * step]
        sent = jnp.dot(theirs, w, preferred_element_type=jnp.float32)
        kept = jnp.dot(mine, w, preferred_element_type=jnp.float32)
        got_half = lax.ppermute(sent, "pair", [(0, 1), (1, 0)])
        pieces.append(lax.psum_scatter(kept + got_half, "batch", scatter_dimension=0, tiled=True))
    logits = jnp.concatenate(pieces, axis=1)
    cond = logits[:out_rows]
    uncond = logits[out_rows:]
    guided = GUIDE * cond + (1.0 - GUIDE) * uncond
    peak_c = jnp.max(cond, axis=1)
    peak_g = jnp.max(guided, axis=1)
    local_c = jnp.sum(jnp.exp(cond - peak_c[:, None]), axis=1)
    local_g = jnp.sum(jnp.exp(guided - peak_g[:, None]), axis=1)
    stats = jnp.zeros((8, lanes), jnp.float32).at[:4, :out_rows].set(
        jnp.stack([peak_c, local_c, peak_g, local_g]))
    every = vocab_gather(stats, nv, 2)[:, :4, :out_rows]
    top_c = jnp.max(every[:, 0], axis=0)
    top_g = jnp.max(every[:, 2], axis=0)
    total_c = jnp.sum(every[:, 1] * jnp.exp(every[:, 0] - top_c[None, :]), axis=0)
    total_g = jnp.sum(every[:, 3] * jnp.exp(every[:, 2] - top_g[None, :]), axis=0)
    cond_out = cond - (top_c + jnp.log(total_c))[:, None]
    guided_out = guided - (top_g + jnp.log(total_g))[:, None]
    return (guided_out, cond_out)


def solution(mesh):
    npair, nb, nv = mesh.shape["pair"], mesh.shape["batch"], mesh.shape["vocab"]
    in_specs = (P("pair", "batch", "vocab"), P("vocab"), P(("pair", "batch"), "vocab"))
    out_specs = (P(("pair", "batch"), "vocab"), P(("pair", "batch"), "vocab"))
    return jax.shard_map(
        functools.partial(on_device, npair, nb, nv),
        mesh=mesh, in_specs=in_specs, out_specs=out_specs, check_vma=False,
    )
```

```python
import functools

import jax
import jax.numpy as jnp
from jax import lax
from jax.experimental import pallas as pl
from jax.experimental.pallas import tpu as pltpu
from jax.sharding import PartitionSpec as P

MESH = pl.DeviceIdType.MESH

EPS = 1e-05
GUIDE = 1.5
CHUNKS = 2


def dispatch_kernel(npair, nb, nv, span, src_ref, out_ref, send_sems, recv_sems):
    beta = lax.axis_index("pair")
    b = lax.axis_index("batch")
    v = lax.axis_index("vocab")
    groups = npair * nb
    mine = beta * nb + b
    q = v // span
    tp = q // nb
    tb = q % nb
    slot = mine * span + v % span
    d = q - mine
    own = 1 - (d * d + groups * groups - 1) // (groups * groups)

    def sources(s):
        bs = s // (nb * span)
        bbs = (s // span) % nb
        sv = mine * span + s % span
        return bs, bbs, sv

    barrier = pltpu.get_barrier_semaphore()
    for w in range(nv):
        @pl.when(jnp.logical_not((tp == beta) & (tb == b) & (v == w)))
        def _():
            pl.semaphore_signal(barrier, inc=1, device_id=(tp, tb, w), device_id_type=MESH)
    for s in range(nv):
        bs, bbs, sv = sources(s)

        @pl.when(jnp.logical_not((bs == beta) & (bbs == b) & (sv == v)))
        def _():
            pl.semaphore_signal(barrier, inc=1, device_id=(bs, bbs, sv), device_id_type=MESH)
    pl.semaphore_wait(barrier, 2 * (nv - own))

    def remote(k):
        return pltpu.make_async_remote_copy(
            src_ref=src_ref,
            dst_ref=out_ref.at[slot],
            send_sem=send_sems.at[k],
            recv_sem=recv_sems.at[slot],
            device_id=(tp, tb, (k + slot) % nv),
            device_id_type=MESH,
        )

    for k in range(nv):
        here = (tp == beta) & (tb == b) & (v == (k + slot) % nv)

        @pl.when(jnp.logical_not(here))
        def _():
            remote(k).start()

        @pl.when(here)
        def _():
            pltpu.make_async_copy(src_ref, out_ref.at[slot], recv_sems.at[slot]).start()

    for k in range(nv):
        here = (tp == beta) & (tb == b) & (v == (k + slot) % nv)

        @pl.when(jnp.logical_not(here))
        def _():
            remote(k).wait_send()

    for s in range(nv):
        bs, bbs, sv = sources(s)
        here = (bs == beta) & (bbs == b) & (sv == v)

        @pl.when(jnp.logical_not(here))
        def _():
            pltpu.make_async_remote_copy(
                src_ref=src_ref,
                dst_ref=out_ref.at[s],
                send_sem=send_sems.at[0],
                recv_sem=recv_sems.at[s],
                device_id=(bs, bbs, sv),
                device_id_type=MESH,
            ).wait_recv()

        @pl.when(here)
        def _():
            pltpu.make_async_copy(src_ref, out_ref.at[s], recv_sems.at[s]).wait()


def dispatch(block, npair, nb, nv):
    span = nv // (npair * nb)
    size = block.size * block.dtype.itemsize
    return pl.pallas_call(
        functools.partial(dispatch_kernel, npair, nb, nv, span),
        out_shape=jax.ShapeDtypeStruct((nv,) + block.shape, block.dtype),
        in_specs=[pl.BlockSpec(memory_space=pltpu.VMEM)],
        out_specs=pl.BlockSpec(memory_space=pltpu.VMEM),
        scratch_shapes=[pltpu.SemaphoreType.DMA((nv,)), pltpu.SemaphoreType.DMA((nv,))],
        compiler_params=pltpu.CompilerParams(collective_id=0, has_side_effects=True),
        cost_estimate=pl.CostEstimate(flops=0, transcendentals=0, bytes_accessed=2 * nv * size),
    )(block)


def gather_kernel(nv, src_ref, out_ref, send_sems, recv_sems):
    beta = lax.axis_index("pair")
    b = lax.axis_index("batch")
    v = lax.axis_index("vocab")
    barrier = pltpu.get_barrier_semaphore()
    for w in range(nv):
        @pl.when(v != w)
        def _():
            pl.semaphore_signal(barrier, inc=1, device_id=(beta, b, w), device_id_type=MESH)
    pl.semaphore_wait(barrier, nv - 1)

    def remote(w, s):
        return pltpu.make_async_remote_copy(
            src_ref=src_ref,
            dst_ref=out_ref.at[s],
            send_sem=send_sems.at[w],
            recv_sem=recv_sems.at[s],
            device_id=(beta, b, w),
            device_id_type=MESH,
        )

    for w in range(nv):
        @pl.when(v != w)
        def _():
            remote(w, v).start()

    pltpu.make_async_copy(src_ref, out_ref.at[v], recv_sems.at[v]).start()
    for w in range(nv):
        @pl.when(v != w)
        def _():
            remote(w, v).wait_send()
    for s in range(nv):
        @pl.when(v != s)
        def _():
            remote(s, s).wait_recv()
    pltpu.make_async_copy(src_ref, out_ref.at[v], recv_sems.at[v]).wait()


def vocab_gather(block, nv, cid):
    size = block.size * block.dtype.itemsize
    return pl.pallas_call(
        functools.partial(gather_kernel, nv),
        out_shape=jax.ShapeDtypeStruct((nv,) + block.shape, block.dtype),
        in_specs=[pl.BlockSpec(memory_space=pltpu.VMEM)],
        out_specs=pl.BlockSpec(memory_space=pltpu.VMEM),
        scratch_shapes=[pltpu.SemaphoreType.DMA((nv,)), pltpu.SemaphoreType.DMA((nv,))],
        compiler_params=pltpu.CompilerParams(collective_id=cid, has_side_effects=True),
        cost_estimate=pl.CostEstimate(flops=0, transcendentals=0, bytes_accessed=2 * nv * size),
    )(block)


def on_device(npair, nb, nv, hidden, norm_gain, head_weight):
    groups = npair * nb
    span = nv // groups
    local_rows, width = hidden.shape[1], hidden.shape[2]
    total_d = width * nv
    wide = hidden[0].astype(jnp.float32)
    part = jnp.sum(wide * wide, axis=1)
    lanes = 128
    part_block = jnp.zeros((8, local_rows), jnp.float32).at[0].set(part)
    parts = vocab_gather(part_block, nv, 1)
    meansq = jnp.sum(parts[:, 0, :], axis=0) / total_d
    scaled = wide * lax.rsqrt(meansq + EPS)[:, None] * norm_gain.astype(jnp.float32)[None, :]
    features = scaled.astype(jnp.bfloat16)
    got = dispatch(features, npair, nb, nv)
    half = local_rows // 2
    raw = got.reshape(npair, nb, span, 2, half, width).transpose(1, 3, 0, 4, 2, 5)
    ordered = raw.reshape(groups * npair * half, span * width)
    out_rows = half
    me = lax.axis_index("pair")
    half_rows = ordered.shape[0] // 2
    mine = lax.dynamic_slice_in_dim(ordered, me * half_rows, half_rows, axis=0)
    theirs = lax.dynamic_slice_in_dim(ordered, (1 - me) * half_rows, half_rows, axis=0)
    cols = head_weight.shape[1]
    step = cols // CHUNKS
    weights = [head_weight[:, j * step:(j + 1) * step] for j in range(CHUNKS)]
    arriving = []
    for j in range(CHUNKS):
        sent = jnp.dot(theirs, weights[j], preferred_element_type=jnp.float32)
        if j > 0:
            arriving[-1], sent = lax.optimization_barrier((arriving[-1], sent))
        arriving.append(lax.ppermute(sent, "pair", [(0, 1), (1, 0)]))
    pieces = []
    for j in range(CHUNKS):
        kept = jnp.dot(mine, weights[j], preferred_element_type=jnp.float32)
        pieces.append(lax.psum_scatter(kept + arriving[j], "batch", scatter_dimension=0, tiled=True))
    logits = jnp.concatenate(pieces, axis=1)
    cond = logits[:out_rows]
    uncond = logits[out_rows:]
    guided = GUIDE * cond + (1.0 - GUIDE) * uncond
    peak_c = jnp.max(cond, axis=1)
    peak_g = jnp.max(guided, axis=1)
    local_c = jnp.sum(jnp.exp(cond - peak_c[:, None]), axis=1)
    local_g = jnp.sum(jnp.exp(guided - peak_g[:, None]), axis=1)
    stats = jnp.zeros((8, lanes), jnp.float32).at[:4, :out_rows].set(
        jnp.stack([peak_c, local_c, peak_g, local_g]))
    every = vocab_gather(stats, nv, 2)[:, :4, :out_rows]
    top_c = jnp.max(every[:, 0], axis=0)
    top_g = jnp.max(every[:, 2], axis=0)
    total_c = jnp.sum(every[:, 1] * jnp.exp(every[:, 0] - top_c[None, :]), axis=0)
    total_g = jnp.sum(every[:, 3] * jnp.exp(every[:, 2] - top_g[None, :]), axis=0)
    cond_out = cond - (top_c + jnp.log(total_c))[:, None]
    guided_out = guided - (top_g + jnp.log(total_g))[:, None]
    return (guided_out, cond_out)


def solution(mesh):
    npair, nb, nv = mesh.shape["pair"], mesh.shape["batch"], mesh.shape["vocab"]
    in_specs = (P("pair", "batch", "vocab"), P("vocab"), P(("pair", "batch"), "vocab"))
    out_specs = (P(("pair", "batch"), "vocab"), P(("pair", "batch"), "vocab"))
    return jax.shard_map(
        functools.partial(on_device, npair, nb, nv),
        mesh=mesh, in_specs=in_specs, out_specs=out_specs, check_vma=False,
    )
```

```python
import functools

import jax
import jax.numpy as jnp
from jax import lax
from jax.experimental import pallas as pl
from jax.experimental.pallas import tpu as pltpu
from jax.sharding import PartitionSpec as P

MESH = pl.DeviceIdType.MESH

EPS = 1e-05
GUIDE = 1.5
CHUNKS = 2


def dispatch_kernel(npair, nb, nv, span, src_ref, out_ref, send_sems, recv_sems):
    beta = lax.axis_index("pair")
    b = lax.axis_index("batch")
    v = lax.axis_index("vocab")
    groups = npair * nb
    mine = beta * nb + b
    q = v // span
    tp = q // nb
    tb = q % nb
    slot = mine * span + v % span
    d = q - mine
    own = 1 - (d * d + groups * groups - 1) // (groups * groups)

    def sources(s):
        bs = s // (nb * span)
        bbs = (s // span) % nb
        sv = mine * span + s % span
        return bs, bbs, sv

    barrier = pltpu.get_barrier_semaphore()
    for w in range(nv):
        @pl.when(jnp.logical_not((tp == beta) & (tb == b) & (v == w)))
        def _():
            pl.semaphore_signal(barrier, inc=1, device_id=(tp, tb, w), device_id_type=MESH)
    for s in range(nv):
        bs, bbs, sv = sources(s)

        @pl.when(jnp.logical_not((bs == beta) & (bbs == b) & (sv == v)))
        def _():
            pl.semaphore_signal(barrier, inc=1, device_id=(bs, bbs, sv), device_id_type=MESH)
    pl.semaphore_wait(barrier, 2 * (nv - own))

    def remote(k):
        return pltpu.make_async_remote_copy(
            src_ref=src_ref,
            dst_ref=out_ref.at[slot],
            send_sem=send_sems.at[k],
            recv_sem=recv_sems.at[slot],
            device_id=(tp, tb, (k + slot) % nv),
            device_id_type=MESH,
        )

    for k in range(nv):
        here = (tp == beta) & (tb == b) & (v == (k + slot) % nv)

        @pl.when(jnp.logical_not(here))
        def _():
            remote(k).start()

        @pl.when(here)
        def _():
            pltpu.make_async_copy(src_ref, out_ref.at[slot], recv_sems.at[slot]).start()

    for k in range(nv):
        here = (tp == beta) & (tb == b) & (v == (k + slot) % nv)

        @pl.when(jnp.logical_not(here))
        def _():
            remote(k).wait_send()

    for s in range(nv):
        bs, bbs, sv = sources(s)
        here = (bs == beta) & (bbs == b) & (sv == v)

        @pl.when(jnp.logical_not(here))
        def _():
            pltpu.make_async_remote_copy(
                src_ref=src_ref,
                dst_ref=out_ref.at[s],
                send_sem=send_sems.at[0],
                recv_sem=recv_sems.at[s],
                device_id=(bs, bbs, sv),
                device_id_type=MESH,
            ).wait_recv()

        @pl.when(here)
        def _():
            pltpu.make_async_copy(src_ref, out_ref.at[s], recv_sems.at[s]).wait()


def dispatch(block, npair, nb, nv):
    span = nv // (npair * nb)
    size = block.size * block.dtype.itemsize
    return pl.pallas_call(
        functools.partial(dispatch_kernel, npair, nb, nv, span),
        out_shape=jax.ShapeDtypeStruct((nv,) + block.shape, block.dtype),
        in_specs=[pl.BlockSpec(memory_space=pltpu.VMEM)],
        out_specs=pl.BlockSpec(memory_space=pltpu.VMEM),
        scratch_shapes=[pltpu.SemaphoreType.DMA((nv,)), pltpu.SemaphoreType.DMA((nv,))],
        compiler_params=pltpu.CompilerParams(collective_id=0, has_side_effects=True),
        cost_estimate=pl.CostEstimate(flops=0, transcendentals=0, bytes_accessed=2 * nv * size),
    )(block)


def gather_kernel(nv, src_ref, out_ref, send_sems, recv_sems):
    beta = lax.axis_index("pair")
    b = lax.axis_index("batch")
    v = lax.axis_index("vocab")
    barrier = pltpu.get_barrier_semaphore()
    for w in range(nv):
        @pl.when(v != w)
        def _():
            pl.semaphore_signal(barrier, inc=1, device_id=(beta, b, w), device_id_type=MESH)
    pl.semaphore_wait(barrier, nv - 1)

    def remote(w, s):
        return pltpu.make_async_remote_copy(
            src_ref=src_ref,
            dst_ref=out_ref.at[s],
            send_sem=send_sems.at[w],
            recv_sem=recv_sems.at[s],
            device_id=(beta, b, w),
            device_id_type=MESH,
        )

    for w in range(nv):
        @pl.when(v != w)
        def _():
            remote(w, v).start()

    pltpu.make_async_copy(src_ref, out_ref.at[v], recv_sems.at[v]).start()
    for w in range(nv):
        @pl.when(v != w)
        def _():
            remote(w, v).wait_send()
    for s in range(nv):
        @pl.when(v != s)
        def _():
            remote(s, s).wait_recv()
    pltpu.make_async_copy(src_ref, out_ref.at[v], recv_sems.at[v]).wait()


def vocab_gather(block, nv, cid):
    size = block.size * block.dtype.itemsize
    return pl.pallas_call(
        functools.partial(gather_kernel, nv),
        out_shape=jax.ShapeDtypeStruct((nv,) + block.shape, block.dtype),
        in_specs=[pl.BlockSpec(memory_space=pltpu.VMEM)],
        out_specs=pl.BlockSpec(memory_space=pltpu.VMEM),
        scratch_shapes=[pltpu.SemaphoreType.DMA((nv,)), pltpu.SemaphoreType.DMA((nv,))],
        compiler_params=pltpu.CompilerParams(collective_id=cid, has_side_effects=True),
        cost_estimate=pl.CostEstimate(flops=0, transcendentals=0, bytes_accessed=2 * nv * size),
    )(block)


def exchange_kernel(nb, src_ref, out_ref, send_sems, recv_sems):
    beta = lax.axis_index("pair")
    b = lax.axis_index("batch")
    v = lax.axis_index("vocab")
    barrier = pltpu.get_barrier_semaphore()
    for w in range(nb):
        @pl.when(b != w)
        def _():
            pl.semaphore_signal(barrier, inc=1, device_id=(beta, w, v), device_id_type=MESH)
    pl.semaphore_wait(barrier, nb - 1)

    def remote(k, s):
        target = (b + k) % nb
        return pltpu.make_async_remote_copy(
            src_ref=src_ref.at[target],
            dst_ref=out_ref.at[s],
            send_sem=send_sems.at[k],
            recv_sem=recv_sems.at[s],
            device_id=(beta, target, v),
            device_id_type=MESH,
        )

    for k in range(1, nb):
        remote(k, b).start()
    for k in range(1, nb):
        remote(k, b).wait_send()
    for k in range(1, nb):
        s = (b + k) % nb
        pltpu.make_async_remote_copy(
            src_ref=src_ref.at[s],
            dst_ref=out_ref.at[s],
            send_sem=send_sems.at[0],
            recv_sem=recv_sems.at[s],
            device_id=(beta, s, v),
            device_id_type=MESH,
        ).wait_recv()


def batch_exchange(blocks, nb):
    size = blocks.size * blocks.dtype.itemsize
    return pl.pallas_call(
        functools.partial(exchange_kernel, nb),
        out_shape=jax.ShapeDtypeStruct(blocks.shape, blocks.dtype),
        in_specs=[pl.BlockSpec(memory_space=pl.ANY)],
        out_specs=pl.BlockSpec(memory_space=pl.ANY),
        scratch_shapes=[pltpu.SemaphoreType.DMA((nb,)), pltpu.SemaphoreType.DMA((nb,))],
        compiler_params=pltpu.CompilerParams(collective_id=3, has_side_effects=True),
        cost_estimate=pl.CostEstimate(flops=0, transcendentals=0, bytes_accessed=2 * size),
    )(blocks)


def on_device(npair, nb, nv, hidden, norm_gain, head_weight):
    groups = npair * nb
    span = nv // groups
    local_rows, width = hidden.shape[1], hidden.shape[2]
    total_d = width * nv
    wide = hidden[0].astype(jnp.float32)
    part = jnp.sum(wide * wide, axis=1)
    lanes = 128
    part_block = jnp.zeros((8, local_rows), jnp.float32).at[0].set(part)
    parts = vocab_gather(part_block, nv, 1)
    meansq = jnp.sum(parts[:, 0, :], axis=0) / total_d
    scaled = wide * lax.rsqrt(meansq + EPS)[:, None] * norm_gain.astype(jnp.float32)[None, :]
    features = scaled.astype(jnp.bfloat16)
    got = dispatch(features, npair, nb, nv)
    half = local_rows // 2
    raw = got.reshape(npair, nb, span, 2, half, width).transpose(1, 3, 0, 4, 2, 5)
    ordered = raw.reshape(groups * npair * half, span * width)
    out_rows = half
    me = lax.axis_index("pair")
    half_rows = ordered.shape[0] // 2
    mine = lax.dynamic_slice_in_dim(ordered, me * half_rows, half_rows, axis=0)
    theirs = lax.dynamic_slice_in_dim(ordered, (1 - me) * half_rows, half_rows, axis=0)
    cols = head_weight.shape[1]
    step = cols // CHUNKS
    pieces = []
    for j in range(CHUNKS):
        w = head_weight[:, j * step:(j + 1) * step]
        sent = jnp.dot(theirs, w, preferred_element_type=jnp.float32)
        kept = jnp.dot(mine, w, preferred_element_type=jnp.float32)
        got_half = lax.ppermute(sent, "pair", [(0, 1), (1, 0)])
        pieces.append(kept + got_half)
    summed = jnp.concatenate(pieces, axis=1).reshape(nb, half_rows // nb, cols)
    arrived = batch_exchange(summed, nb)
    mb = lax.axis_index("batch")
    own = lax.dynamic_index_in_dim(summed, mb, axis=0, keepdims=False)
    slots = lax.broadcasted_iota(jnp.int32, (nb, 1, 1), 0)
    logits = own + jnp.sum(jnp.where(slots == mb, 0.0, arrived), axis=0)
    cond = logits[:out_rows]
    uncond = logits[out_rows:]
    guided = GUIDE * cond + (1.0 - GUIDE) * uncond
    peak_c = jnp.max(cond, axis=1)
    peak_g = jnp.max(guided, axis=1)
    local_c = jnp.sum(jnp.exp(cond - peak_c[:, None]), axis=1)
    local_g = jnp.sum(jnp.exp(guided - peak_g[:, None]), axis=1)
    stats = jnp.zeros((8, lanes), jnp.float32).at[:4, :out_rows].set(
        jnp.stack([peak_c, local_c, peak_g, local_g]))
    every = vocab_gather(stats, nv, 2)[:, :4, :out_rows]
    top_c = jnp.max(every[:, 0], axis=0)
    top_g = jnp.max(every[:, 2], axis=0)
    total_c = jnp.sum(every[:, 1] * jnp.exp(every[:, 0] - top_c[None, :]), axis=0)
    total_g = jnp.sum(every[:, 3] * jnp.exp(every[:, 2] - top_g[None, :]), axis=0)
    cond_out = cond - (top_c + jnp.log(total_c))[:, None]
    guided_out = guided - (top_g + jnp.log(total_g))[:, None]
    return (guided_out, cond_out)


def solution(mesh):
    npair, nb, nv = mesh.shape["pair"], mesh.shape["batch"], mesh.shape["vocab"]
    in_specs = (P("pair", "batch", "vocab"), P("vocab"), P(("pair", "batch"), "vocab"))
    out_specs = (P(("pair", "batch"), "vocab"), P(("pair", "batch"), "vocab"))
    return jax.shard_map(
        functools.partial(on_device, npair, nb, nv),
        mesh=mesh, in_specs=in_specs, out_specs=out_specs, check_vma=False,
    )
```

```python
import functools

import jax
import jax.numpy as jnp
from jax import lax
from jax.experimental import pallas as pl
from jax.experimental.pallas import tpu as pltpu
from jax.sharding import PartitionSpec as P

MESH = pl.DeviceIdType.MESH

EPS = 1e-05
GUIDE = 1.5
CHUNKS = 4


def dispatch_kernel(npair, nb, nv, span, src_ref, out_ref, send_sems, recv_sems):
    beta = lax.axis_index("pair")
    b = lax.axis_index("batch")
    v = lax.axis_index("vocab")
    groups = npair * nb
    mine = beta * nb + b
    q = v // span
    tp = q // nb
    tb = q % nb
    slot = mine * span + v % span
    d = q - mine
    own = 1 - (d * d + groups * groups - 1) // (groups * groups)

    def sources(s):
        bs = s // (nb * span)
        bbs = (s // span) % nb
        sv = mine * span + s % span
        return bs, bbs, sv

    barrier = pltpu.get_barrier_semaphore()
    for w in range(nv):
        @pl.when(jnp.logical_not((tp == beta) & (tb == b) & (v == w)))
        def _():
            pl.semaphore_signal(barrier, inc=1, device_id=(tp, tb, w), device_id_type=MESH)
    for s in range(nv):
        bs, bbs, sv = sources(s)

        @pl.when(jnp.logical_not((bs == beta) & (bbs == b) & (sv == v)))
        def _():
            pl.semaphore_signal(barrier, inc=1, device_id=(bs, bbs, sv), device_id_type=MESH)
    pl.semaphore_wait(barrier, 2 * (nv - own))

    def remote(k):
        return pltpu.make_async_remote_copy(
            src_ref=src_ref,
            dst_ref=out_ref.at[slot],
            send_sem=send_sems.at[k],
            recv_sem=recv_sems.at[slot],
            device_id=(tp, tb, (k + slot) % nv),
            device_id_type=MESH,
        )

    for k in range(nv):
        here = (tp == beta) & (tb == b) & (v == (k + slot) % nv)

        @pl.when(jnp.logical_not(here))
        def _():
            remote(k).start()

        @pl.when(here)
        def _():
            pltpu.make_async_copy(src_ref, out_ref.at[slot], recv_sems.at[slot]).start()

    for k in range(nv):
        here = (tp == beta) & (tb == b) & (v == (k + slot) % nv)

        @pl.when(jnp.logical_not(here))
        def _():
            remote(k).wait_send()

    for s in range(nv):
        bs, bbs, sv = sources(s)
        here = (bs == beta) & (bbs == b) & (sv == v)

        @pl.when(jnp.logical_not(here))
        def _():
            pltpu.make_async_remote_copy(
                src_ref=src_ref,
                dst_ref=out_ref.at[s],
                send_sem=send_sems.at[0],
                recv_sem=recv_sems.at[s],
                device_id=(bs, bbs, sv),
                device_id_type=MESH,
            ).wait_recv()

        @pl.when(here)
        def _():
            pltpu.make_async_copy(src_ref, out_ref.at[s], recv_sems.at[s]).wait()


def dispatch(block, npair, nb, nv):
    span = nv // (npair * nb)
    size = block.size * block.dtype.itemsize
    return pl.pallas_call(
        functools.partial(dispatch_kernel, npair, nb, nv, span),
        out_shape=jax.ShapeDtypeStruct((nv,) + block.shape, block.dtype),
        in_specs=[pl.BlockSpec(memory_space=pltpu.VMEM)],
        out_specs=pl.BlockSpec(memory_space=pltpu.VMEM),
        scratch_shapes=[pltpu.SemaphoreType.DMA((nv,)), pltpu.SemaphoreType.DMA((nv,))],
        compiler_params=pltpu.CompilerParams(collective_id=0, has_side_effects=True),
        cost_estimate=pl.CostEstimate(flops=0, transcendentals=0, bytes_accessed=2 * nv * size),
    )(block)


def gather_kernel(nv, src_ref, out_ref, send_sems, recv_sems):
    beta = lax.axis_index("pair")
    b = lax.axis_index("batch")
    v = lax.axis_index("vocab")
    barrier = pltpu.get_barrier_semaphore()
    for w in range(nv):
        @pl.when(v != w)
        def _():
            pl.semaphore_signal(barrier, inc=1, device_id=(beta, b, w), device_id_type=MESH)
    pl.semaphore_wait(barrier, nv - 1)

    def remote(w, s):
        return pltpu.make_async_remote_copy(
            src_ref=src_ref,
            dst_ref=out_ref.at[s],
            send_sem=send_sems.at[w],
            recv_sem=recv_sems.at[s],
            device_id=(beta, b, w),
            device_id_type=MESH,
        )

    for w in range(nv):
        @pl.when(v != w)
        def _():
            remote(w, v).start()

    pltpu.make_async_copy(src_ref, out_ref.at[v], recv_sems.at[v]).start()
    for w in range(nv):
        @pl.when(v != w)
        def _():
            remote(w, v).wait_send()
    for s in range(nv):
        @pl.when(v != s)
        def _():
            remote(s, s).wait_recv()
    pltpu.make_async_copy(src_ref, out_ref.at[v], recv_sems.at[v]).wait()


def vocab_gather(block, nv, cid):
    size = block.size * block.dtype.itemsize
    return pl.pallas_call(
        functools.partial(gather_kernel, nv),
        out_shape=jax.ShapeDtypeStruct((nv,) + block.shape, block.dtype),
        in_specs=[pl.BlockSpec(memory_space=pltpu.VMEM)],
        out_specs=pl.BlockSpec(memory_space=pltpu.VMEM),
        scratch_shapes=[pltpu.SemaphoreType.DMA((nv,)), pltpu.SemaphoreType.DMA((nv,))],
        compiler_params=pltpu.CompilerParams(collective_id=cid, has_side_effects=True),
        cost_estimate=pl.CostEstimate(flops=0, transcendentals=0, bytes_accessed=2 * nv * size),
    )(block)


def on_device(npair, nb, nv, hidden, norm_gain, head_weight):
    groups = npair * nb
    span = nv // groups
    local_rows, width = hidden.shape[1], hidden.shape[2]
    total_d = width * nv
    wide = hidden[0].astype(jnp.float32)
    part = jnp.sum(wide * wide, axis=1)
    lanes = 128
    part_block = jnp.zeros((8, local_rows), jnp.float32).at[0].set(part)
    parts = vocab_gather(part_block, nv, 1)
    meansq = jnp.sum(parts[:, 0, :], axis=0) / total_d
    scaled = wide * lax.rsqrt(meansq + EPS)[:, None] * norm_gain.astype(jnp.float32)[None, :]
    features = scaled.astype(jnp.bfloat16)
    got = dispatch(features, npair, nb, nv)
    half = local_rows // 2
    raw = got.reshape(npair, nb, span, 2, half, width).transpose(1, 3, 0, 4, 2, 5)
    ordered = raw.reshape(groups * npair * half, span * width)
    out_rows = half
    me = lax.axis_index("pair")
    half_rows = ordered.shape[0] // 2
    mine = lax.dynamic_slice_in_dim(ordered, me * half_rows, half_rows, axis=0)
    theirs = lax.dynamic_slice_in_dim(ordered, (1 - me) * half_rows, half_rows, axis=0)
    cols = head_weight.shape[1]
    step = cols // CHUNKS
    pieces = []
    for j in range(CHUNKS):
        w = head_weight[:, j * step:(j + 1) * step]
        sent = jnp.dot(theirs, w, preferred_element_type=jnp.float32)
        kept = jnp.dot(mine, w, preferred_element_type=jnp.float32)
        got_half = lax.ppermute(sent, "pair", [(0, 1), (1, 0)])
        pieces.append(lax.psum_scatter(kept + got_half, "batch", scatter_dimension=0, tiled=True))
    logits = jnp.concatenate(pieces, axis=1)
    cond = logits[:out_rows]
    uncond = logits[out_rows:]
    guided = GUIDE * cond + (1.0 - GUIDE) * uncond
    peak_c = jnp.max(cond, axis=1)
    peak_g = jnp.max(guided, axis=1)
    local_c = jnp.sum(jnp.exp(cond - peak_c[:, None]), axis=1)
    local_g = jnp.sum(jnp.exp(guided - peak_g[:, None]), axis=1)
    stats = jnp.zeros((8, lanes), jnp.float32).at[:4, :out_rows].set(
        jnp.stack([peak_c, local_c, peak_g, local_g]))
    every = vocab_gather(stats, nv, 2)[:, :4, :out_rows]
    top_c = jnp.max(every[:, 0], axis=0)
    top_g = jnp.max(every[:, 2], axis=0)
    total_c = jnp.sum(every[:, 1] * jnp.exp(every[:, 0] - top_c[None, :]), axis=0)
    total_g = jnp.sum(every[:, 3] * jnp.exp(every[:, 2] - top_g[None, :]), axis=0)
    cond_out = cond - (top_c + jnp.log(total_c))[:, None]
    guided_out = guided - (top_g + jnp.log(total_g))[:, None]
    return (guided_out, cond_out)


def solution(mesh):
    npair, nb, nv = mesh.shape["pair"], mesh.shape["batch"], mesh.shape["vocab"]
    in_specs = (P("pair", "batch", "vocab"), P("vocab"), P(("pair", "batch"), "vocab"))
    out_specs = (P(("pair", "batch"), "vocab"), P(("pair", "batch"), "vocab"))
    return jax.shard_map(
        functools.partial(on_device, npair, nb, nv),
        mesh=mesh, in_specs=in_specs, out_specs=out_specs, check_vma=False,
    )
```

```python
import functools

import jax
import jax.numpy as jnp
from jax import lax
from jax.experimental import pallas as pl
from jax.experimental.pallas import tpu as pltpu
from jax.sharding import PartitionSpec as P

MESH = pl.DeviceIdType.MESH

EPS = 1e-05
GUIDE = 1.5
CHUNKS = 1


def dispatch_kernel(npair, nb, nv, span, src_ref, out_ref, send_sems, recv_sems):
    beta = lax.axis_index("pair")
    b = lax.axis_index("batch")
    v = lax.axis_index("vocab")
    groups = npair * nb
    mine = beta * nb + b
    q = v // span
    tp = q // nb
    tb = q % nb
    slot = mine * span + v % span
    d = q - mine
    own = 1 - (d * d + groups * groups - 1) // (groups * groups)

    def sources(s):
        bs = s // (nb * span)
        bbs = (s // span) % nb
        sv = mine * span + s % span
        return bs, bbs, sv

    barrier = pltpu.get_barrier_semaphore()
    for w in range(nv):
        @pl.when(jnp.logical_not((tp == beta) & (tb == b) & (v == w)))
        def _():
            pl.semaphore_signal(barrier, inc=1, device_id=(tp, tb, w), device_id_type=MESH)
    for s in range(nv):
        bs, bbs, sv = sources(s)

        @pl.when(jnp.logical_not((bs == beta) & (bbs == b) & (sv == v)))
        def _():
            pl.semaphore_signal(barrier, inc=1, device_id=(bs, bbs, sv), device_id_type=MESH)
    pl.semaphore_wait(barrier, 2 * (nv - own))

    def remote(k):
        return pltpu.make_async_remote_copy(
            src_ref=src_ref,
            dst_ref=out_ref.at[slot],
            send_sem=send_sems.at[k],
            recv_sem=recv_sems.at[slot],
            device_id=(tp, tb, (k + slot) % nv),
            device_id_type=MESH,
        )

    for k in range(nv):
        here = (tp == beta) & (tb == b) & (v == (k + slot) % nv)

        @pl.when(jnp.logical_not(here))
        def _():
            remote(k).start()

        @pl.when(here)
        def _():
            pltpu.make_async_copy(src_ref, out_ref.at[slot], recv_sems.at[slot]).start()

    for k in range(nv):
        here = (tp == beta) & (tb == b) & (v == (k + slot) % nv)

        @pl.when(jnp.logical_not(here))
        def _():
            remote(k).wait_send()

    for s in range(nv):
        bs, bbs, sv = sources(s)
        here = (bs == beta) & (bbs == b) & (sv == v)

        @pl.when(jnp.logical_not(here))
        def _():
            pltpu.make_async_remote_copy(
                src_ref=src_ref,
                dst_ref=out_ref.at[s],
                send_sem=send_sems.at[0],
                recv_sem=recv_sems.at[s],
                device_id=(bs, bbs, sv),
                device_id_type=MESH,
            ).wait_recv()

        @pl.when(here)
        def _():
            pltpu.make_async_copy(src_ref, out_ref.at[s], recv_sems.at[s]).wait()


def dispatch(block, npair, nb, nv):
    span = nv // (npair * nb)
    size = block.size * block.dtype.itemsize
    return pl.pallas_call(
        functools.partial(dispatch_kernel, npair, nb, nv, span),
        out_shape=jax.ShapeDtypeStruct((nv,) + block.shape, block.dtype),
        in_specs=[pl.BlockSpec(memory_space=pltpu.VMEM)],
        out_specs=pl.BlockSpec(memory_space=pltpu.VMEM),
        scratch_shapes=[pltpu.SemaphoreType.DMA((nv,)), pltpu.SemaphoreType.DMA((nv,))],
        compiler_params=pltpu.CompilerParams(collective_id=0, has_side_effects=True),
        cost_estimate=pl.CostEstimate(flops=0, transcendentals=0, bytes_accessed=2 * nv * size),
    )(block)


def gather_kernel(nv, src_ref, out_ref, send_sems, recv_sems):
    beta = lax.axis_index("pair")
    b = lax.axis_index("batch")
    v = lax.axis_index("vocab")
    barrier = pltpu.get_barrier_semaphore()
    for w in range(nv):
        @pl.when(v != w)
        def _():
            pl.semaphore_signal(barrier, inc=1, device_id=(beta, b, w), device_id_type=MESH)
    pl.semaphore_wait(barrier, nv - 1)

    def remote(w, s):
        return pltpu.make_async_remote_copy(
            src_ref=src_ref,
            dst_ref=out_ref.at[s],
            send_sem=send_sems.at[w],
            recv_sem=recv_sems.at[s],
            device_id=(beta, b, w),
            device_id_type=MESH,
        )

    for w in range(nv):
        @pl.when(v != w)
        def _():
            remote(w, v).start()

    pltpu.make_async_copy(src_ref, out_ref.at[v], recv_sems.at[v]).start()
    for w in range(nv):
        @pl.when(v != w)
        def _():
            remote(w, v).wait_send()
    for s in range(nv):
        @pl.when(v != s)
        def _():
            remote(s, s).wait_recv()
    pltpu.make_async_copy(src_ref, out_ref.at[v], recv_sems.at[v]).wait()


def vocab_gather(block, nv, cid):
    size = block.size * block.dtype.itemsize
    return pl.pallas_call(
        functools.partial(gather_kernel, nv),
        out_shape=jax.ShapeDtypeStruct((nv,) + block.shape, block.dtype),
        in_specs=[pl.BlockSpec(memory_space=pltpu.VMEM)],
        out_specs=pl.BlockSpec(memory_space=pltpu.VMEM),
        scratch_shapes=[pltpu.SemaphoreType.DMA((nv,)), pltpu.SemaphoreType.DMA((nv,))],
        compiler_params=pltpu.CompilerParams(collective_id=cid, has_side_effects=True),
        cost_estimate=pl.CostEstimate(flops=0, transcendentals=0, bytes_accessed=2 * nv * size),
    )(block)


def on_device(npair, nb, nv, hidden, norm_gain, head_weight):
    groups = npair * nb
    span = nv // groups
    local_rows, width = hidden.shape[1], hidden.shape[2]
    total_d = width * nv
    wide = hidden[0].astype(jnp.float32)
    part = jnp.sum(wide * wide, axis=1)
    lanes = 128
    part_block = jnp.zeros((8, local_rows), jnp.float32).at[0].set(part)
    parts = vocab_gather(part_block, nv, 1)
    meansq = jnp.sum(parts[:, 0, :], axis=0) / total_d
    scaled = wide * lax.rsqrt(meansq + EPS)[:, None] * norm_gain.astype(jnp.float32)[None, :]
    features = scaled.astype(jnp.bfloat16)
    got = dispatch(features, npair, nb, nv)
    half = local_rows // 2
    raw = got.reshape(npair, nb, span, 2, half, width).transpose(1, 3, 0, 4, 2, 5)
    ordered = raw.reshape(groups * npair * half, span * width)
    out_rows = half
    me = lax.axis_index("pair")
    half_rows = ordered.shape[0] // 2
    mine = lax.dynamic_slice_in_dim(ordered, me * half_rows, half_rows, axis=0)
    theirs = lax.dynamic_slice_in_dim(ordered, (1 - me) * half_rows, half_rows, axis=0)
    cols = head_weight.shape[1]
    step = cols // CHUNKS
    pieces = []
    for j in range(CHUNKS):
        w = head_weight[:, j * step:(j + 1) * step]
        sent = jnp.dot(theirs, w, preferred_element_type=jnp.float32)
        kept = jnp.dot(mine, w, preferred_element_type=jnp.float32)
        got_half = lax.ppermute(sent, "pair", [(0, 1), (1, 0)])
        pieces.append(lax.psum_scatter(kept + got_half, "batch", scatter_dimension=0, tiled=True))
    logits = jnp.concatenate(pieces, axis=1)
    cond = logits[:out_rows]
    uncond = logits[out_rows:]
    guided = GUIDE * cond + (1.0 - GUIDE) * uncond
    peak_c = jnp.max(cond, axis=1)
    peak_g = jnp.max(guided, axis=1)
    local_c = jnp.sum(jnp.exp(cond - peak_c[:, None]), axis=1)
    local_g = jnp.sum(jnp.exp(guided - peak_g[:, None]), axis=1)
    stats = jnp.zeros((8, lanes), jnp.float32).at[:4, :out_rows].set(
        jnp.stack([peak_c, local_c, peak_g, local_g]))
    every = vocab_gather(stats, nv, 2)[:, :4, :out_rows]
    top_c = jnp.max(every[:, 0], axis=0)
    top_g = jnp.max(every[:, 2], axis=0)
    total_c = jnp.sum(every[:, 1] * jnp.exp(every[:, 0] - top_c[None, :]), axis=0)
    total_g = jnp.sum(every[:, 3] * jnp.exp(every[:, 2] - top_g[None, :]), axis=0)
    cond_out = cond - (top_c + jnp.log(total_c))[:, None]
    guided_out = guided - (top_g + jnp.log(total_g))[:, None]
    return (guided_out, cond_out)


def solution(mesh):
    npair, nb, nv = mesh.shape["pair"], mesh.shape["batch"], mesh.shape["vocab"]
    in_specs = (P("pair", "batch", "vocab"), P("vocab"), P(("pair", "batch"), "vocab"))
    out_specs = (P(("pair", "batch"), "vocab"), P(("pair", "batch"), "vocab"))
    return jax.shard_map(
        functools.partial(on_device, npair, nb, nv),
        mesh=mesh, in_specs=in_specs, out_specs=out_specs, check_vma=False,
    )
```

```python
import functools

import jax
import jax.numpy as jnp
from jax import lax
from jax.experimental import pallas as pl
from jax.experimental.pallas import tpu as pltpu
from jax.sharding import PartitionSpec as P

MESH = pl.DeviceIdType.MESH

EPS = 1e-05
GUIDE = 1.5
CHUNKS = 2


def dispatch_kernel(npair, nb, nv, span, src_ref, out_ref, send_sems, recv_sems):
    beta = lax.axis_index("pair")
    b = lax.axis_index("batch")
    v = lax.axis_index("vocab")
    groups = npair * nb
    mine = beta * nb + b
    q = v // span
    tp = q // nb
    tb = q % nb
    slot = mine * span + v % span
    d = q - mine
    own = 1 - (d * d + groups * groups - 1) // (groups * groups)

    def sources(s):
        bs = s // (nb * span)
        bbs = (s // span) % nb
        sv = mine * span + s % span
        return bs, bbs, sv

    barrier = pltpu.get_barrier_semaphore()
    for w in range(nv):
        @pl.when(jnp.logical_not((tp == beta) & (tb == b) & (v == w)))
        def _():
            pl.semaphore_signal(barrier, inc=1, device_id=(tp, tb, w), device_id_type=MESH)
    for s in range(nv):
        bs, bbs, sv = sources(s)

        @pl.when(jnp.logical_not((bs == beta) & (bbs == b) & (sv == v)))
        def _():
            pl.semaphore_signal(barrier, inc=1, device_id=(bs, bbs, sv), device_id_type=MESH)
    pl.semaphore_wait(barrier, 2 * (nv - own))

    def remote(k):
        return pltpu.make_async_remote_copy(
            src_ref=src_ref,
            dst_ref=out_ref.at[slot],
            send_sem=send_sems.at[k],
            recv_sem=recv_sems.at[slot],
            device_id=(tp, tb, (k + slot) % nv),
            device_id_type=MESH,
        )

    for k in range(nv):
        here = (tp == beta) & (tb == b) & (v == (k + slot) % nv)

        @pl.when(jnp.logical_not(here))
        def _():
            remote(k).start()

        @pl.when(here)
        def _():
            pltpu.make_async_copy(src_ref, out_ref.at[slot], recv_sems.at[slot]).start()

    for k in range(nv):
        here = (tp == beta) & (tb == b) & (v == (k + slot) % nv)

        @pl.when(jnp.logical_not(here))
        def _():
            remote(k).wait_send()

    for s in range(nv):
        bs, bbs, sv = sources(s)
        here = (bs == beta) & (bbs == b) & (sv == v)

        @pl.when(jnp.logical_not(here))
        def _():
            pltpu.make_async_remote_copy(
                src_ref=src_ref,
                dst_ref=out_ref.at[s],
                send_sem=send_sems.at[0],
                recv_sem=recv_sems.at[s],
                device_id=(bs, bbs, sv),
                device_id_type=MESH,
            ).wait_recv()

        @pl.when(here)
        def _():
            pltpu.make_async_copy(src_ref, out_ref.at[s], recv_sems.at[s]).wait()


def dispatch(block, npair, nb, nv):
    span = nv // (npair * nb)
    size = block.size * block.dtype.itemsize
    return pl.pallas_call(
        functools.partial(dispatch_kernel, npair, nb, nv, span),
        out_shape=jax.ShapeDtypeStruct((nv,) + block.shape, block.dtype),
        in_specs=[pl.BlockSpec(memory_space=pltpu.VMEM)],
        out_specs=pl.BlockSpec(memory_space=pltpu.VMEM),
        scratch_shapes=[pltpu.SemaphoreType.DMA((nv,)), pltpu.SemaphoreType.DMA((nv,))],
        compiler_params=pltpu.CompilerParams(collective_id=0, has_side_effects=True),
        cost_estimate=pl.CostEstimate(flops=0, transcendentals=0, bytes_accessed=2 * nv * size),
    )(block)


def gather_kernel(nv, src_ref, out_ref, send_sems, recv_sems):
    beta = lax.axis_index("pair")
    b = lax.axis_index("batch")
    v = lax.axis_index("vocab")
    barrier = pltpu.get_barrier_semaphore()
    for w in range(nv):
        @pl.when(v != w)
        def _():
            pl.semaphore_signal(barrier, inc=1, device_id=(beta, b, w), device_id_type=MESH)
    pl.semaphore_wait(barrier, nv - 1)

    def remote(w, s):
        return pltpu.make_async_remote_copy(
            src_ref=src_ref,
            dst_ref=out_ref.at[s],
            send_sem=send_sems.at[w],
            recv_sem=recv_sems.at[s],
            device_id=(beta, b, w),
            device_id_type=MESH,
        )

    for w in range(nv):
        @pl.when(v != w)
        def _():
            remote(w, v).start()

    pltpu.make_async_copy(src_ref, out_ref.at[v], recv_sems.at[v]).start()
    for w in range(nv):
        @pl.when(v != w)
        def _():
            remote(w, v).wait_send()
    for s in range(nv):
        @pl.when(v != s)
        def _():
            remote(s, s).wait_recv()
    pltpu.make_async_copy(src_ref, out_ref.at[v], recv_sems.at[v]).wait()


def vocab_gather(block, nv, cid):
    size = block.size * block.dtype.itemsize
    return pl.pallas_call(
        functools.partial(gather_kernel, nv),
        out_shape=jax.ShapeDtypeStruct((nv,) + block.shape, block.dtype),
        in_specs=[pl.BlockSpec(memory_space=pltpu.VMEM)],
        out_specs=pl.BlockSpec(memory_space=pltpu.VMEM),
        scratch_shapes=[pltpu.SemaphoreType.DMA((nv,)), pltpu.SemaphoreType.DMA((nv,))],
        compiler_params=pltpu.CompilerParams(collective_id=cid, has_side_effects=True),
        cost_estimate=pl.CostEstimate(flops=0, transcendentals=0, bytes_accessed=2 * nv * size),
    )(block)


def scatter_kernel(npair, nb, src_ref, out_ref, send_sems, recv_sems):
    beta = lax.axis_index("pair")
    b = lax.axis_index("batch")
    v = lax.axis_index("vocab")
    groups = npair * nb
    me = beta * nb + b
    rows = out_ref.shape[3]
    depth = out_ref.shape[4]
    barrier = pltpu.get_barrier_semaphore()
    for k in range(1, groups):
        t = (me + k) % groups
        pl.semaphore_signal(barrier, inc=1, device_id=(t // nb, t % nb, v), device_id_type=MESH)
    pl.semaphore_wait(barrier, groups - 1)

    def piece(t, h):
        return src_ref.at[pl.ds(h * rows, rows), pl.ds(pl.multiple_of(t * depth, depth), depth)]

    def remote(k, h):
        t = (me + k) % groups
        return pltpu.make_async_remote_copy(
            src_ref=piece(t, h),
            dst_ref=out_ref.at[b, h, beta],
            send_sem=send_sems.at[k * 2 + h],
            recv_sem=recv_sems.at[(b * 2 + h) * npair + beta],
            device_id=(t // nb, t % nb, v),
            device_id_type=MESH,
        )

    def local(h):
        return pltpu.make_async_copy(
            piece(me, h), out_ref.at[b, h, beta], recv_sems.at[(b * 2 + h) * npair + beta])

    for k in range(1, groups):
        for h in range(2):
            remote(k, h).start()
    for h in range(2):
        local(h).start()
    for k in range(1, groups):
        for h in range(2):
            remote(k, h).wait_send()
    for k in range(1, groups):
        s = (me + k) % groups
        sp, sb = s // nb, s % nb
        for h in range(2):
            pltpu.make_async_remote_copy(
                src_ref=piece(me, h),
                dst_ref=out_ref.at[sb, h, sp],
                send_sem=send_sems.at[0],
                recv_sem=recv_sems.at[(sb * 2 + h) * npair + sp],
                device_id=(sp, sb, v),
                device_id_type=MESH,
            ).wait_recv()
    for h in range(2):
        local(h).wait()


def kblock_scatter(feats, npair, nb):
    groups = npair * nb
    rows = feats.shape[0] // 2
    depth = feats.shape[1] // groups
    size = feats.size * feats.dtype.itemsize
    return pl.pallas_call(
        functools.partial(scatter_kernel, npair, nb),
        out_shape=jax.ShapeDtypeStruct((nb, 2, npair, rows, depth), feats.dtype),
        in_specs=[pl.BlockSpec(memory_space=pltpu.VMEM)],
        out_specs=pl.BlockSpec(memory_space=pltpu.VMEM),
        scratch_shapes=[pltpu.SemaphoreType.DMA((2 * groups,)), pltpu.SemaphoreType.DMA((2 * groups,))],
        compiler_params=pltpu.CompilerParams(collective_id=0, has_side_effects=True),
        cost_estimate=pl.CostEstimate(flops=0, transcendentals=0, bytes_accessed=2 * size),
    )(feats)


def on_device(npair, nb, nv, hidden, norm_gain, head_weight):
    groups = npair * nb
    span = nv // groups
    local_rows, width = hidden.shape[1], hidden.shape[2]
    total_d = width * nv
    pad = jnp.zeros((15, width), hidden.dtype)
    block = jnp.concatenate([hidden[0], norm_gain[None, :], pad], axis=0)
    got = vocab_gather(block, nv, 1)
    wide = got[:, :local_rows, :].transpose(1, 0, 2).reshape(local_rows, total_d).astype(jnp.float32)
    gain = got[:, local_rows, :].reshape(total_d)
    meansq = jnp.sum(wide * wide, axis=1) / total_d
    scaled = wide * lax.rsqrt(meansq + EPS)[:, None] * gain.astype(jnp.float32)[None, :]
    features = scaled.astype(jnp.bfloat16)
    ordered = kblock_scatter(features, npair, nb).reshape(groups * local_rows, total_d // groups)
    half = local_rows // 2
    out_rows = half
    lanes = 128
    me = lax.axis_index("pair")
    half_rows = ordered.shape[0] // 2
    mine = lax.dynamic_slice_in_dim(ordered, me * half_rows, half_rows, axis=0)
    theirs = lax.dynamic_slice_in_dim(ordered, (1 - me) * half_rows, half_rows, axis=0)
    cols = head_weight.shape[1]
    step = cols // CHUNKS
    pieces = []
    for j in range(CHUNKS):
        w = head_weight[:, j * step:(j + 1) * step]
        sent = jnp.dot(theirs, w, preferred_element_type=jnp.float32)
        kept = jnp.dot(mine, w, preferred_element_type=jnp.float32)
        got_half = lax.ppermute(sent, "pair", [(0, 1), (1, 0)])
        pieces.append(lax.psum_scatter(kept + got_half, "batch", scatter_dimension=0, tiled=True))
    logits = jnp.concatenate(pieces, axis=1)
    cond = logits[:out_rows]
    uncond = logits[out_rows:]
    guided = GUIDE * cond + (1.0 - GUIDE) * uncond
    peak_c = jnp.max(cond, axis=1)
    peak_g = jnp.max(guided, axis=1)
    local_c = jnp.sum(jnp.exp(cond - peak_c[:, None]), axis=1)
    local_g = jnp.sum(jnp.exp(guided - peak_g[:, None]), axis=1)
    stats = jnp.zeros((8, lanes), jnp.float32).at[:4, :out_rows].set(
        jnp.stack([peak_c, local_c, peak_g, local_g]))
    every = vocab_gather(stats, nv, 2)[:, :4, :out_rows]
    top_c = jnp.max(every[:, 0], axis=0)
    top_g = jnp.max(every[:, 2], axis=0)
    total_c = jnp.sum(every[:, 1] * jnp.exp(every[:, 0] - top_c[None, :]), axis=0)
    total_g = jnp.sum(every[:, 3] * jnp.exp(every[:, 2] - top_g[None, :]), axis=0)
    cond_out = cond - (top_c + jnp.log(total_c))[:, None]
    guided_out = guided - (top_g + jnp.log(total_g))[:, None]
    return (guided_out, cond_out)


def solution(mesh):
    npair, nb, nv = mesh.shape["pair"], mesh.shape["batch"], mesh.shape["vocab"]
    in_specs = (P("pair", "batch", "vocab"), P("vocab"), P(("pair", "batch"), "vocab"))
    out_specs = (P(("pair", "batch"), "vocab"), P(("pair", "batch"), "vocab"))
    return jax.shard_map(
        functools.partial(on_device, npair, nb, nv),
        mesh=mesh, in_specs=in_specs, out_specs=out_specs, check_vma=False,
    )
```

```python
import functools

import jax
import jax.numpy as jnp
from jax import lax
from jax.experimental import pallas as pl
from jax.experimental.pallas import tpu as pltpu
from jax.sharding import PartitionSpec as P

MESH = pl.DeviceIdType.MESH

EPS = 1e-05
GUIDE = 1.5
CHUNKS = 2


def dispatch_kernel(npair, nb, nv, span, src_ref, out_ref, send_sems, recv_sems):
    beta = lax.axis_index("pair")
    b = lax.axis_index("batch")
    v = lax.axis_index("vocab")
    groups = npair * nb
    mine = beta * nb + b
    q = v // span
    tp = q // nb
    tb = q % nb
    slot = mine * span + v % span
    d = q - mine
    own = 1 - (d * d + groups * groups - 1) // (groups * groups)

    def sources(s):
        bs = s // (nb * span)
        bbs = (s // span) % nb
        sv = mine * span + s % span
        return bs, bbs, sv

    barrier = pltpu.get_barrier_semaphore()
    for w in range(nv):
        @pl.when(jnp.logical_not((tp == beta) & (tb == b) & (v == w)))
        def _():
            pl.semaphore_signal(barrier, inc=1, device_id=(tp, tb, w), device_id_type=MESH)
    for s in range(nv):
        bs, bbs, sv = sources(s)

        @pl.when(jnp.logical_not((bs == beta) & (bbs == b) & (sv == v)))
        def _():
            pl.semaphore_signal(barrier, inc=1, device_id=(bs, bbs, sv), device_id_type=MESH)
    pl.semaphore_wait(barrier, 2 * (nv - own))

    def remote(k):
        return pltpu.make_async_remote_copy(
            src_ref=src_ref,
            dst_ref=out_ref.at[slot],
            send_sem=send_sems.at[k],
            recv_sem=recv_sems.at[slot],
            device_id=(tp, tb, (k + slot) % nv),
            device_id_type=MESH,
        )

    for k in range(nv):
        here = (tp == beta) & (tb == b) & (v == (k + slot) % nv)

        @pl.when(jnp.logical_not(here))
        def _():
            remote(k).start()

        @pl.when(here)
        def _():
            pltpu.make_async_copy(src_ref, out_ref.at[slot], recv_sems.at[slot]).start()

    for k in range(nv):
        here = (tp == beta) & (tb == b) & (v == (k + slot) % nv)

        @pl.when(jnp.logical_not(here))
        def _():
            remote(k).wait_send()

    for s in range(nv):
        bs, bbs, sv = sources(s)
        here = (bs == beta) & (bbs == b) & (sv == v)

        @pl.when(jnp.logical_not(here))
        def _():
            pltpu.make_async_remote_copy(
                src_ref=src_ref,
                dst_ref=out_ref.at[s],
                send_sem=send_sems.at[0],
                recv_sem=recv_sems.at[s],
                device_id=(bs, bbs, sv),
                device_id_type=MESH,
            ).wait_recv()

        @pl.when(here)
        def _():
            pltpu.make_async_copy(src_ref, out_ref.at[s], recv_sems.at[s]).wait()


def dispatch(block, npair, nb, nv):
    span = nv // (npair * nb)
    size = block.size * block.dtype.itemsize
    return pl.pallas_call(
        functools.partial(dispatch_kernel, npair, nb, nv, span),
        out_shape=jax.ShapeDtypeStruct((nv,) + block.shape, block.dtype),
        in_specs=[pl.BlockSpec(memory_space=pltpu.VMEM)],
        out_specs=pl.BlockSpec(memory_space=pltpu.VMEM),
        scratch_shapes=[pltpu.SemaphoreType.DMA((nv,)), pltpu.SemaphoreType.DMA((nv,))],
        compiler_params=pltpu.CompilerParams(collective_id=0, has_side_effects=True),
        cost_estimate=pl.CostEstimate(flops=0, transcendentals=0, bytes_accessed=2 * nv * size),
    )(block)


def gather_kernel(nv, src_ref, out_ref, send_sems, recv_sems):
    beta = lax.axis_index("pair")
    b = lax.axis_index("batch")
    v = lax.axis_index("vocab")
    barrier = pltpu.get_barrier_semaphore()
    for k in range(1, nv):
        pl.semaphore_signal(barrier, inc=1, device_id=(beta, b, (v + k) % nv), device_id_type=MESH)
    pl.semaphore_wait(barrier, nv - 1)

    def remote(w, s):
        return pltpu.make_async_remote_copy(
            src_ref=src_ref,
            dst_ref=out_ref.at[s],
            send_sem=send_sems.at[w],
            recv_sem=recv_sems.at[s],
            device_id=(beta, b, w),
            device_id_type=MESH,
        )

    for k in range(1, nv):
        remote((v + k) % nv, v).start()

    pltpu.make_async_copy(src_ref, out_ref.at[v], recv_sems.at[v]).start()
    for k in range(1, nv):
        remote((v + k) % nv, v).wait_send()
    for k in range(1, nv):
        s = (v + k) % nv
        remote(s, s).wait_recv()
    pltpu.make_async_copy(src_ref, out_ref.at[v], recv_sems.at[v]).wait()


def vocab_gather(block, nv, cid):
    size = block.size * block.dtype.itemsize
    return pl.pallas_call(
        functools.partial(gather_kernel, nv),
        out_shape=jax.ShapeDtypeStruct((nv,) + block.shape, block.dtype),
        in_specs=[pl.BlockSpec(memory_space=pltpu.VMEM)],
        out_specs=pl.BlockSpec(memory_space=pltpu.VMEM),
        scratch_shapes=[pltpu.SemaphoreType.DMA((nv,)), pltpu.SemaphoreType.DMA((nv,))],
        compiler_params=pltpu.CompilerParams(collective_id=cid, has_side_effects=True),
        cost_estimate=pl.CostEstimate(flops=0, transcendentals=0, bytes_accessed=2 * nv * size),
    )(block)


def scatter_kernel(npair, nb, src_ref, out_ref, send_sems, recv_sems):
    beta = lax.axis_index("pair")
    b = lax.axis_index("batch")
    v = lax.axis_index("vocab")
    groups = npair * nb
    me = beta * nb + b
    rows = out_ref.shape[3]
    depth = out_ref.shape[4]
    barrier = pltpu.get_barrier_semaphore()
    for k in range(1, groups):
        t = (me + k) % groups
        pl.semaphore_signal(barrier, inc=1, device_id=(t // nb, t % nb, v), device_id_type=MESH)
    pl.semaphore_wait(barrier, groups - 1)

    def piece(t, h):
        return src_ref.at[pl.ds(h * rows, rows), pl.ds(pl.multiple_of(t * depth, depth), depth)]

    def remote(k, h):
        t = (me + k) % groups
        return pltpu.make_async_remote_copy(
            src_ref=piece(t, h),
            dst_ref=out_ref.at[b, h, beta],
            send_sem=send_sems.at[k * 2 + h],
            recv_sem=recv_sems.at[(b * 2 + h) * npair + beta],
            device_id=(t // nb, t % nb, v),
            device_id_type=MESH,
        )

    def local(h):
        return pltpu.make_async_copy(
            piece(me, h), out_ref.at[b, h, beta], recv_sems.at[(b * 2 + h) * npair + beta])

    for k in range(1, groups):
        for h in range(2):
            remote(k, h).start()
    for h in range(2):
        local(h).start()
    for k in range(1, groups):
        for h in range(2):
            remote(k, h).wait_send()
    for k in range(1, groups):
        s = (me + k) % groups
        sp, sb = s // nb, s % nb
        for h in range(2):
            pltpu.make_async_remote_copy(
                src_ref=piece(me, h),
                dst_ref=out_ref.at[sb, h, sp],
                send_sem=send_sems.at[0],
                recv_sem=recv_sems.at[(sb * 2 + h) * npair + sp],
                device_id=(sp, sb, v),
                device_id_type=MESH,
            ).wait_recv()
    for h in range(2):
        local(h).wait()


def kblock_scatter(feats, npair, nb):
    groups = npair * nb
    rows = feats.shape[0] // 2
    depth = feats.shape[1] // groups
    size = feats.size * feats.dtype.itemsize
    return pl.pallas_call(
        functools.partial(scatter_kernel, npair, nb),
        out_shape=jax.ShapeDtypeStruct((nb, 2, npair, rows, depth), feats.dtype),
        in_specs=[pl.BlockSpec(memory_space=pltpu.VMEM)],
        out_specs=pl.BlockSpec(memory_space=pltpu.VMEM),
        scratch_shapes=[pltpu.SemaphoreType.DMA((2 * groups,)), pltpu.SemaphoreType.DMA((2 * groups,))],
        compiler_params=pltpu.CompilerParams(collective_id=0, has_side_effects=True),
        cost_estimate=pl.CostEstimate(flops=0, transcendentals=0, bytes_accessed=2 * size),
    )(feats)


def on_device(npair, nb, nv, hidden, norm_gain, head_weight):
    groups = npair * nb
    span = nv // groups
    local_rows, width = hidden.shape[1], hidden.shape[2]
    total_d = width * nv
    pad = jnp.zeros((15, width), hidden.dtype)
    block = jnp.concatenate([hidden[0], norm_gain[None, :], pad], axis=0)
    got = vocab_gather(block, nv, 1)
    wide = got[:, :local_rows, :].transpose(1, 0, 2).reshape(local_rows, total_d).astype(jnp.float32)
    gain = got[:, local_rows, :].reshape(total_d)
    meansq = jnp.sum(wide * wide, axis=1) / total_d
    scaled = wide * lax.rsqrt(meansq + EPS)[:, None] * gain.astype(jnp.float32)[None, :]
    features = scaled.astype(jnp.bfloat16)
    ordered = kblock_scatter(features, npair, nb).reshape(groups * local_rows, total_d // groups)
    half = local_rows // 2
    out_rows = half
    lanes = 128
    me = lax.axis_index("pair")
    half_rows = ordered.shape[0] // 2
    mine = lax.dynamic_slice_in_dim(ordered, me * half_rows, half_rows, axis=0)
    theirs = lax.dynamic_slice_in_dim(ordered, (1 - me) * half_rows, half_rows, axis=0)
    cols = head_weight.shape[1]
    step = cols // CHUNKS
    pieces = []
    for j in range(CHUNKS):
        w = head_weight[:, j * step:(j + 1) * step]
        sent = jnp.dot(theirs, w, preferred_element_type=jnp.float32)
        kept = jnp.dot(mine, w, preferred_element_type=jnp.float32)
        got_half = lax.ppermute(sent, "pair", [(0, 1), (1, 0)])
        pieces.append(lax.psum_scatter(kept + got_half, "batch", scatter_dimension=0, tiled=True))
    logits = jnp.concatenate(pieces, axis=1)
    cond = logits[:out_rows]
    uncond = logits[out_rows:]
    guided = GUIDE * cond + (1.0 - GUIDE) * uncond
    peak_c = jnp.max(cond, axis=1)
    peak_g = jnp.max(guided, axis=1)
    local_c = jnp.sum(jnp.exp(cond - peak_c[:, None]), axis=1)
    local_g = jnp.sum(jnp.exp(guided - peak_g[:, None]), axis=1)
    stats = jnp.zeros((8, lanes), jnp.float32).at[:4, :out_rows].set(
        jnp.stack([peak_c, local_c, peak_g, local_g]))
    every = vocab_gather(stats, nv, 2)[:, :4, :out_rows]
    top_c = jnp.max(every[:, 0], axis=0)
    top_g = jnp.max(every[:, 2], axis=0)
    total_c = jnp.sum(every[:, 1] * jnp.exp(every[:, 0] - top_c[None, :]), axis=0)
    total_g = jnp.sum(every[:, 3] * jnp.exp(every[:, 2] - top_g[None, :]), axis=0)
    cond_out = cond - (top_c + jnp.log(total_c))[:, None]
    guided_out = guided - (top_g + jnp.log(total_g))[:, None]
    return (guided_out, cond_out)


def solution(mesh):
    npair, nb, nv = mesh.shape["pair"], mesh.shape["batch"], mesh.shape["vocab"]
    in_specs = (P("pair", "batch", "vocab"), P("vocab"), P(("pair", "batch"), "vocab"))
    out_specs = (P(("pair", "batch"), "vocab"), P(("pair", "batch"), "vocab"))
    return jax.shard_map(
        functools.partial(on_device, npair, nb, nv),
        mesh=mesh, in_specs=in_specs, out_specs=out_specs, check_vma=False,
    )
```

```python
import functools

import jax
import jax.numpy as jnp
from jax import lax
from jax.experimental import pallas as pl
from jax.experimental.pallas import tpu as pltpu
from jax.sharding import PartitionSpec as P

MESH = pl.DeviceIdType.MESH

EPS = 1e-05
GUIDE = 1.5


def dispatch_kernel(npair, nb, nv, span, src_ref, out_ref, send_sems, recv_sems):
    beta = lax.axis_index("pair")
    b = lax.axis_index("batch")
    v = lax.axis_index("vocab")
    groups = npair * nb
    mine = beta * nb + b
    q = v // span
    tp = q // nb
    tb = q % nb
    slot = mine * span + v % span
    d = q - mine
    own = 1 - (d * d + groups * groups - 1) // (groups * groups)

    def sources(s):
        bs = s // (nb * span)
        bbs = (s // span) % nb
        sv = mine * span + s % span
        return bs, bbs, sv

    barrier = pltpu.get_barrier_semaphore()
    for w in range(nv):
        @pl.when(jnp.logical_not((tp == beta) & (tb == b) & (v == w)))
        def _():
            pl.semaphore_signal(barrier, inc=1, device_id=(tp, tb, w), device_id_type=MESH)
    for s in range(nv):
        bs, bbs, sv = sources(s)

        @pl.when(jnp.logical_not((bs == beta) & (bbs == b) & (sv == v)))
        def _():
            pl.semaphore_signal(barrier, inc=1, device_id=(bs, bbs, sv), device_id_type=MESH)
    pl.semaphore_wait(barrier, 2 * (nv - own))

    def remote(k):
        return pltpu.make_async_remote_copy(
            src_ref=src_ref,
            dst_ref=out_ref.at[slot],
            send_sem=send_sems.at[k],
            recv_sem=recv_sems.at[slot],
            device_id=(tp, tb, (k + slot) % nv),
            device_id_type=MESH,
        )

    for k in range(nv):
        here = (tp == beta) & (tb == b) & (v == (k + slot) % nv)

        @pl.when(jnp.logical_not(here))
        def _():
            remote(k).start()

        @pl.when(here)
        def _():
            pltpu.make_async_copy(src_ref, out_ref.at[slot], recv_sems.at[slot]).start()

    for k in range(nv):
        here = (tp == beta) & (tb == b) & (v == (k + slot) % nv)

        @pl.when(jnp.logical_not(here))
        def _():
            remote(k).wait_send()

    for s in range(nv):
        bs, bbs, sv = sources(s)
        here = (bs == beta) & (bbs == b) & (sv == v)

        @pl.when(jnp.logical_not(here))
        def _():
            pltpu.make_async_remote_copy(
                src_ref=src_ref,
                dst_ref=out_ref.at[s],
                send_sem=send_sems.at[0],
                recv_sem=recv_sems.at[s],
                device_id=(bs, bbs, sv),
                device_id_type=MESH,
            ).wait_recv()

        @pl.when(here)
        def _():
            pltpu.make_async_copy(src_ref, out_ref.at[s], recv_sems.at[s]).wait()


def dispatch(block, npair, nb, nv):
    span = nv // (npair * nb)
    size = block.size * block.dtype.itemsize
    return pl.pallas_call(
        functools.partial(dispatch_kernel, npair, nb, nv, span),
        out_shape=jax.ShapeDtypeStruct((nv,) + block.shape, block.dtype),
        in_specs=[pl.BlockSpec(memory_space=pltpu.VMEM)],
        out_specs=pl.BlockSpec(memory_space=pltpu.VMEM),
        scratch_shapes=[pltpu.SemaphoreType.DMA((nv,)), pltpu.SemaphoreType.DMA((nv,))],
        compiler_params=pltpu.CompilerParams(collective_id=0, has_side_effects=True),
        cost_estimate=pl.CostEstimate(flops=0, transcendentals=0, bytes_accessed=2 * nv * size),
    )(block)


def gather_kernel(nv, src_ref, out_ref, send_sems, recv_sems):
    beta = lax.axis_index("pair")
    b = lax.axis_index("batch")
    v = lax.axis_index("vocab")
    barrier = pltpu.get_barrier_semaphore()
    for k in range(1, nv):
        pl.semaphore_signal(barrier, inc=1, device_id=(beta, b, (v + k) % nv), device_id_type=MESH)
    pl.semaphore_wait(barrier, nv - 1)

    def remote(w, s):
        return pltpu.make_async_remote_copy(
            src_ref=src_ref,
            dst_ref=out_ref.at[s],
            send_sem=send_sems.at[w],
            recv_sem=recv_sems.at[s],
            device_id=(beta, b, w),
            device_id_type=MESH,
        )

    for k in range(1, nv):
        remote((v + k) % nv, v).start()

    pltpu.make_async_copy(src_ref, out_ref.at[v], recv_sems.at[v]).start()
    for k in range(1, nv):
        remote((v + k) % nv, v).wait_send()
    for k in range(1, nv):
        s = (v + k) % nv
        remote(s, s).wait_recv()
    pltpu.make_async_copy(src_ref, out_ref.at[v], recv_sems.at[v]).wait()


def vocab_gather(block, nv, cid):
    size = block.size * block.dtype.itemsize
    return pl.pallas_call(
        functools.partial(gather_kernel, nv),
        out_shape=jax.ShapeDtypeStruct((nv,) + block.shape, block.dtype),
        in_specs=[pl.BlockSpec(memory_space=pltpu.VMEM)],
        out_specs=pl.BlockSpec(memory_space=pltpu.VMEM),
        scratch_shapes=[pltpu.SemaphoreType.DMA((nv,)), pltpu.SemaphoreType.DMA((nv,))],
        compiler_params=pltpu.CompilerParams(collective_id=cid, has_side_effects=True),
        cost_estimate=pl.CostEstimate(flops=0, transcendentals=0, bytes_accessed=2 * nv * size),
    )(block)


def scatter_kernel(npair, nb, src_ref, out_ref, send_sems, recv_sems):
    beta = lax.axis_index("pair")
    b = lax.axis_index("batch")
    v = lax.axis_index("vocab")
    groups = npair * nb
    me = beta * nb + b
    rows = out_ref.shape[3]
    depth = out_ref.shape[4]
    barrier = pltpu.get_barrier_semaphore()
    for k in range(1, groups):
        t = (me + k) % groups
        pl.semaphore_signal(barrier, inc=1, device_id=(t // nb, t % nb, v), device_id_type=MESH)
    pl.semaphore_wait(barrier, groups - 1)

    def piece(t, h):
        return src_ref.at[pl.ds(h * rows, rows), pl.ds(pl.multiple_of(t * depth, depth), depth)]

    def remote(k, h):
        t = (me + k) % groups
        return pltpu.make_async_remote_copy(
            src_ref=piece(t, h),
            dst_ref=out_ref.at[b, h, beta],
            send_sem=send_sems.at[k * 2 + h],
            recv_sem=recv_sems.at[(b * 2 + h) * npair + beta],
            device_id=(t // nb, t % nb, v),
            device_id_type=MESH,
        )

    def local(h):
        return pltpu.make_async_copy(
            piece(me, h), out_ref.at[b, h, beta], recv_sems.at[(b * 2 + h) * npair + beta])

    for k in range(1, groups):
        for h in range(2):
            remote(k, h).start()
    for h in range(2):
        local(h).start()
    for k in range(1, groups):
        for h in range(2):
            remote(k, h).wait_send()
    for k in range(1, groups):
        s = (me + k) % groups
        sp, sb = s // nb, s % nb
        for h in range(2):
            pltpu.make_async_remote_copy(
                src_ref=piece(me, h),
                dst_ref=out_ref.at[sb, h, sp],
                send_sem=send_sems.at[0],
                recv_sem=recv_sems.at[(sb * 2 + h) * npair + sp],
                device_id=(sp, sb, v),
                device_id_type=MESH,
            ).wait_recv()
    for h in range(2):
        local(h).wait()


def kblock_scatter(feats, npair, nb):
    groups = npair * nb
    rows = feats.shape[0] // 2
    depth = feats.shape[1] // groups
    size = feats.size * feats.dtype.itemsize
    return pl.pallas_call(
        functools.partial(scatter_kernel, npair, nb),
        out_shape=jax.ShapeDtypeStruct((nb, 2, npair, rows, depth), feats.dtype),
        in_specs=[pl.BlockSpec(memory_space=pltpu.VMEM)],
        out_specs=pl.BlockSpec(memory_space=pltpu.VMEM),
        scratch_shapes=[pltpu.SemaphoreType.DMA((2 * groups,)), pltpu.SemaphoreType.DMA((2 * groups,))],
        compiler_params=pltpu.CompilerParams(collective_id=0, has_side_effects=True),
        cost_estimate=pl.CostEstimate(flops=0, transcendentals=0, bytes_accessed=2 * size),
    )(feats)


def on_device(npair, nb, nv, hidden, norm_gain, head_weight):
    groups = npair * nb
    span = nv // groups
    local_rows, width = hidden.shape[1], hidden.shape[2]
    total_d = width * nv
    pad = jnp.zeros((15, width), hidden.dtype)
    block = jnp.concatenate([hidden[0], norm_gain[None, :], pad], axis=0)
    got = vocab_gather(block, nv, 1)
    wide = got[:, :local_rows, :].transpose(1, 0, 2).reshape(local_rows, total_d).astype(jnp.float32)
    gain = got[:, local_rows, :].reshape(total_d)
    meansq = jnp.sum(wide * wide, axis=1) / total_d
    scaled = wide * lax.rsqrt(meansq + EPS)[:, None] * gain.astype(jnp.float32)[None, :]
    features = scaled.astype(jnp.bfloat16)
    ordered = kblock_scatter(features, npair, nb).reshape(groups * local_rows, total_d // groups)
    half = local_rows // 2
    out_rows = half
    lanes = 128
    me = lax.axis_index("pair")
    half_rows = ordered.shape[0] // 2
    mine = lax.dynamic_slice_in_dim(ordered, me * half_rows, half_rows, axis=0)
    theirs = lax.dynamic_slice_in_dim(ordered, (1 - me) * half_rows, half_rows, axis=0)
    cols = head_weight.shape[1]
    edges = [0, cols // 4, cols]
    pieces = []
    for j in range(len(edges) - 1):
        w = head_weight[:, edges[j]:edges[j + 1]]
        sent = jnp.dot(theirs, w, preferred_element_type=jnp.float32)
        kept = jnp.dot(mine, w, preferred_element_type=jnp.float32)
        got_half = lax.ppermute(sent, "pair", [(0, 1), (1, 0)])
        pieces.append(lax.psum_scatter(kept + got_half, "batch", scatter_dimension=0, tiled=True))
    logits = jnp.concatenate(pieces, axis=1)
    cond = logits[:out_rows]
    uncond = logits[out_rows:]
    guided = GUIDE * cond + (1.0 - GUIDE) * uncond
    peak_c = jnp.max(cond, axis=1)
    peak_g = jnp.max(guided, axis=1)
    local_c = jnp.sum(jnp.exp(cond - peak_c[:, None]), axis=1)
    local_g = jnp.sum(jnp.exp(guided - peak_g[:, None]), axis=1)
    stats = jnp.zeros((8, lanes), jnp.float32).at[:4, :out_rows].set(
        jnp.stack([peak_c, local_c, peak_g, local_g]))
    every = vocab_gather(stats, nv, 2)[:, :4, :out_rows]
    top_c = jnp.max(every[:, 0], axis=0)
    top_g = jnp.max(every[:, 2], axis=0)
    total_c = jnp.sum(every[:, 1] * jnp.exp(every[:, 0] - top_c[None, :]), axis=0)
    total_g = jnp.sum(every[:, 3] * jnp.exp(every[:, 2] - top_g[None, :]), axis=0)
    cond_out = cond - (top_c + jnp.log(total_c))[:, None]
    guided_out = guided - (top_g + jnp.log(total_g))[:, None]
    return (guided_out, cond_out)


def solution(mesh):
    npair, nb, nv = mesh.shape["pair"], mesh.shape["batch"], mesh.shape["vocab"]
    in_specs = (P("pair", "batch", "vocab"), P("vocab"), P(("pair", "batch"), "vocab"))
    out_specs = (P(("pair", "batch"), "vocab"), P(("pair", "batch"), "vocab"))
    return jax.shard_map(
        functools.partial(on_device, npair, nb, nv),
        mesh=mesh, in_specs=in_specs, out_specs=out_specs, check_vma=False,
    )
```

```python
import functools

import jax
import jax.numpy as jnp
from jax import lax
from jax.experimental import pallas as pl
from jax.experimental.pallas import tpu as pltpu
from jax.sharding import PartitionSpec as P

MESH = pl.DeviceIdType.MESH

EPS = 1e-05
GUIDE = 1.5


def dispatch_kernel(npair, nb, nv, span, src_ref, out_ref, send_sems, recv_sems):
    beta = lax.axis_index("pair")
    b = lax.axis_index("batch")
    v = lax.axis_index("vocab")
    groups = npair * nb
    mine = beta * nb + b
    q = v // span
    tp = q // nb
    tb = q % nb
    slot = mine * span + v % span
    d = q - mine
    own = 1 - (d * d + groups * groups - 1) // (groups * groups)

    def sources(s):
        bs = s // (nb * span)
        bbs = (s // span) % nb
        sv = mine * span + s % span
        return bs, bbs, sv

    barrier = pltpu.get_barrier_semaphore()
    for w in range(nv):
        @pl.when(jnp.logical_not((tp == beta) & (tb == b) & (v == w)))
        def _():
            pl.semaphore_signal(barrier, inc=1, device_id=(tp, tb, w), device_id_type=MESH)
    for s in range(nv):
        bs, bbs, sv = sources(s)

        @pl.when(jnp.logical_not((bs == beta) & (bbs == b) & (sv == v)))
        def _():
            pl.semaphore_signal(barrier, inc=1, device_id=(bs, bbs, sv), device_id_type=MESH)
    pl.semaphore_wait(barrier, 2 * (nv - own))

    def remote(k):
        return pltpu.make_async_remote_copy(
            src_ref=src_ref,
            dst_ref=out_ref.at[slot],
            send_sem=send_sems.at[k],
            recv_sem=recv_sems.at[slot],
            device_id=(tp, tb, (k + slot) % nv),
            device_id_type=MESH,
        )

    for k in range(nv):
        here = (tp == beta) & (tb == b) & (v == (k + slot) % nv)

        @pl.when(jnp.logical_not(here))
        def _():
            remote(k).start()

        @pl.when(here)
        def _():
            pltpu.make_async_copy(src_ref, out_ref.at[slot], recv_sems.at[slot]).start()

    for k in range(nv):
        here = (tp == beta) & (tb == b) & (v == (k + slot) % nv)

        @pl.when(jnp.logical_not(here))
        def _():
            remote(k).wait_send()

    for s in range(nv):
        bs, bbs, sv = sources(s)
        here = (bs == beta) & (bbs == b) & (sv == v)

        @pl.when(jnp.logical_not(here))
        def _():
            pltpu.make_async_remote_copy(
                src_ref=src_ref,
                dst_ref=out_ref.at[s],
                send_sem=send_sems.at[0],
                recv_sem=recv_sems.at[s],
                device_id=(bs, bbs, sv),
                device_id_type=MESH,
            ).wait_recv()

        @pl.when(here)
        def _():
            pltpu.make_async_copy(src_ref, out_ref.at[s], recv_sems.at[s]).wait()


def dispatch(block, npair, nb, nv):
    span = nv // (npair * nb)
    size = block.size * block.dtype.itemsize
    return pl.pallas_call(
        functools.partial(dispatch_kernel, npair, nb, nv, span),
        out_shape=jax.ShapeDtypeStruct((nv,) + block.shape, block.dtype),
        in_specs=[pl.BlockSpec(memory_space=pltpu.VMEM)],
        out_specs=pl.BlockSpec(memory_space=pltpu.VMEM),
        scratch_shapes=[pltpu.SemaphoreType.DMA((nv,)), pltpu.SemaphoreType.DMA((nv,))],
        compiler_params=pltpu.CompilerParams(collective_id=0, has_side_effects=True),
        cost_estimate=pl.CostEstimate(flops=0, transcendentals=0, bytes_accessed=2 * nv * size),
    )(block)


def gather_kernel(nv, src_ref, out_ref, send_sems, recv_sems):
    beta = lax.axis_index("pair")
    b = lax.axis_index("batch")
    v = lax.axis_index("vocab")
    barrier = pltpu.get_barrier_semaphore()
    for k in range(1, nv):
        pl.semaphore_signal(barrier, inc=1, device_id=(beta, b, (v + k) % nv), device_id_type=MESH)
    pl.semaphore_wait(barrier, nv - 1)

    def remote(w, s):
        return pltpu.make_async_remote_copy(
            src_ref=src_ref,
            dst_ref=out_ref.at[s],
            send_sem=send_sems.at[w],
            recv_sem=recv_sems.at[s],
            device_id=(beta, b, w),
            device_id_type=MESH,
        )

    for k in range(1, nv):
        remote((v + k) % nv, v).start()

    pltpu.make_async_copy(src_ref, out_ref.at[v], recv_sems.at[v]).start()
    for k in range(1, nv):
        remote((v + k) % nv, v).wait_send()
    for k in range(1, nv):
        s = (v + k) % nv
        remote(s, s).wait_recv()
    pltpu.make_async_copy(src_ref, out_ref.at[v], recv_sems.at[v]).wait()


def vocab_gather(block, nv, cid):
    size = block.size * block.dtype.itemsize
    return pl.pallas_call(
        functools.partial(gather_kernel, nv),
        out_shape=jax.ShapeDtypeStruct((nv,) + block.shape, block.dtype),
        in_specs=[pl.BlockSpec(memory_space=pltpu.VMEM)],
        out_specs=pl.BlockSpec(memory_space=pltpu.VMEM),
        scratch_shapes=[pltpu.SemaphoreType.DMA((nv,)), pltpu.SemaphoreType.DMA((nv,))],
        compiler_params=pltpu.CompilerParams(collective_id=cid, has_side_effects=True),
        cost_estimate=pl.CostEstimate(flops=0, transcendentals=0, bytes_accessed=2 * nv * size),
    )(block)


def scatter_kernel(npair, nb, src_ref, out_ref, send_sems, recv_sems):
    beta = lax.axis_index("pair")
    b = lax.axis_index("batch")
    v = lax.axis_index("vocab")
    groups = npair * nb
    me = beta * nb + b
    rows = out_ref.shape[3]
    depth = out_ref.shape[4]
    barrier = pltpu.get_barrier_semaphore()
    for k in range(1, groups):
        t = (me + k) % groups
        pl.semaphore_signal(barrier, inc=1, device_id=(t // nb, t % nb, v), device_id_type=MESH)
    pl.semaphore_wait(barrier, groups - 1)

    def piece(t, h):
        return src_ref.at[pl.ds(h * rows, rows), pl.ds(pl.multiple_of(t * depth, depth), depth)]

    def remote(k, h):
        t = (me + k) % groups
        return pltpu.make_async_remote_copy(
            src_ref=piece(t, h),
            dst_ref=out_ref.at[b, h, beta],
            send_sem=send_sems.at[k * 2 + h],
            recv_sem=recv_sems.at[(b * 2 + h) * npair + beta],
            device_id=(t // nb, t % nb, v),
            device_id_type=MESH,
        )

    def local(h):
        return pltpu.make_async_copy(
            piece(me, h), out_ref.at[b, h, beta], recv_sems.at[(b * 2 + h) * npair + beta])

    for k in range(1, groups):
        for h in range(2):
            remote(k, h).start()
    for h in range(2):
        local(h).start()
    for k in range(1, groups):
        for h in range(2):
            remote(k, h).wait_send()
    for k in range(1, groups):
        s = (me + k) % groups
        sp, sb = s // nb, s % nb
        for h in range(2):
            pltpu.make_async_remote_copy(
                src_ref=piece(me, h),
                dst_ref=out_ref.at[sb, h, sp],
                send_sem=send_sems.at[0],
                recv_sem=recv_sems.at[(sb * 2 + h) * npair + sp],
                device_id=(sp, sb, v),
                device_id_type=MESH,
            ).wait_recv()
    for h in range(2):
        local(h).wait()


def kblock_scatter(feats, npair, nb):
    groups = npair * nb
    rows = feats.shape[0] // 2
    depth = feats.shape[1] // groups
    size = feats.size * feats.dtype.itemsize
    return pl.pallas_call(
        functools.partial(scatter_kernel, npair, nb),
        out_shape=jax.ShapeDtypeStruct((nb, 2, npair, rows, depth), feats.dtype),
        in_specs=[pl.BlockSpec(memory_space=pltpu.VMEM)],
        out_specs=pl.BlockSpec(memory_space=pltpu.VMEM),
        scratch_shapes=[pltpu.SemaphoreType.DMA((2 * groups,)), pltpu.SemaphoreType.DMA((2 * groups,))],
        compiler_params=pltpu.CompilerParams(collective_id=0, has_side_effects=True),
        cost_estimate=pl.CostEstimate(flops=0, transcendentals=0, bytes_accessed=2 * size),
    )(feats)


def on_device(npair, nb, nv, hidden, norm_gain, head_weight):
    groups = npair * nb
    span = nv // groups
    local_rows, width = hidden.shape[1], hidden.shape[2]
    total_d = width * nv
    pad = jnp.zeros((15, width), hidden.dtype)
    block = jnp.concatenate([hidden[0], norm_gain[None, :], pad], axis=0)
    got = vocab_gather(block, nv, 1)
    wide = got[:, :local_rows, :].transpose(1, 0, 2).reshape(local_rows, total_d).astype(jnp.float32)
    gain = got[:, local_rows, :].reshape(total_d)
    meansq = jnp.sum(wide * wide, axis=1) / total_d
    scaled = wide * lax.rsqrt(meansq + EPS)[:, None] * gain.astype(jnp.float32)[None, :]
    features = scaled.astype(jnp.bfloat16)
    ordered = kblock_scatter(features, npair, nb).reshape(groups * local_rows, total_d // groups)
    half = local_rows // 2
    out_rows = half
    lanes = 128
    me = lax.axis_index("pair")
    half_rows = ordered.shape[0] // 2
    mine = lax.dynamic_slice_in_dim(ordered, me * half_rows, half_rows, axis=0)
    theirs = lax.dynamic_slice_in_dim(ordered, (1 - me) * half_rows, half_rows, axis=0)
    cols = head_weight.shape[1]
    edges = [0, cols // 4, cols]
    pieces = []
    weight = head_weight
    for j in range(len(edges) - 1):
        w = weight[:, edges[j]:edges[j + 1]]
        sent = jnp.dot(theirs, w, preferred_element_type=jnp.float32)
        kept = jnp.dot(mine, w, preferred_element_type=jnp.float32)
        got_half = lax.ppermute(sent, "pair", [(0, 1), (1, 0)])
        summed = kept + got_half
        summed, weight, theirs, mine = lax.optimization_barrier((summed, weight, theirs, mine))
        pieces.append(lax.psum_scatter(summed, "batch", scatter_dimension=0, tiled=True))
    logits = jnp.concatenate(pieces, axis=1)
    cond = logits[:out_rows]
    uncond = logits[out_rows:]
    guided = GUIDE * cond + (1.0 - GUIDE) * uncond
    peak_c = jnp.max(cond, axis=1)
    peak_g = jnp.max(guided, axis=1)
    local_c = jnp.sum(jnp.exp(cond - peak_c[:, None]), axis=1)
    local_g = jnp.sum(jnp.exp(guided - peak_g[:, None]), axis=1)
    stats = jnp.zeros((8, lanes), jnp.float32).at[:4, :out_rows].set(
        jnp.stack([peak_c, local_c, peak_g, local_g]))
    every = vocab_gather(stats, nv, 2)[:, :4, :out_rows]
    top_c = jnp.max(every[:, 0], axis=0)
    top_g = jnp.max(every[:, 2], axis=0)
    total_c = jnp.sum(every[:, 1] * jnp.exp(every[:, 0] - top_c[None, :]), axis=0)
    total_g = jnp.sum(every[:, 3] * jnp.exp(every[:, 2] - top_g[None, :]), axis=0)
    cond_out = cond - (top_c + jnp.log(total_c))[:, None]
    guided_out = guided - (top_g + jnp.log(total_g))[:, None]
    return (guided_out, cond_out)


def solution(mesh):
    npair, nb, nv = mesh.shape["pair"], mesh.shape["batch"], mesh.shape["vocab"]
    in_specs = (P("pair", "batch", "vocab"), P("vocab"), P(("pair", "batch"), "vocab"))
    out_specs = (P(("pair", "batch"), "vocab"), P(("pair", "batch"), "vocab"))
    return jax.shard_map(
        functools.partial(on_device, npair, nb, nv),
        mesh=mesh, in_specs=in_specs, out_specs=out_specs, check_vma=False,
    )
```

```python
import functools

import jax
import jax.numpy as jnp
from jax import lax
from jax.experimental import pallas as pl
from jax.experimental.pallas import tpu as pltpu
from jax.sharding import PartitionSpec as P

MESH = pl.DeviceIdType.MESH

EPS = 1e-05
GUIDE = 1.5


def dispatch_kernel(npair, nb, nv, span, src_ref, out_ref, send_sems, recv_sems):
    beta = lax.axis_index("pair")
    b = lax.axis_index("batch")
    v = lax.axis_index("vocab")
    groups = npair * nb
    mine = beta * nb + b
    q = v // span
    tp = q // nb
    tb = q % nb
    slot = mine * span + v % span
    d = q - mine
    own = 1 - (d * d + groups * groups - 1) // (groups * groups)

    def sources(s):
        bs = s // (nb * span)
        bbs = (s // span) % nb
        sv = mine * span + s % span
        return bs, bbs, sv

    barrier = pltpu.get_barrier_semaphore()
    for w in range(nv):
        @pl.when(jnp.logical_not((tp == beta) & (tb == b) & (v == w)))
        def _():
            pl.semaphore_signal(barrier, inc=1, device_id=(tp, tb, w), device_id_type=MESH)
    for s in range(nv):
        bs, bbs, sv = sources(s)

        @pl.when(jnp.logical_not((bs == beta) & (bbs == b) & (sv == v)))
        def _():
            pl.semaphore_signal(barrier, inc=1, device_id=(bs, bbs, sv), device_id_type=MESH)
    pl.semaphore_wait(barrier, 2 * (nv - own))

    def remote(k):
        return pltpu.make_async_remote_copy(
            src_ref=src_ref,
            dst_ref=out_ref.at[slot],
            send_sem=send_sems.at[k],
            recv_sem=recv_sems.at[slot],
            device_id=(tp, tb, (k + slot) % nv),
            device_id_type=MESH,
        )

    for k in range(nv):
        here = (tp == beta) & (tb == b) & (v == (k + slot) % nv)

        @pl.when(jnp.logical_not(here))
        def _():
            remote(k).start()

        @pl.when(here)
        def _():
            pltpu.make_async_copy(src_ref, out_ref.at[slot], recv_sems.at[slot]).start()

    for k in range(nv):
        here = (tp == beta) & (tb == b) & (v == (k + slot) % nv)

        @pl.when(jnp.logical_not(here))
        def _():
            remote(k).wait_send()

    for s in range(nv):
        bs, bbs, sv = sources(s)
        here = (bs == beta) & (bbs == b) & (sv == v)

        @pl.when(jnp.logical_not(here))
        def _():
            pltpu.make_async_remote_copy(
                src_ref=src_ref,
                dst_ref=out_ref.at[s],
                send_sem=send_sems.at[0],
                recv_sem=recv_sems.at[s],
                device_id=(bs, bbs, sv),
                device_id_type=MESH,
            ).wait_recv()

        @pl.when(here)
        def _():
            pltpu.make_async_copy(src_ref, out_ref.at[s], recv_sems.at[s]).wait()


def dispatch(block, npair, nb, nv):
    span = nv // (npair * nb)
    size = block.size * block.dtype.itemsize
    return pl.pallas_call(
        functools.partial(dispatch_kernel, npair, nb, nv, span),
        out_shape=jax.ShapeDtypeStruct((nv,) + block.shape, block.dtype),
        in_specs=[pl.BlockSpec(memory_space=pltpu.VMEM)],
        out_specs=pl.BlockSpec(memory_space=pltpu.VMEM),
        scratch_shapes=[pltpu.SemaphoreType.DMA((nv,)), pltpu.SemaphoreType.DMA((nv,))],
        compiler_params=pltpu.CompilerParams(collective_id=0, has_side_effects=True),
        cost_estimate=pl.CostEstimate(flops=0, transcendentals=0, bytes_accessed=2 * nv * size),
    )(block)


def gather_kernel(nv, src_ref, out_ref, send_sems, recv_sems):
    beta = lax.axis_index("pair")
    b = lax.axis_index("batch")
    v = lax.axis_index("vocab")
    barrier = pltpu.get_barrier_semaphore()
    for k in range(1, nv):
        pl.semaphore_signal(barrier, inc=1, device_id=(beta, b, (v + k) % nv), device_id_type=MESH)
    pl.semaphore_wait(barrier, nv - 1)

    def remote(w, s):
        return pltpu.make_async_remote_copy(
            src_ref=src_ref,
            dst_ref=out_ref.at[s],
            send_sem=send_sems.at[w],
            recv_sem=recv_sems.at[s],
            device_id=(beta, b, w),
            device_id_type=MESH,
        )

    for k in range(1, nv):
        remote((v + k) % nv, v).start()

    pltpu.make_async_copy(src_ref, out_ref.at[v], recv_sems.at[v]).start()
    for k in range(1, nv):
        remote((v + k) % nv, v).wait_send()
    for k in range(1, nv):
        s = (v + k) % nv
        remote(s, s).wait_recv()
    pltpu.make_async_copy(src_ref, out_ref.at[v], recv_sems.at[v]).wait()


def vocab_gather(block, nv, cid):
    size = block.size * block.dtype.itemsize
    return pl.pallas_call(
        functools.partial(gather_kernel, nv),
        out_shape=jax.ShapeDtypeStruct((nv,) + block.shape, block.dtype),
        in_specs=[pl.BlockSpec(memory_space=pltpu.VMEM)],
        out_specs=pl.BlockSpec(memory_space=pltpu.VMEM),
        scratch_shapes=[pltpu.SemaphoreType.DMA((nv,)), pltpu.SemaphoreType.DMA((nv,))],
        compiler_params=pltpu.CompilerParams(collective_id=cid, has_side_effects=True),
        cost_estimate=pl.CostEstimate(flops=0, transcendentals=0, bytes_accessed=2 * nv * size),
    )(block)


def scatter_kernel(npair, nb, src_ref, out_ref, send_sems, recv_sems):
    beta = lax.axis_index("pair")
    b = lax.axis_index("batch")
    v = lax.axis_index("vocab")
    groups = npair * nb
    me = beta * nb + b
    rows = out_ref.shape[3]
    depth = out_ref.shape[4]
    barrier = pltpu.get_barrier_semaphore()
    for k in range(1, groups):
        t = (me + k) % groups
        pl.semaphore_signal(barrier, inc=1, device_id=(t // nb, t % nb, v), device_id_type=MESH)
    pl.semaphore_wait(barrier, groups - 1)

    def piece(t, h):
        return src_ref.at[pl.ds(h * rows, rows), pl.ds(pl.multiple_of(t * depth, depth), depth)]

    def remote(k, h):
        t = (me + k) % groups
        return pltpu.make_async_remote_copy(
            src_ref=piece(t, h),
            dst_ref=out_ref.at[b, h, beta],
            send_sem=send_sems.at[k * 2 + h],
            recv_sem=recv_sems.at[(b * 2 + h) * npair + beta],
            device_id=(t // nb, t % nb, v),
            device_id_type=MESH,
        )

    def local(h):
        return pltpu.make_async_copy(
            piece(me, h), out_ref.at[b, h, beta], recv_sems.at[(b * 2 + h) * npair + beta])

    for k in range(1, groups):
        for h in range(2):
            remote(k, h).start()
    for h in range(2):
        local(h).start()
    for k in range(1, groups):
        for h in range(2):
            remote(k, h).wait_send()
    for k in range(1, groups):
        s = (me + k) % groups
        sp, sb = s // nb, s % nb
        for h in range(2):
            pltpu.make_async_remote_copy(
                src_ref=piece(me, h),
                dst_ref=out_ref.at[sb, h, sp],
                send_sem=send_sems.at[0],
                recv_sem=recv_sems.at[(sb * 2 + h) * npair + sp],
                device_id=(sp, sb, v),
                device_id_type=MESH,
            ).wait_recv()
    for h in range(2):
        local(h).wait()


def kblock_scatter(feats, npair, nb):
    groups = npair * nb
    rows = feats.shape[0] // 2
    depth = feats.shape[1] // groups
    size = feats.size * feats.dtype.itemsize
    return pl.pallas_call(
        functools.partial(scatter_kernel, npair, nb),
        out_shape=jax.ShapeDtypeStruct((nb, 2, npair, rows, depth), feats.dtype),
        in_specs=[pl.BlockSpec(memory_space=pltpu.VMEM)],
        out_specs=pl.BlockSpec(memory_space=pltpu.VMEM),
        scratch_shapes=[pltpu.SemaphoreType.DMA((2 * groups,)), pltpu.SemaphoreType.DMA((2 * groups,))],
        compiler_params=pltpu.CompilerParams(collective_id=0, has_side_effects=True),
        cost_estimate=pl.CostEstimate(flops=0, transcendentals=0, bytes_accessed=2 * size),
    )(feats)


def on_device(npair, nb, nv, hidden, norm_gain, head_weight):
    groups = npair * nb
    span = nv // groups
    local_rows, width = hidden.shape[1], hidden.shape[2]
    total_d = width * nv
    pad = jnp.zeros((15, width), hidden.dtype)
    block = jnp.concatenate([hidden[0], norm_gain[None, :], pad], axis=0)
    got = vocab_gather(block, nv, 1)
    wide = got[:, :local_rows, :].transpose(1, 0, 2).reshape(local_rows, total_d).astype(jnp.float32)
    gain = got[:, local_rows, :].reshape(total_d)
    meansq = jnp.sum(wide * wide, axis=1) / total_d
    scaled = wide * lax.rsqrt(meansq + EPS)[:, None] * gain.astype(jnp.float32)[None, :]
    features = scaled.astype(jnp.bfloat16)
    ordered = kblock_scatter(features, npair, nb).reshape(groups * local_rows, total_d // groups)
    half = local_rows // 2
    out_rows = half
    lanes = 128
    me = lax.axis_index("pair")
    half_rows = ordered.shape[0] // 2
    mine = lax.dynamic_slice_in_dim(ordered, me * half_rows, half_rows, axis=0)
    theirs = lax.dynamic_slice_in_dim(ordered, (1 - me) * half_rows, half_rows, axis=0)
    cols = head_weight.shape[1]
    edges = [0, cols // 8, cols]
    pieces = []
    weight = head_weight
    for j in range(len(edges) - 1):
        w = weight[:, edges[j]:edges[j + 1]]
        sent = jnp.dot(theirs, w, preferred_element_type=jnp.float32)
        kept = jnp.dot(mine, w, preferred_element_type=jnp.float32)
        got_half = lax.ppermute(sent, "pair", [(0, 1), (1, 0)])
        summed = kept + got_half
        summed, weight, theirs, mine = lax.optimization_barrier((summed, weight, theirs, mine))
        pieces.append(lax.psum_scatter(summed, "batch", scatter_dimension=0, tiled=True))
    logits = jnp.concatenate(pieces, axis=1)
    cond = logits[:out_rows]
    uncond = logits[out_rows:]
    guided = GUIDE * cond + (1.0 - GUIDE) * uncond
    peak_c = jnp.max(cond, axis=1)
    peak_g = jnp.max(guided, axis=1)
    local_c = jnp.sum(jnp.exp(cond - peak_c[:, None]), axis=1)
    local_g = jnp.sum(jnp.exp(guided - peak_g[:, None]), axis=1)
    stats = jnp.zeros((8, lanes), jnp.float32).at[:4, :out_rows].set(
        jnp.stack([peak_c, local_c, peak_g, local_g]))
    every = vocab_gather(stats, nv, 2)[:, :4, :out_rows]
    top_c = jnp.max(every[:, 0], axis=0)
    top_g = jnp.max(every[:, 2], axis=0)
    total_c = jnp.sum(every[:, 1] * jnp.exp(every[:, 0] - top_c[None, :]), axis=0)
    total_g = jnp.sum(every[:, 3] * jnp.exp(every[:, 2] - top_g[None, :]), axis=0)
    cond_out = cond - (top_c + jnp.log(total_c))[:, None]
    guided_out = guided - (top_g + jnp.log(total_g))[:, None]
    return (guided_out, cond_out)


def solution(mesh):
    npair, nb, nv = mesh.shape["pair"], mesh.shape["batch"], mesh.shape["vocab"]
    in_specs = (P("pair", "batch", "vocab"), P("vocab"), P(("pair", "batch"), "vocab"))
    out_specs = (P(("pair", "batch"), "vocab"), P(("pair", "batch"), "vocab"))
    return jax.shard_map(
        functools.partial(on_device, npair, nb, nv),
        mesh=mesh, in_specs=in_specs, out_specs=out_specs, check_vma=False,
    )
```

```python
import functools

import jax
import jax.numpy as jnp
from jax import lax
from jax.experimental import pallas as pl
from jax.experimental.pallas import tpu as pltpu
from jax.sharding import PartitionSpec as P

MESH = pl.DeviceIdType.MESH

EPS = 1e-05
GUIDE = 1.5


def dispatch_kernel(npair, nb, nv, span, src_ref, out_ref, send_sems, recv_sems):
    beta = lax.axis_index("pair")
    b = lax.axis_index("batch")
    v = lax.axis_index("vocab")
    groups = npair * nb
    mine = beta * nb + b
    q = v // span
    tp = q // nb
    tb = q % nb
    slot = mine * span + v % span
    d = q - mine
    own = 1 - (d * d + groups * groups - 1) // (groups * groups)

    def sources(s):
        bs = s // (nb * span)
        bbs = (s // span) % nb
        sv = mine * span + s % span
        return bs, bbs, sv

    barrier = pltpu.get_barrier_semaphore()
    for w in range(nv):
        @pl.when(jnp.logical_not((tp == beta) & (tb == b) & (v == w)))
        def _():
            pl.semaphore_signal(barrier, inc=1, device_id=(tp, tb, w), device_id_type=MESH)
    for s in range(nv):
        bs, bbs, sv = sources(s)

        @pl.when(jnp.logical_not((bs == beta) & (bbs == b) & (sv == v)))
        def _():
            pl.semaphore_signal(barrier, inc=1, device_id=(bs, bbs, sv), device_id_type=MESH)
    pl.semaphore_wait(barrier, 2 * (nv - own))

    def remote(k):
        return pltpu.make_async_remote_copy(
            src_ref=src_ref,
            dst_ref=out_ref.at[slot],
            send_sem=send_sems.at[k],
            recv_sem=recv_sems.at[slot],
            device_id=(tp, tb, (k + slot) % nv),
            device_id_type=MESH,
        )

    for k in range(nv):
        here = (tp == beta) & (tb == b) & (v == (k + slot) % nv)

        @pl.when(jnp.logical_not(here))
        def _():
            remote(k).start()

        @pl.when(here)
        def _():
            pltpu.make_async_copy(src_ref, out_ref.at[slot], recv_sems.at[slot]).start()

    for k in range(nv):
        here = (tp == beta) & (tb == b) & (v == (k + slot) % nv)

        @pl.when(jnp.logical_not(here))
        def _():
            remote(k).wait_send()

    for s in range(nv):
        bs, bbs, sv = sources(s)
        here = (bs == beta) & (bbs == b) & (sv == v)

        @pl.when(jnp.logical_not(here))
        def _():
            pltpu.make_async_remote_copy(
                src_ref=src_ref,
                dst_ref=out_ref.at[s],
                send_sem=send_sems.at[0],
                recv_sem=recv_sems.at[s],
                device_id=(bs, bbs, sv),
                device_id_type=MESH,
            ).wait_recv()

        @pl.when(here)
        def _():
            pltpu.make_async_copy(src_ref, out_ref.at[s], recv_sems.at[s]).wait()


def dispatch(block, npair, nb, nv):
    span = nv // (npair * nb)
    size = block.size * block.dtype.itemsize
    return pl.pallas_call(
        functools.partial(dispatch_kernel, npair, nb, nv, span),
        out_shape=jax.ShapeDtypeStruct((nv,) + block.shape, block.dtype),
        in_specs=[pl.BlockSpec(memory_space=pltpu.VMEM)],
        out_specs=pl.BlockSpec(memory_space=pltpu.VMEM),
        scratch_shapes=[pltpu.SemaphoreType.DMA((nv,)), pltpu.SemaphoreType.DMA((nv,))],
        compiler_params=pltpu.CompilerParams(collective_id=0, has_side_effects=True),
        cost_estimate=pl.CostEstimate(flops=0, transcendentals=0, bytes_accessed=2 * nv * size),
    )(block)


def gather_kernel(nv, src_ref, out_ref, send_sems, recv_sems):
    beta = lax.axis_index("pair")
    b = lax.axis_index("batch")
    v = lax.axis_index("vocab")
    barrier = pltpu.get_barrier_semaphore()
    for k in range(1, nv):
        pl.semaphore_signal(barrier, inc=1, device_id=(beta, b, (v + k) % nv), device_id_type=MESH)
    pl.semaphore_wait(barrier, nv - 1)

    def remote(w, s):
        return pltpu.make_async_remote_copy(
            src_ref=src_ref,
            dst_ref=out_ref.at[s],
            send_sem=send_sems.at[w],
            recv_sem=recv_sems.at[s],
            device_id=(beta, b, w),
            device_id_type=MESH,
        )

    for k in range(1, nv):
        remote((v + k) % nv, v).start()

    pltpu.make_async_copy(src_ref, out_ref.at[v], recv_sems.at[v]).start()
    for k in range(1, nv):
        remote((v + k) % nv, v).wait_send()
    for k in range(1, nv):
        s = (v + k) % nv
        remote(s, s).wait_recv()
    pltpu.make_async_copy(src_ref, out_ref.at[v], recv_sems.at[v]).wait()


def vocab_gather(block, nv, cid):
    size = block.size * block.dtype.itemsize
    return pl.pallas_call(
        functools.partial(gather_kernel, nv),
        out_shape=jax.ShapeDtypeStruct((nv,) + block.shape, block.dtype),
        in_specs=[pl.BlockSpec(memory_space=pltpu.VMEM)],
        out_specs=pl.BlockSpec(memory_space=pltpu.VMEM),
        scratch_shapes=[pltpu.SemaphoreType.DMA((nv,)), pltpu.SemaphoreType.DMA((nv,))],
        compiler_params=pltpu.CompilerParams(collective_id=cid, has_side_effects=True),
        cost_estimate=pl.CostEstimate(flops=0, transcendentals=0, bytes_accessed=2 * nv * size),
    )(block)


def gather_pair_kernel(nv, h_ref, g_ref, ho_ref, go_ref, hs, hr, gs, gr):
    beta = lax.axis_index("pair")
    b = lax.axis_index("batch")
    v = lax.axis_index("vocab")
    barrier = pltpu.get_barrier_semaphore()
    for k in range(1, nv):
        pl.semaphore_signal(barrier, inc=1, device_id=(beta, b, (v + k) % nv), device_id_type=MESH)
    pl.semaphore_wait(barrier, nv - 1)

    def remote(src, dst, send, recv, w, s):
        return pltpu.make_async_remote_copy(
            src_ref=src,
            dst_ref=dst.at[s],
            send_sem=send.at[w],
            recv_sem=recv.at[s],
            device_id=(beta, b, w),
            device_id_type=MESH,
        )

    pairs = ((h_ref, ho_ref, hs, hr), (g_ref, go_ref, gs, gr))
    for k in range(1, nv):
        for src, dst, send, recv in pairs:
            remote(src, dst, send, recv, (v + k) % nv, v).start()
    for src, dst, send, recv in pairs:
        pltpu.make_async_copy(src, dst.at[v], recv.at[v]).start()
    for k in range(1, nv):
        for src, dst, send, recv in pairs:
            remote(src, dst, send, recv, (v + k) % nv, v).wait_send()
    for k in range(1, nv):
        s = (v + k) % nv
        for src, dst, send, recv in pairs:
            remote(src, dst, send, recv, s, s).wait_recv()
    for src, dst, send, recv in pairs:
        pltpu.make_async_copy(src, dst.at[v], recv.at[v]).wait()


def vocab_gather_pair(rows, gain, nv, cid):
    size = rows.size * rows.dtype.itemsize + gain.size * gain.dtype.itemsize
    sems = [pltpu.SemaphoreType.DMA((nv,))] * 4
    return pl.pallas_call(
        functools.partial(gather_pair_kernel, nv),
        out_shape=(jax.ShapeDtypeStruct((nv,) + rows.shape, rows.dtype),
                   jax.ShapeDtypeStruct((nv,) + gain.shape, gain.dtype)),
        in_specs=[pl.BlockSpec(memory_space=pltpu.VMEM)] * 2,
        out_specs=(pl.BlockSpec(memory_space=pltpu.VMEM), pl.BlockSpec(memory_space=pltpu.VMEM)),
        scratch_shapes=sems,
        compiler_params=pltpu.CompilerParams(collective_id=cid, has_side_effects=True),
        cost_estimate=pl.CostEstimate(flops=0, transcendentals=0, bytes_accessed=2 * nv * size),
    )(rows, gain)


def scatter_kernel(npair, nb, src_ref, out_ref, send_sems, recv_sems):
    beta = lax.axis_index("pair")
    b = lax.axis_index("batch")
    v = lax.axis_index("vocab")
    groups = npair * nb
    me = beta * nb + b
    rows = out_ref.shape[3]
    depth = out_ref.shape[4]
    barrier = pltpu.get_barrier_semaphore()
    for k in range(1, groups):
        t = (me + k) % groups
        pl.semaphore_signal(barrier, inc=1, device_id=(t // nb, t % nb, v), device_id_type=MESH)
    pl.semaphore_wait(barrier, groups - 1)

    def piece(t, h):
        return src_ref.at[pl.ds(h * rows, rows), pl.ds(pl.multiple_of(t * depth, depth), depth)]

    def remote(k, h):
        t = (me + k) % groups
        return pltpu.make_async_remote_copy(
            src_ref=piece(t, h),
            dst_ref=out_ref.at[b, h, beta],
            send_sem=send_sems.at[k * 2 + h],
            recv_sem=recv_sems.at[(b * 2 + h) * npair + beta],
            device_id=(t // nb, t % nb, v),
            device_id_type=MESH,
        )

    def local(h):
        return pltpu.make_async_copy(
            piece(me, h), out_ref.at[b, h, beta], recv_sems.at[(b * 2 + h) * npair + beta])

    for k in range(1, groups):
        for h in range(2):
            remote(k, h).start()
    for h in range(2):
        local(h).start()
    for k in range(1, groups):
        for h in range(2):
            remote(k, h).wait_send()
    for k in range(1, groups):
        s = (me + k) % groups
        sp, sb = s // nb, s % nb
        for h in range(2):
            pltpu.make_async_remote_copy(
                src_ref=piece(me, h),
                dst_ref=out_ref.at[sb, h, sp],
                send_sem=send_sems.at[0],
                recv_sem=recv_sems.at[(sb * 2 + h) * npair + sp],
                device_id=(sp, sb, v),
                device_id_type=MESH,
            ).wait_recv()
    for h in range(2):
        local(h).wait()


def kblock_scatter(feats, npair, nb):
    groups = npair * nb
    rows = feats.shape[0] // 2
    depth = feats.shape[1] // groups
    size = feats.size * feats.dtype.itemsize
    return pl.pallas_call(
        functools.partial(scatter_kernel, npair, nb),
        out_shape=jax.ShapeDtypeStruct((nb, 2, npair, rows, depth), feats.dtype),
        in_specs=[pl.BlockSpec(memory_space=pltpu.VMEM)],
        out_specs=pl.BlockSpec(memory_space=pltpu.VMEM),
        scratch_shapes=[pltpu.SemaphoreType.DMA((2 * groups,)), pltpu.SemaphoreType.DMA((2 * groups,))],
        compiler_params=pltpu.CompilerParams(collective_id=0, has_side_effects=True),
        cost_estimate=pl.CostEstimate(flops=0, transcendentals=0, bytes_accessed=2 * size),
    )(feats)


def on_device(npair, nb, nv, hidden, norm_gain, head_weight):
    groups = npair * nb
    span = nv // groups
    local_rows, width = hidden.shape[1], hidden.shape[2]
    total_d = width * nv
    lanes = 128
    gain_rows = width // lanes
    gain_block = jnp.zeros((16, lanes), norm_gain.dtype).at[:gain_rows].set(norm_gain.reshape(gain_rows, lanes))
    got, got_gain = vocab_gather_pair(hidden[0], gain_block, nv, 1)
    wide = got.transpose(1, 0, 2).reshape(local_rows, total_d).astype(jnp.float32)
    gain = got_gain[:, :gain_rows, :].reshape(total_d)
    meansq = jnp.sum(wide * wide, axis=1) / total_d
    scaled = wide * lax.rsqrt(meansq + EPS)[:, None] * gain.astype(jnp.float32)[None, :]
    features = scaled.astype(jnp.bfloat16)
    ordered = kblock_scatter(features, npair, nb).reshape(groups * local_rows, total_d // groups)
    half = local_rows // 2
    out_rows = half
    lanes = 128
    me = lax.axis_index("pair")
    half_rows = ordered.shape[0] // 2
    mine = lax.dynamic_slice_in_dim(ordered, me * half_rows, half_rows, axis=0)
    theirs = lax.dynamic_slice_in_dim(ordered, (1 - me) * half_rows, half_rows, axis=0)
    cols = head_weight.shape[1]
    edges = [0, cols // 8, cols]
    pieces = []
    weight = head_weight
    for j in range(len(edges) - 1):
        w = weight[:, edges[j]:edges[j + 1]]
        sent = jnp.dot(theirs, w, preferred_element_type=jnp.float32)
        kept = jnp.dot(mine, w, preferred_element_type=jnp.float32)
        got_half = lax.ppermute(sent, "pair", [(0, 1), (1, 0)])
        summed = kept + got_half
        summed, weight, theirs, mine = lax.optimization_barrier((summed, weight, theirs, mine))
        pieces.append(lax.psum_scatter(summed, "batch", scatter_dimension=0, tiled=True))
    logits = jnp.concatenate(pieces, axis=1)
    cond = logits[:out_rows]
    uncond = logits[out_rows:]
    guided = GUIDE * cond + (1.0 - GUIDE) * uncond
    peak_c = jnp.max(cond, axis=1)
    peak_g = jnp.max(guided, axis=1)
    local_c = jnp.sum(jnp.exp(cond - peak_c[:, None]), axis=1)
    local_g = jnp.sum(jnp.exp(guided - peak_g[:, None]), axis=1)
    stats = jnp.zeros((8, lanes), jnp.float32).at[:4, :out_rows].set(
        jnp.stack([peak_c, local_c, peak_g, local_g]))
    every = vocab_gather(stats, nv, 2)[:, :4, :out_rows]
    top_c = jnp.max(every[:, 0], axis=0)
    top_g = jnp.max(every[:, 2], axis=0)
    total_c = jnp.sum(every[:, 1] * jnp.exp(every[:, 0] - top_c[None, :]), axis=0)
    total_g = jnp.sum(every[:, 3] * jnp.exp(every[:, 2] - top_g[None, :]), axis=0)
    cond_out = cond - (top_c + jnp.log(total_c))[:, None]
    guided_out = guided - (top_g + jnp.log(total_g))[:, None]
    return (guided_out, cond_out)


def solution(mesh):
    npair, nb, nv = mesh.shape["pair"], mesh.shape["batch"], mesh.shape["vocab"]
    in_specs = (P("pair", "batch", "vocab"), P("vocab"), P(("pair", "batch"), "vocab"))
    out_specs = (P(("pair", "batch"), "vocab"), P(("pair", "batch"), "vocab"))
    return jax.shard_map(
        functools.partial(on_device, npair, nb, nv),
        mesh=mesh, in_specs=in_specs, out_specs=out_specs, check_vma=False,
    )
```

```python
import functools

import jax
import jax.numpy as jnp
from jax import lax
from jax.experimental import pallas as pl
from jax.experimental.pallas import tpu as pltpu
from jax.sharding import PartitionSpec as P

MESH = pl.DeviceIdType.MESH

EPS = 1e-05
GUIDE = 1.5


def dispatch_kernel(npair, nb, nv, span, src_ref, out_ref, send_sems, recv_sems):
    beta = lax.axis_index("pair")
    b = lax.axis_index("batch")
    v = lax.axis_index("vocab")
    groups = npair * nb
    mine = beta * nb + b
    q = v // span
    tp = q // nb
    tb = q % nb
    slot = mine * span + v % span
    d = q - mine
    own = 1 - (d * d + groups * groups - 1) // (groups * groups)

    def sources(s):
        bs = s // (nb * span)
        bbs = (s // span) % nb
        sv = mine * span + s % span
        return bs, bbs, sv

    barrier = pltpu.get_barrier_semaphore()
    for w in range(nv):
        @pl.when(jnp.logical_not((tp == beta) & (tb == b) & (v == w)))
        def _():
            pl.semaphore_signal(barrier, inc=1, device_id=(tp, tb, w), device_id_type=MESH)
    for s in range(nv):
        bs, bbs, sv = sources(s)

        @pl.when(jnp.logical_not((bs == beta) & (bbs == b) & (sv == v)))
        def _():
            pl.semaphore_signal(barrier, inc=1, device_id=(bs, bbs, sv), device_id_type=MESH)
    pl.semaphore_wait(barrier, 2 * (nv - own))

    def remote(k):
        return pltpu.make_async_remote_copy(
            src_ref=src_ref,
            dst_ref=out_ref.at[slot],
            send_sem=send_sems.at[k],
            recv_sem=recv_sems.at[slot],
            device_id=(tp, tb, (k + slot) % nv),
            device_id_type=MESH,
        )

    for k in range(nv):
        here = (tp == beta) & (tb == b) & (v == (k + slot) % nv)

        @pl.when(jnp.logical_not(here))
        def _():
            remote(k).start()

        @pl.when(here)
        def _():
            pltpu.make_async_copy(src_ref, out_ref.at[slot], recv_sems.at[slot]).start()

    for k in range(nv):
        here = (tp == beta) & (tb == b) & (v == (k + slot) % nv)

        @pl.when(jnp.logical_not(here))
        def _():
            remote(k).wait_send()

    for s in range(nv):
        bs, bbs, sv = sources(s)
        here = (bs == beta) & (bbs == b) & (sv == v)

        @pl.when(jnp.logical_not(here))
        def _():
            pltpu.make_async_remote_copy(
                src_ref=src_ref,
                dst_ref=out_ref.at[s],
                send_sem=send_sems.at[0],
                recv_sem=recv_sems.at[s],
                device_id=(bs, bbs, sv),
                device_id_type=MESH,
            ).wait_recv()

        @pl.when(here)
        def _():
            pltpu.make_async_copy(src_ref, out_ref.at[s], recv_sems.at[s]).wait()


def dispatch(block, npair, nb, nv):
    span = nv // (npair * nb)
    size = block.size * block.dtype.itemsize
    return pl.pallas_call(
        functools.partial(dispatch_kernel, npair, nb, nv, span),
        out_shape=jax.ShapeDtypeStruct((nv,) + block.shape, block.dtype),
        in_specs=[pl.BlockSpec(memory_space=pltpu.VMEM)],
        out_specs=pl.BlockSpec(memory_space=pltpu.VMEM),
        scratch_shapes=[pltpu.SemaphoreType.DMA((nv,)), pltpu.SemaphoreType.DMA((nv,))],
        compiler_params=pltpu.CompilerParams(collective_id=0, has_side_effects=True),
        cost_estimate=pl.CostEstimate(flops=0, transcendentals=0, bytes_accessed=2 * nv * size),
    )(block)


def gather_kernel(nv, src_ref, out_ref, send_sems, recv_sems):
    beta = lax.axis_index("pair")
    b = lax.axis_index("batch")
    v = lax.axis_index("vocab")
    barrier = pltpu.get_barrier_semaphore()
    for k in range(1, nv):
        pl.semaphore_signal(barrier, inc=1, device_id=(beta, b, (v + k) % nv), device_id_type=MESH)
    pl.semaphore_wait(barrier, nv - 1)

    def remote(w, s):
        return pltpu.make_async_remote_copy(
            src_ref=src_ref,
            dst_ref=out_ref.at[s],
            send_sem=send_sems.at[w],
            recv_sem=recv_sems.at[s],
            device_id=(beta, b, w),
            device_id_type=MESH,
        )

    for k in range(1, nv):
        remote((v + k) % nv, v).start()

    pltpu.make_async_copy(src_ref, out_ref.at[v], recv_sems.at[v]).start()
    for k in range(1, nv):
        remote((v + k) % nv, v).wait_send()
    for k in range(1, nv):
        s = (v + k) % nv
        remote(s, s).wait_recv()
    pltpu.make_async_copy(src_ref, out_ref.at[v], recv_sems.at[v]).wait()


def vocab_gather(block, nv, cid):
    size = block.size * block.dtype.itemsize
    return pl.pallas_call(
        functools.partial(gather_kernel, nv),
        out_shape=jax.ShapeDtypeStruct((nv,) + block.shape, block.dtype),
        in_specs=[pl.BlockSpec(memory_space=pltpu.VMEM)],
        out_specs=pl.BlockSpec(memory_space=pltpu.VMEM),
        scratch_shapes=[pltpu.SemaphoreType.DMA((nv,)), pltpu.SemaphoreType.DMA((nv,))],
        compiler_params=pltpu.CompilerParams(collective_id=cid, has_side_effects=True),
        cost_estimate=pl.CostEstimate(flops=0, transcendentals=0, bytes_accessed=2 * nv * size),
    )(block)


def gather_pair_kernel(nv, h_ref, g_ref, ho_ref, go_ref, hs, hr, gs, gr):
    beta = lax.axis_index("pair")
    b = lax.axis_index("batch")
    v = lax.axis_index("vocab")
    barrier = pltpu.get_barrier_semaphore()
    for k in range(1, nv):
        pl.semaphore_signal(barrier, inc=1, device_id=(beta, b, (v + k) % nv), device_id_type=MESH)
    pl.semaphore_wait(barrier, nv - 1)

    def remote(src, dst, send, recv, w, s):
        return pltpu.make_async_remote_copy(
            src_ref=src,
            dst_ref=dst.at[s],
            send_sem=send.at[w],
            recv_sem=recv.at[s],
            device_id=(beta, b, w),
            device_id_type=MESH,
        )

    pairs = ((h_ref, ho_ref, hs, hr), (g_ref, go_ref, gs, gr))
    for k in range(1, nv):
        for src, dst, send, recv in pairs:
            remote(src, dst, send, recv, (v + k) % nv, v).start()
    for src, dst, send, recv in pairs:
        pltpu.make_async_copy(src, dst.at[v], recv.at[v]).start()
    for k in range(1, nv):
        for src, dst, send, recv in pairs:
            remote(src, dst, send, recv, (v + k) % nv, v).wait_send()
    for k in range(1, nv):
        s = (v + k) % nv
        for src, dst, send, recv in pairs:
            remote(src, dst, send, recv, s, s).wait_recv()
    for src, dst, send, recv in pairs:
        pltpu.make_async_copy(src, dst.at[v], recv.at[v]).wait()


def vocab_gather_pair(rows, gain, nv, cid):
    size = rows.size * rows.dtype.itemsize + gain.size * gain.dtype.itemsize
    sems = [pltpu.SemaphoreType.DMA((nv,))] * 4
    return pl.pallas_call(
        functools.partial(gather_pair_kernel, nv),
        out_shape=(jax.ShapeDtypeStruct((nv,) + rows.shape, rows.dtype),
                   jax.ShapeDtypeStruct((nv,) + gain.shape, gain.dtype)),
        in_specs=[pl.BlockSpec(memory_space=pltpu.VMEM)] * 2,
        out_specs=(pl.BlockSpec(memory_space=pltpu.VMEM), pl.BlockSpec(memory_space=pltpu.VMEM)),
        scratch_shapes=sems,
        compiler_params=pltpu.CompilerParams(collective_id=cid, has_side_effects=True),
        cost_estimate=pl.CostEstimate(flops=0, transcendentals=0, bytes_accessed=2 * nv * size),
    )(rows, gain)


def scatter_kernel(npair, nb, src_ref, out_ref, send_sems, recv_sems):
    beta = lax.axis_index("pair")
    b = lax.axis_index("batch")
    v = lax.axis_index("vocab")
    groups = npair * nb
    me = beta * nb + b
    rows = out_ref.shape[3]
    depth = out_ref.shape[4]
    barrier = pltpu.get_barrier_semaphore()
    for k in range(1, groups):
        t = (me + k) % groups
        pl.semaphore_signal(barrier, inc=1, device_id=(t // nb, t % nb, v), device_id_type=MESH)
    pl.semaphore_wait(barrier, groups - 1)

    def piece(t, h):
        return src_ref.at[pl.ds(h * rows, rows), pl.ds(pl.multiple_of(t * depth, depth), depth)]

    def remote(k, h):
        t = (me + k) % groups
        return pltpu.make_async_remote_copy(
            src_ref=piece(t, h),
            dst_ref=out_ref.at[b, h, beta],
            send_sem=send_sems.at[k * 2 + h],
            recv_sem=recv_sems.at[(b * 2 + h) * npair + beta],
            device_id=(t // nb, t % nb, v),
            device_id_type=MESH,
        )

    def local(h):
        return pltpu.make_async_copy(
            piece(me, h), out_ref.at[b, h, beta], recv_sems.at[(b * 2 + h) * npair + beta])

    for k in range(1, groups):
        for h in range(2):
            remote(k, h).start()
    for h in range(2):
        local(h).start()
    for k in range(1, groups):
        for h in range(2):
            remote(k, h).wait_send()
    for k in range(1, groups):
        s = (me + k) % groups
        sp, sb = s // nb, s % nb
        for h in range(2):
            pltpu.make_async_remote_copy(
                src_ref=piece(me, h),
                dst_ref=out_ref.at[sb, h, sp],
                send_sem=send_sems.at[0],
                recv_sem=recv_sems.at[(sb * 2 + h) * npair + sp],
                device_id=(sp, sb, v),
                device_id_type=MESH,
            ).wait_recv()
    for h in range(2):
        local(h).wait()


def kblock_scatter(feats, npair, nb):
    groups = npair * nb
    rows = feats.shape[0] // 2
    depth = feats.shape[1] // groups
    size = feats.size * feats.dtype.itemsize
    return pl.pallas_call(
        functools.partial(scatter_kernel, npair, nb),
        out_shape=jax.ShapeDtypeStruct((nb, 2, npair, rows, depth), feats.dtype),
        in_specs=[pl.BlockSpec(memory_space=pltpu.VMEM)],
        out_specs=pl.BlockSpec(memory_space=pltpu.VMEM),
        scratch_shapes=[pltpu.SemaphoreType.DMA((2 * groups,)), pltpu.SemaphoreType.DMA((2 * groups,))],
        compiler_params=pltpu.CompilerParams(collective_id=0, has_side_effects=True),
        cost_estimate=pl.CostEstimate(flops=0, transcendentals=0, bytes_accessed=2 * size),
    )(feats)


def on_device(npair, nb, nv, hidden, norm_gain, head_weight):
    groups = npair * nb
    span = nv // groups
    local_rows, width = hidden.shape[1], hidden.shape[2]
    total_d = width * nv
    lanes = 128
    gain_rows = width // lanes
    gain_block = jnp.zeros((16, lanes), norm_gain.dtype).at[:gain_rows].set(norm_gain.reshape(gain_rows, lanes))
    got, got_gain = vocab_gather_pair(hidden[0], gain_block, nv, 1)
    wide = got.transpose(1, 0, 2).reshape(local_rows, total_d).astype(jnp.float32)
    gain = got_gain[:, :gain_rows, :].reshape(total_d)
    meansq = jnp.sum(wide * wide, axis=1) / total_d
    scaled = wide * lax.rsqrt(meansq + EPS)[:, None] * gain.astype(jnp.float32)[None, :]
    features = scaled.astype(jnp.bfloat16)
    ordered = kblock_scatter(features, npair, nb).reshape(groups * local_rows, total_d // groups)
    half = local_rows // 2
    out_rows = half
    lanes = 128
    me = lax.axis_index("pair")
    half_rows = ordered.shape[0] // 2
    mine = lax.dynamic_slice_in_dim(ordered, me * half_rows, half_rows, axis=0)
    theirs = lax.dynamic_slice_in_dim(ordered, (1 - me) * half_rows, half_rows, axis=0)
    cols = head_weight.shape[1]
    edges = [0, cols // 16, cols]
    pieces = []
    weight = head_weight
    for j in range(len(edges) - 1):
        w = weight[:, edges[j]:edges[j + 1]]
        sent = jnp.dot(theirs, w, preferred_element_type=jnp.float32)
        kept = jnp.dot(mine, w, preferred_element_type=jnp.float32)
        got_half = lax.ppermute(sent, "pair", [(0, 1), (1, 0)])
        summed = kept + got_half
        summed, weight, theirs, mine = lax.optimization_barrier((summed, weight, theirs, mine))
        pieces.append(lax.psum_scatter(summed, "batch", scatter_dimension=0, tiled=True))
    logits = jnp.concatenate(pieces, axis=1)
    cond = logits[:out_rows]
    uncond = logits[out_rows:]
    guided = GUIDE * cond + (1.0 - GUIDE) * uncond
    peak_c = jnp.max(cond, axis=1)
    peak_g = jnp.max(guided, axis=1)
    local_c = jnp.sum(jnp.exp(cond - peak_c[:, None]), axis=1)
    local_g = jnp.sum(jnp.exp(guided - peak_g[:, None]), axis=1)
    stats = jnp.zeros((8, lanes), jnp.float32).at[:4, :out_rows].set(
        jnp.stack([peak_c, local_c, peak_g, local_g]))
    every = vocab_gather(stats, nv, 2)[:, :4, :out_rows]
    top_c = jnp.max(every[:, 0], axis=0)
    top_g = jnp.max(every[:, 2], axis=0)
    total_c = jnp.sum(every[:, 1] * jnp.exp(every[:, 0] - top_c[None, :]), axis=0)
    total_g = jnp.sum(every[:, 3] * jnp.exp(every[:, 2] - top_g[None, :]), axis=0)
    cond_out = cond - (top_c + jnp.log(total_c))[:, None]
    guided_out = guided - (top_g + jnp.log(total_g))[:, None]
    return (guided_out, cond_out)


def solution(mesh):
    npair, nb, nv = mesh.shape["pair"], mesh.shape["batch"], mesh.shape["vocab"]
    in_specs = (P("pair", "batch", "vocab"), P("vocab"), P(("pair", "batch"), "vocab"))
    out_specs = (P(("pair", "batch"), "vocab"), P(("pair", "batch"), "vocab"))
    return jax.shard_map(
        functools.partial(on_device, npair, nb, nv),
        mesh=mesh, in_specs=in_specs, out_specs=out_specs, check_vma=False,
    )
```

```python
import functools

import jax
import jax.numpy as jnp
from jax import lax
from jax.experimental import pallas as pl
from jax.experimental.pallas import tpu as pltpu
from jax.sharding import PartitionSpec as P

MESH = pl.DeviceIdType.MESH

EPS = 1e-05
GUIDE = 1.5


def dispatch_kernel(npair, nb, nv, span, src_ref, out_ref, send_sems, recv_sems):
    beta = lax.axis_index("pair")
    b = lax.axis_index("batch")
    v = lax.axis_index("vocab")
    groups = npair * nb
    mine = beta * nb + b
    q = v // span
    tp = q // nb
    tb = q % nb
    slot = mine * span + v % span
    d = q - mine
    own = 1 - (d * d + groups * groups - 1) // (groups * groups)

    def sources(s):
        bs = s // (nb * span)
        bbs = (s // span) % nb
        sv = mine * span + s % span
        return bs, bbs, sv

    barrier = pltpu.get_barrier_semaphore()
    for w in range(nv):
        @pl.when(jnp.logical_not((tp == beta) & (tb == b) & (v == w)))
        def _():
            pl.semaphore_signal(barrier, inc=1, device_id=(tp, tb, w), device_id_type=MESH)
    for s in range(nv):
        bs, bbs, sv = sources(s)

        @pl.when(jnp.logical_not((bs == beta) & (bbs == b) & (sv == v)))
        def _():
            pl.semaphore_signal(barrier, inc=1, device_id=(bs, bbs, sv), device_id_type=MESH)
    pl.semaphore_wait(barrier, 2 * (nv - own))

    def remote(k):
        return pltpu.make_async_remote_copy(
            src_ref=src_ref,
            dst_ref=out_ref.at[slot],
            send_sem=send_sems.at[k],
            recv_sem=recv_sems.at[slot],
            device_id=(tp, tb, (k + slot) % nv),
            device_id_type=MESH,
        )

    for k in range(nv):
        here = (tp == beta) & (tb == b) & (v == (k + slot) % nv)

        @pl.when(jnp.logical_not(here))
        def _():
            remote(k).start()

        @pl.when(here)
        def _():
            pltpu.make_async_copy(src_ref, out_ref.at[slot], recv_sems.at[slot]).start()

    for k in range(nv):
        here = (tp == beta) & (tb == b) & (v == (k + slot) % nv)

        @pl.when(jnp.logical_not(here))
        def _():
            remote(k).wait_send()

    for s in range(nv):
        bs, bbs, sv = sources(s)
        here = (bs == beta) & (bbs == b) & (sv == v)

        @pl.when(jnp.logical_not(here))
        def _():
            pltpu.make_async_remote_copy(
                src_ref=src_ref,
                dst_ref=out_ref.at[s],
                send_sem=send_sems.at[0],
                recv_sem=recv_sems.at[s],
                device_id=(bs, bbs, sv),
                device_id_type=MESH,
            ).wait_recv()

        @pl.when(here)
        def _():
            pltpu.make_async_copy(src_ref, out_ref.at[s], recv_sems.at[s]).wait()


def dispatch(block, npair, nb, nv):
    span = nv // (npair * nb)
    size = block.size * block.dtype.itemsize
    return pl.pallas_call(
        functools.partial(dispatch_kernel, npair, nb, nv, span),
        out_shape=jax.ShapeDtypeStruct((nv,) + block.shape, block.dtype),
        in_specs=[pl.BlockSpec(memory_space=pltpu.VMEM)],
        out_specs=pl.BlockSpec(memory_space=pltpu.VMEM),
        scratch_shapes=[pltpu.SemaphoreType.DMA((nv,)), pltpu.SemaphoreType.DMA((nv,))],
        compiler_params=pltpu.CompilerParams(collective_id=0, has_side_effects=True),
        cost_estimate=pl.CostEstimate(flops=0, transcendentals=0, bytes_accessed=2 * nv * size),
    )(block)


def gather_kernel(nv, src_ref, out_ref, send_sems, recv_sems):
    beta = lax.axis_index("pair")
    b = lax.axis_index("batch")
    v = lax.axis_index("vocab")
    barrier = pltpu.get_barrier_semaphore()
    for k in range(1, nv):
        pl.semaphore_signal(barrier, inc=1, device_id=(beta, b, (v + k) % nv), device_id_type=MESH)
    pl.semaphore_wait(barrier, nv - 1)

    def remote(w, s):
        return pltpu.make_async_remote_copy(
            src_ref=src_ref,
            dst_ref=out_ref.at[s],
            send_sem=send_sems.at[w],
            recv_sem=recv_sems.at[s],
            device_id=(beta, b, w),
            device_id_type=MESH,
        )

    for k in range(1, nv):
        remote((v + k) % nv, v).start()

    pltpu.make_async_copy(src_ref, out_ref.at[v], recv_sems.at[v]).start()
    for k in range(1, nv):
        remote((v + k) % nv, v).wait_send()
    for k in range(1, nv):
        s = (v + k) % nv
        remote(s, s).wait_recv()
    pltpu.make_async_copy(src_ref, out_ref.at[v], recv_sems.at[v]).wait()


def vocab_gather(block, nv, cid):
    size = block.size * block.dtype.itemsize
    return pl.pallas_call(
        functools.partial(gather_kernel, nv),
        out_shape=jax.ShapeDtypeStruct((nv,) + block.shape, block.dtype),
        in_specs=[pl.BlockSpec(memory_space=pltpu.VMEM)],
        out_specs=pl.BlockSpec(memory_space=pltpu.VMEM),
        scratch_shapes=[pltpu.SemaphoreType.DMA((nv,)), pltpu.SemaphoreType.DMA((nv,))],
        compiler_params=pltpu.CompilerParams(collective_id=cid, has_side_effects=True),
        cost_estimate=pl.CostEstimate(flops=0, transcendentals=0, bytes_accessed=2 * nv * size),
    )(block)


def gather_pair_kernel(nv, h_ref, g_ref, ho_ref, go_ref, hs, hr, gs, gr):
    beta = lax.axis_index("pair")
    b = lax.axis_index("batch")
    v = lax.axis_index("vocab")
    barrier = pltpu.get_barrier_semaphore()
    for k in range(1, nv):
        pl.semaphore_signal(barrier, inc=1, device_id=(beta, b, (v + k) % nv), device_id_type=MESH)
    pl.semaphore_wait(barrier, nv - 1)

    def remote(src, dst, send, recv, w, s):
        return pltpu.make_async_remote_copy(
            src_ref=src,
            dst_ref=dst.at[s],
            send_sem=send.at[w],
            recv_sem=recv.at[s],
            device_id=(beta, b, w),
            device_id_type=MESH,
        )

    pairs = ((h_ref, ho_ref, hs, hr), (g_ref, go_ref, gs, gr))
    for k in range(1, nv):
        for src, dst, send, recv in pairs:
            remote(src, dst, send, recv, (v + k) % nv, v).start()
    for src, dst, send, recv in pairs:
        pltpu.make_async_copy(src, dst.at[v], recv.at[v]).start()
    for k in range(1, nv):
        for src, dst, send, recv in pairs:
            remote(src, dst, send, recv, (v + k) % nv, v).wait_send()
    for k in range(1, nv):
        s = (v + k) % nv
        for src, dst, send, recv in pairs:
            remote(src, dst, send, recv, s, s).wait_recv()
    for src, dst, send, recv in pairs:
        pltpu.make_async_copy(src, dst.at[v], recv.at[v]).wait()


def vocab_gather_pair(rows, gain, nv, cid):
    size = rows.size * rows.dtype.itemsize + gain.size * gain.dtype.itemsize
    sems = [pltpu.SemaphoreType.DMA((nv,))] * 4
    return pl.pallas_call(
        functools.partial(gather_pair_kernel, nv),
        out_shape=(jax.ShapeDtypeStruct((nv,) + rows.shape, rows.dtype),
                   jax.ShapeDtypeStruct((nv,) + gain.shape, gain.dtype)),
        in_specs=[pl.BlockSpec(memory_space=pltpu.VMEM)] * 2,
        out_specs=(pl.BlockSpec(memory_space=pltpu.VMEM), pl.BlockSpec(memory_space=pltpu.VMEM)),
        scratch_shapes=sems,
        compiler_params=pltpu.CompilerParams(collective_id=cid, has_side_effects=True),
        cost_estimate=pl.CostEstimate(flops=0, transcendentals=0, bytes_accessed=2 * nv * size),
    )(rows, gain)


def scatter_kernel(npair, nb, src_ref, out_ref, send_sems, recv_sems):
    beta = lax.axis_index("pair")
    b = lax.axis_index("batch")
    v = lax.axis_index("vocab")
    groups = npair * nb
    me = beta * nb + b
    rows = out_ref.shape[3]
    depth = out_ref.shape[4]
    barrier = pltpu.get_barrier_semaphore()
    for k in range(1, groups):
        t = (me + k) % groups
        pl.semaphore_signal(barrier, inc=1, device_id=(t // nb, t % nb, v), device_id_type=MESH)
    pl.semaphore_wait(barrier, groups - 1)

    def piece(t, h):
        return src_ref.at[pl.ds(h * rows, rows), pl.ds(pl.multiple_of(t * depth, depth), depth)]

    def remote(k, h):
        t = (me + k) % groups
        return pltpu.make_async_remote_copy(
            src_ref=piece(t, h),
            dst_ref=out_ref.at[b, h, beta],
            send_sem=send_sems.at[k * 2 + h],
            recv_sem=recv_sems.at[(b * 2 + h) * npair + beta],
            device_id=(t // nb, t % nb, v),
            device_id_type=MESH,
        )

    def local(h):
        return pltpu.make_async_copy(
            piece(me, h), out_ref.at[b, h, beta], recv_sems.at[(b * 2 + h) * npair + beta])

    for k in range(1, groups):
        for h in range(2):
            remote(k, h).start()
    for h in range(2):
        local(h).start()
    for k in range(1, groups):
        for h in range(2):
            remote(k, h).wait_send()
    for k in range(1, groups):
        s = (me + k) % groups
        sp, sb = s // nb, s % nb
        for h in range(2):
            pltpu.make_async_remote_copy(
                src_ref=piece(me, h),
                dst_ref=out_ref.at[sb, h, sp],
                send_sem=send_sems.at[0],
                recv_sem=recv_sems.at[(sb * 2 + h) * npair + sp],
                device_id=(sp, sb, v),
                device_id_type=MESH,
            ).wait_recv()
    for h in range(2):
        local(h).wait()


def kblock_scatter(feats, npair, nb):
    groups = npair * nb
    rows = feats.shape[0] // 2
    depth = feats.shape[1] // groups
    size = feats.size * feats.dtype.itemsize
    return pl.pallas_call(
        functools.partial(scatter_kernel, npair, nb),
        out_shape=jax.ShapeDtypeStruct((nb, 2, npair, rows, depth), feats.dtype),
        in_specs=[pl.BlockSpec(memory_space=pltpu.VMEM)],
        out_specs=pl.BlockSpec(memory_space=pltpu.VMEM),
        scratch_shapes=[pltpu.SemaphoreType.DMA((2 * groups,)), pltpu.SemaphoreType.DMA((2 * groups,))],
        compiler_params=pltpu.CompilerParams(collective_id=0, has_side_effects=True),
        cost_estimate=pl.CostEstimate(flops=0, transcendentals=0, bytes_accessed=2 * size),
    )(feats)


def on_device(npair, nb, nv, hidden, norm_gain, head_weight):
    groups = npair * nb
    span = nv // groups
    local_rows, width = hidden.shape[1], hidden.shape[2]
    total_d = width * nv
    lanes = 128
    gain_rows = width // lanes
    gain_block = jnp.zeros((16, lanes), norm_gain.dtype).at[:gain_rows].set(norm_gain.reshape(gain_rows, lanes))
    got, got_gain = vocab_gather_pair(hidden[0], gain_block, nv, 1)
    wide = got.transpose(1, 0, 2).reshape(local_rows, total_d).astype(jnp.float32)
    gain = got_gain[:, :gain_rows, :].reshape(total_d)
    meansq = jnp.sum(wide * wide, axis=1) / total_d
    scaled = wide * lax.rsqrt(meansq + EPS)[:, None] * gain.astype(jnp.float32)[None, :]
    features = scaled.astype(jnp.bfloat16)
    ordered = kblock_scatter(features, npair, nb).reshape(groups * local_rows, total_d // groups)
    half = local_rows // 2
    out_rows = half
    lanes = 128
    me = lax.axis_index("pair")
    half_rows = ordered.shape[0] // 2
    mine = lax.dynamic_slice_in_dim(ordered, me * half_rows, half_rows, axis=0)
    theirs = lax.dynamic_slice_in_dim(ordered, (1 - me) * half_rows, half_rows, axis=0)
    cols = head_weight.shape[1]
    edges = [0, cols // 8, cols]
    pieces = []
    weight = head_weight
    for j in range(len(edges) - 1):
        w = weight[:, edges[j]:edges[j + 1]]
        if j == 0:
            full = jnp.dot(ordered, w, preferred_element_type=jnp.float32)
            full, weight, theirs, mine = lax.optimization_barrier((full, weight, theirs, mine))
            pieces.append(lax.psum_scatter(full, ("pair", "batch"), scatter_dimension=0, tiled=True))
            continue
        sent = jnp.dot(theirs, w, preferred_element_type=jnp.float32)
        kept = jnp.dot(mine, w, preferred_element_type=jnp.float32)
        got_half = lax.ppermute(sent, "pair", [(0, 1), (1, 0)])
        summed = kept + got_half
        summed, weight, theirs, mine = lax.optimization_barrier((summed, weight, theirs, mine))
        pieces.append(lax.psum_scatter(summed, "batch", scatter_dimension=0, tiled=True))
    logits = jnp.concatenate(pieces, axis=1)
    cond = logits[:out_rows]
    uncond = logits[out_rows:]
    guided = GUIDE * cond + (1.0 - GUIDE) * uncond
    peak_c = jnp.max(cond, axis=1)
    peak_g = jnp.max(guided, axis=1)
    local_c = jnp.sum(jnp.exp(cond - peak_c[:, None]), axis=1)
    local_g = jnp.sum(jnp.exp(guided - peak_g[:, None]), axis=1)
    stats = jnp.zeros((8, lanes), jnp.float32).at[:4, :out_rows].set(
        jnp.stack([peak_c, local_c, peak_g, local_g]))
    every = vocab_gather(stats, nv, 2)[:, :4, :out_rows]
    top_c = jnp.max(every[:, 0], axis=0)
    top_g = jnp.max(every[:, 2], axis=0)
    total_c = jnp.sum(every[:, 1] * jnp.exp(every[:, 0] - top_c[None, :]), axis=0)
    total_g = jnp.sum(every[:, 3] * jnp.exp(every[:, 2] - top_g[None, :]), axis=0)
    cond_out = cond - (top_c + jnp.log(total_c))[:, None]
    guided_out = guided - (top_g + jnp.log(total_g))[:, None]
    return (guided_out, cond_out)


def solution(mesh):
    npair, nb, nv = mesh.shape["pair"], mesh.shape["batch"], mesh.shape["vocab"]
    in_specs = (P("pair", "batch", "vocab"), P("vocab"), P(("pair", "batch"), "vocab"))
    out_specs = (P(("pair", "batch"), "vocab"), P(("pair", "batch"), "vocab"))
    return jax.shard_map(
        functools.partial(on_device, npair, nb, nv),
        mesh=mesh, in_specs=in_specs, out_specs=out_specs, check_vma=False,
    )
```

```python
import functools

import jax
import jax.numpy as jnp
from jax import lax
from jax.experimental import pallas as pl
from jax.experimental.pallas import tpu as pltpu
from jax.sharding import PartitionSpec as P

MESH = pl.DeviceIdType.MESH

EPS = 1e-05
GUIDE = 1.5


def STEPS(nv):
    return [(i + 1) // 2 if i % 2 else nv - i // 2 for i in range(1, nv)]


def dispatch_kernel(npair, nb, nv, span, src_ref, out_ref, send_sems, recv_sems):
    beta = lax.axis_index("pair")
    b = lax.axis_index("batch")
    v = lax.axis_index("vocab")
    groups = npair * nb
    mine = beta * nb + b
    q = v // span
    tp = q // nb
    tb = q % nb
    slot = mine * span + v % span
    d = q - mine
    own = 1 - (d * d + groups * groups - 1) // (groups * groups)

    def sources(s):
        bs = s // (nb * span)
        bbs = (s // span) % nb
        sv = mine * span + s % span
        return bs, bbs, sv

    barrier = pltpu.get_barrier_semaphore()
    for w in range(nv):
        @pl.when(jnp.logical_not((tp == beta) & (tb == b) & (v == w)))
        def _():
            pl.semaphore_signal(barrier, inc=1, device_id=(tp, tb, w), device_id_type=MESH)
    for s in range(nv):
        bs, bbs, sv = sources(s)

        @pl.when(jnp.logical_not((bs == beta) & (bbs == b) & (sv == v)))
        def _():
            pl.semaphore_signal(barrier, inc=1, device_id=(bs, bbs, sv), device_id_type=MESH)
    pl.semaphore_wait(barrier, 2 * (nv - own))

    def remote(k):
        return pltpu.make_async_remote_copy(
            src_ref=src_ref,
            dst_ref=out_ref.at[slot],
            send_sem=send_sems.at[k],
            recv_sem=recv_sems.at[slot],
            device_id=(tp, tb, (k + slot) % nv),
            device_id_type=MESH,
        )

    for k in range(nv):
        here = (tp == beta) & (tb == b) & (v == (k + slot) % nv)

        @pl.when(jnp.logical_not(here))
        def _():
            remote(k).start()

        @pl.when(here)
        def _():
            pltpu.make_async_copy(src_ref, out_ref.at[slot], recv_sems.at[slot]).start()

    for k in range(nv):
        here = (tp == beta) & (tb == b) & (v == (k + slot) % nv)

        @pl.when(jnp.logical_not(here))
        def _():
            remote(k).wait_send()

    for s in range(nv):
        bs, bbs, sv = sources(s)
        here = (bs == beta) & (bbs == b) & (sv == v)

        @pl.when(jnp.logical_not(here))
        def _():
            pltpu.make_async_remote_copy(
                src_ref=src_ref,
                dst_ref=out_ref.at[s],
                send_sem=send_sems.at[0],
                recv_sem=recv_sems.at[s],
                device_id=(bs, bbs, sv),
                device_id_type=MESH,
            ).wait_recv()

        @pl.when(here)
        def _():
            pltpu.make_async_copy(src_ref, out_ref.at[s], recv_sems.at[s]).wait()


def dispatch(block, npair, nb, nv):
    span = nv // (npair * nb)
    size = block.size * block.dtype.itemsize
    return pl.pallas_call(
        functools.partial(dispatch_kernel, npair, nb, nv, span),
        out_shape=jax.ShapeDtypeStruct((nv,) + block.shape, block.dtype),
        in_specs=[pl.BlockSpec(memory_space=pltpu.VMEM)],
        out_specs=pl.BlockSpec(memory_space=pltpu.VMEM),
        scratch_shapes=[pltpu.SemaphoreType.DMA((nv,)), pltpu.SemaphoreType.DMA((nv,))],
        compiler_params=pltpu.CompilerParams(collective_id=0, has_side_effects=True),
        cost_estimate=pl.CostEstimate(flops=0, transcendentals=0, bytes_accessed=2 * nv * size),
    )(block)


def gather_kernel(nv, src_ref, out_ref, send_sems, recv_sems):
    beta = lax.axis_index("pair")
    b = lax.axis_index("batch")
    v = lax.axis_index("vocab")
    barrier = pltpu.get_barrier_semaphore()
    for k in STEPS(nv):
        pl.semaphore_signal(barrier, inc=1, device_id=(beta, b, (v + k) % nv), device_id_type=MESH)
    pl.semaphore_wait(barrier, nv - 1)

    def remote(w, s):
        return pltpu.make_async_remote_copy(
            src_ref=src_ref,
            dst_ref=out_ref.at[s],
            send_sem=send_sems.at[w],
            recv_sem=recv_sems.at[s],
            device_id=(beta, b, w),
            device_id_type=MESH,
        )

    for k in STEPS(nv):
        remote((v + k) % nv, v).start()

    pltpu.make_async_copy(src_ref, out_ref.at[v], recv_sems.at[v]).start()
    for k in STEPS(nv):
        remote((v + k) % nv, v).wait_send()
    for k in STEPS(nv):
        s = (v + k) % nv
        remote(s, s).wait_recv()
    pltpu.make_async_copy(src_ref, out_ref.at[v], recv_sems.at[v]).wait()


def vocab_gather(block, nv, cid):
    size = block.size * block.dtype.itemsize
    return pl.pallas_call(
        functools.partial(gather_kernel, nv),
        out_shape=jax.ShapeDtypeStruct((nv,) + block.shape, block.dtype),
        in_specs=[pl.BlockSpec(memory_space=pltpu.VMEM)],
        out_specs=pl.BlockSpec(memory_space=pltpu.VMEM),
        scratch_shapes=[pltpu.SemaphoreType.DMA((nv,)), pltpu.SemaphoreType.DMA((nv,))],
        compiler_params=pltpu.CompilerParams(collective_id=cid, has_side_effects=True),
        cost_estimate=pl.CostEstimate(flops=0, transcendentals=0, bytes_accessed=2 * nv * size),
    )(block)


def gather_pair_kernel(nv, h_ref, g_ref, ho_ref, go_ref, hs, hr, gs, gr):
    beta = lax.axis_index("pair")
    b = lax.axis_index("batch")
    v = lax.axis_index("vocab")
    barrier = pltpu.get_barrier_semaphore()
    for k in STEPS(nv):
        pl.semaphore_signal(barrier, inc=1, device_id=(beta, b, (v + k) % nv), device_id_type=MESH)
    pl.semaphore_wait(barrier, nv - 1)

    def remote(src, dst, send, recv, w, s):
        return pltpu.make_async_remote_copy(
            src_ref=src,
            dst_ref=dst.at[s],
            send_sem=send.at[w],
            recv_sem=recv.at[s],
            device_id=(beta, b, w),
            device_id_type=MESH,
        )

    pairs = ((h_ref, ho_ref, hs, hr), (g_ref, go_ref, gs, gr))
    for k in STEPS(nv):
        for src, dst, send, recv in pairs:
            remote(src, dst, send, recv, (v + k) % nv, v).start()
    for src, dst, send, recv in pairs:
        pltpu.make_async_copy(src, dst.at[v], recv.at[v]).start()
    for k in STEPS(nv):
        for src, dst, send, recv in pairs:
            remote(src, dst, send, recv, (v + k) % nv, v).wait_send()
    for k in STEPS(nv):
        s = (v + k) % nv
        for src, dst, send, recv in pairs:
            remote(src, dst, send, recv, s, s).wait_recv()
    for src, dst, send, recv in pairs:
        pltpu.make_async_copy(src, dst.at[v], recv.at[v]).wait()


def vocab_gather_pair(rows, gain, nv, cid):
    size = rows.size * rows.dtype.itemsize + gain.size * gain.dtype.itemsize
    sems = [pltpu.SemaphoreType.DMA((nv,))] * 4
    return pl.pallas_call(
        functools.partial(gather_pair_kernel, nv),
        out_shape=(jax.ShapeDtypeStruct((nv,) + rows.shape, rows.dtype),
                   jax.ShapeDtypeStruct((nv,) + gain.shape, gain.dtype)),
        in_specs=[pl.BlockSpec(memory_space=pltpu.VMEM)] * 2,
        out_specs=(pl.BlockSpec(memory_space=pltpu.VMEM), pl.BlockSpec(memory_space=pltpu.VMEM)),
        scratch_shapes=sems,
        compiler_params=pltpu.CompilerParams(collective_id=cid, has_side_effects=True),
        cost_estimate=pl.CostEstimate(flops=0, transcendentals=0, bytes_accessed=2 * nv * size),
    )(rows, gain)


def scatter_kernel(npair, nb, src_ref, out_ref, send_sems, recv_sems):
    beta = lax.axis_index("pair")
    b = lax.axis_index("batch")
    v = lax.axis_index("vocab")
    groups = npair * nb
    me = beta * nb + b
    rows = out_ref.shape[3]
    depth = out_ref.shape[4]
    barrier = pltpu.get_barrier_semaphore()
    for k in range(1, groups):
        t = (me + k) % groups
        pl.semaphore_signal(barrier, inc=1, device_id=(t // nb, t % nb, v), device_id_type=MESH)
    pl.semaphore_wait(barrier, groups - 1)

    def piece(t, h):
        return src_ref.at[pl.ds(h * rows, rows), pl.ds(pl.multiple_of(t * depth, depth), depth)]

    def remote(k, h):
        t = (me + k) % groups
        return pltpu.make_async_remote_copy(
            src_ref=piece(t, h),
            dst_ref=out_ref.at[b, h, beta],
            send_sem=send_sems.at[k * 2 + h],
            recv_sem=recv_sems.at[(b * 2 + h) * npair + beta],
            device_id=(t // nb, t % nb, v),
            device_id_type=MESH,
        )

    def local(h):
        return pltpu.make_async_copy(
            piece(me, h), out_ref.at[b, h, beta], recv_sems.at[(b * 2 + h) * npair + beta])

    for k in range(1, groups):
        for h in range(2):
            remote(k, h).start()
    for h in range(2):
        local(h).start()
    for k in range(1, groups):
        for h in range(2):
            remote(k, h).wait_send()
    for k in range(1, groups):
        s = (me + k) % groups
        sp, sb = s // nb, s % nb
        for h in range(2):
            pltpu.make_async_remote_copy(
                src_ref=piece(me, h),
                dst_ref=out_ref.at[sb, h, sp],
                send_sem=send_sems.at[0],
                recv_sem=recv_sems.at[(sb * 2 + h) * npair + sp],
                device_id=(sp, sb, v),
                device_id_type=MESH,
            ).wait_recv()
    for h in range(2):
        local(h).wait()


def kblock_scatter(feats, npair, nb):
    groups = npair * nb
    rows = feats.shape[0] // 2
    depth = feats.shape[1] // groups
    size = feats.size * feats.dtype.itemsize
    return pl.pallas_call(
        functools.partial(scatter_kernel, npair, nb),
        out_shape=jax.ShapeDtypeStruct((nb, 2, npair, rows, depth), feats.dtype),
        in_specs=[pl.BlockSpec(memory_space=pltpu.VMEM)],
        out_specs=pl.BlockSpec(memory_space=pltpu.VMEM),
        scratch_shapes=[pltpu.SemaphoreType.DMA((2 * groups,)), pltpu.SemaphoreType.DMA((2 * groups,))],
        compiler_params=pltpu.CompilerParams(collective_id=0, has_side_effects=True),
        cost_estimate=pl.CostEstimate(flops=0, transcendentals=0, bytes_accessed=2 * size),
    )(feats)


def on_device(npair, nb, nv, hidden, norm_gain, head_weight):
    groups = npair * nb
    span = nv // groups
    local_rows, width = hidden.shape[1], hidden.shape[2]
    total_d = width * nv
    lanes = 128
    gain_rows = width // lanes
    gain_block = jnp.zeros((16, lanes), norm_gain.dtype).at[:gain_rows].set(norm_gain.reshape(gain_rows, lanes))
    got, got_gain = vocab_gather_pair(hidden[0], gain_block, nv, 1)
    wide = got.transpose(1, 0, 2).reshape(local_rows, total_d).astype(jnp.float32)
    gain = got_gain[:, :gain_rows, :].reshape(total_d)
    meansq = jnp.sum(wide * wide, axis=1) / total_d
    scaled = wide * lax.rsqrt(meansq + EPS)[:, None] * gain.astype(jnp.float32)[None, :]
    features = scaled.astype(jnp.bfloat16)
    ordered = kblock_scatter(features, npair, nb).reshape(groups * local_rows, total_d // groups)
    half = local_rows // 2
    out_rows = half
    lanes = 128
    me = lax.axis_index("pair")
    half_rows = ordered.shape[0] // 2
    mine = lax.dynamic_slice_in_dim(ordered, me * half_rows, half_rows, axis=0)
    theirs = lax.dynamic_slice_in_dim(ordered, (1 - me) * half_rows, half_rows, axis=0)
    cols = head_weight.shape[1]
    edges = [0, cols // 8, cols]
    pieces = []
    weight = head_weight
    for j in range(len(edges) - 1):
        w = weight[:, edges[j]:edges[j + 1]]
        sent = jnp.dot(theirs, w, preferred_element_type=jnp.float32)
        kept = jnp.dot(mine, w, preferred_element_type=jnp.float32)
        got_half = lax.ppermute(sent, "pair", [(0, 1), (1, 0)])
        summed = kept + got_half
        summed, weight, theirs, mine = lax.optimization_barrier((summed, weight, theirs, mine))
        pieces.append(lax.psum_scatter(summed, "batch", scatter_dimension=0, tiled=True))
    logits = jnp.concatenate(pieces, axis=1)
    cond = logits[:out_rows]
    uncond = logits[out_rows:]
    guided = GUIDE * cond + (1.0 - GUIDE) * uncond
    peak_c = jnp.max(cond, axis=1)
    peak_g = jnp.max(guided, axis=1)
    local_c = jnp.sum(jnp.exp(cond - peak_c[:, None]), axis=1)
    local_g = jnp.sum(jnp.exp(guided - peak_g[:, None]), axis=1)
    stats = jnp.zeros((8, lanes), jnp.float32).at[:4, :out_rows].set(
        jnp.stack([peak_c, local_c, peak_g, local_g]))
    every = vocab_gather(stats, nv, 2)[:, :4, :out_rows]
    top_c = jnp.max(every[:, 0], axis=0)
    top_g = jnp.max(every[:, 2], axis=0)
    total_c = jnp.sum(every[:, 1] * jnp.exp(every[:, 0] - top_c[None, :]), axis=0)
    total_g = jnp.sum(every[:, 3] * jnp.exp(every[:, 2] - top_g[None, :]), axis=0)
    cond_out = cond - (top_c + jnp.log(total_c))[:, None]
    guided_out = guided - (top_g + jnp.log(total_g))[:, None]
    return (guided_out, cond_out)


def solution(mesh):
    npair, nb, nv = mesh.shape["pair"], mesh.shape["batch"], mesh.shape["vocab"]
    in_specs = (P("pair", "batch", "vocab"), P("vocab"), P(("pair", "batch"), "vocab"))
    out_specs = (P(("pair", "batch"), "vocab"), P(("pair", "batch"), "vocab"))
    return jax.shard_map(
        functools.partial(on_device, npair, nb, nv),
        mesh=mesh, in_specs=in_specs, out_specs=out_specs, check_vma=False,
    )
```

```python
import functools

import jax
import jax.numpy as jnp
from jax import lax
from jax.experimental import pallas as pl
from jax.experimental.pallas import tpu as pltpu
from jax.sharding import PartitionSpec as P

MESH = pl.DeviceIdType.MESH

EPS = 1e-05
GUIDE = 1.5


def STEPS(nv):
    return [(i + 1) // 2 if i % 2 else nv - i // 2 for i in range(1, nv)]


def dispatch_kernel(npair, nb, nv, span, src_ref, out_ref, send_sems, recv_sems):
    beta = lax.axis_index("pair")
    b = lax.axis_index("batch")
    v = lax.axis_index("vocab")
    groups = npair * nb
    mine = beta * nb + b
    q = v // span
    tp = q // nb
    tb = q % nb
    slot = mine * span + v % span
    d = q - mine
    own = 1 - (d * d + groups * groups - 1) // (groups * groups)

    def sources(s):
        bs = s // (nb * span)
        bbs = (s // span) % nb
        sv = mine * span + s % span
        return bs, bbs, sv

    barrier = pltpu.get_barrier_semaphore()
    for w in range(nv):
        @pl.when(jnp.logical_not((tp == beta) & (tb == b) & (v == w)))
        def _():
            pl.semaphore_signal(barrier, inc=1, device_id=(tp, tb, w), device_id_type=MESH)
    for s in range(nv):
        bs, bbs, sv = sources(s)

        @pl.when(jnp.logical_not((bs == beta) & (bbs == b) & (sv == v)))
        def _():
            pl.semaphore_signal(barrier, inc=1, device_id=(bs, bbs, sv), device_id_type=MESH)
    pl.semaphore_wait(barrier, 2 * (nv - own))

    def remote(k):
        return pltpu.make_async_remote_copy(
            src_ref=src_ref,
            dst_ref=out_ref.at[slot],
            send_sem=send_sems.at[k],
            recv_sem=recv_sems.at[slot],
            device_id=(tp, tb, (k + slot) % nv),
            device_id_type=MESH,
        )

    for k in range(nv):
        here = (tp == beta) & (tb == b) & (v == (k + slot) % nv)

        @pl.when(jnp.logical_not(here))
        def _():
            remote(k).start()

        @pl.when(here)
        def _():
            pltpu.make_async_copy(src_ref, out_ref.at[slot], recv_sems.at[slot]).start()

    for k in range(nv):
        here = (tp == beta) & (tb == b) & (v == (k + slot) % nv)

        @pl.when(jnp.logical_not(here))
        def _():
            remote(k).wait_send()

    for s in range(nv):
        bs, bbs, sv = sources(s)
        here = (bs == beta) & (bbs == b) & (sv == v)

        @pl.when(jnp.logical_not(here))
        def _():
            pltpu.make_async_remote_copy(
                src_ref=src_ref,
                dst_ref=out_ref.at[s],
                send_sem=send_sems.at[0],
                recv_sem=recv_sems.at[s],
                device_id=(bs, bbs, sv),
                device_id_type=MESH,
            ).wait_recv()

        @pl.when(here)
        def _():
            pltpu.make_async_copy(src_ref, out_ref.at[s], recv_sems.at[s]).wait()


def dispatch(block, npair, nb, nv):
    span = nv // (npair * nb)
    size = block.size * block.dtype.itemsize
    return pl.pallas_call(
        functools.partial(dispatch_kernel, npair, nb, nv, span),
        out_shape=jax.ShapeDtypeStruct((nv,) + block.shape, block.dtype),
        in_specs=[pl.BlockSpec(memory_space=pltpu.VMEM)],
        out_specs=pl.BlockSpec(memory_space=pltpu.VMEM),
        scratch_shapes=[pltpu.SemaphoreType.DMA((nv,)), pltpu.SemaphoreType.DMA((nv,))],
        compiler_params=pltpu.CompilerParams(collective_id=0, has_side_effects=True),
        cost_estimate=pl.CostEstimate(flops=0, transcendentals=0, bytes_accessed=2 * nv * size),
    )(block)


def gather_kernel(nv, src_ref, out_ref, send_sems, recv_sems):
    beta = lax.axis_index("pair")
    b = lax.axis_index("batch")
    v = lax.axis_index("vocab")
    barrier = pltpu.get_barrier_semaphore()
    for k in STEPS(nv):
        pl.semaphore_signal(barrier, inc=1, device_id=(beta, b, (v + k) % nv), device_id_type=MESH)
    pl.semaphore_wait(barrier, nv - 1)

    def remote(w, s):
        return pltpu.make_async_remote_copy(
            src_ref=src_ref,
            dst_ref=out_ref.at[s],
            send_sem=send_sems.at[w],
            recv_sem=recv_sems.at[s],
            device_id=(beta, b, w),
            device_id_type=MESH,
        )

    for k in STEPS(nv):
        remote((v + k) % nv, v).start()

    pltpu.make_async_copy(src_ref, out_ref.at[v], recv_sems.at[v]).start()
    for k in STEPS(nv):
        remote((v + k) % nv, v).wait_send()
    for k in STEPS(nv):
        s = (v + k) % nv
        remote(s, s).wait_recv()
    pltpu.make_async_copy(src_ref, out_ref.at[v], recv_sems.at[v]).wait()


def vocab_gather(block, nv, cid):
    size = block.size * block.dtype.itemsize
    return pl.pallas_call(
        functools.partial(gather_kernel, nv),
        out_shape=jax.ShapeDtypeStruct((nv,) + block.shape, block.dtype),
        in_specs=[pl.BlockSpec(memory_space=pltpu.VMEM)],
        out_specs=pl.BlockSpec(memory_space=pltpu.VMEM),
        scratch_shapes=[pltpu.SemaphoreType.DMA((nv,)), pltpu.SemaphoreType.DMA((nv,))],
        compiler_params=pltpu.CompilerParams(collective_id=cid, has_side_effects=True),
        cost_estimate=pl.CostEstimate(flops=0, transcendentals=0, bytes_accessed=2 * nv * size),
    )(block)


def gather_pair_kernel(nv, h_ref, g_ref, ho_ref, go_ref, hs, hr, gs, gr):
    beta = lax.axis_index("pair")
    b = lax.axis_index("batch")
    v = lax.axis_index("vocab")
    barrier = pltpu.get_barrier_semaphore()
    for k in STEPS(nv):
        pl.semaphore_signal(barrier, inc=1, device_id=(beta, b, (v + k) % nv), device_id_type=MESH)
    pl.semaphore_wait(barrier, nv - 1)

    def remote(src, dst, send, recv, w, s):
        return pltpu.make_async_remote_copy(
            src_ref=src,
            dst_ref=dst.at[s],
            send_sem=send.at[w],
            recv_sem=recv.at[s],
            device_id=(beta, b, w),
            device_id_type=MESH,
        )

    pairs = ((h_ref, ho_ref, hs, hr), (g_ref, go_ref, gs, gr))
    for k in STEPS(nv):
        for src, dst, send, recv in pairs:
            remote(src, dst, send, recv, (v + k) % nv, v).start()
    for src, dst, send, recv in pairs:
        pltpu.make_async_copy(src, dst.at[v], recv.at[v]).start()
    for k in STEPS(nv):
        for src, dst, send, recv in pairs:
            remote(src, dst, send, recv, (v + k) % nv, v).wait_send()
    for k in STEPS(nv):
        s = (v + k) % nv
        for src, dst, send, recv in pairs:
            remote(src, dst, send, recv, s, s).wait_recv()
    for src, dst, send, recv in pairs:
        pltpu.make_async_copy(src, dst.at[v], recv.at[v]).wait()


def vocab_gather_pair(rows, gain, nv, cid):
    size = rows.size * rows.dtype.itemsize + gain.size * gain.dtype.itemsize
    sems = [pltpu.SemaphoreType.DMA((nv,))] * 4
    return pl.pallas_call(
        functools.partial(gather_pair_kernel, nv),
        out_shape=(jax.ShapeDtypeStruct((nv,) + rows.shape, rows.dtype),
                   jax.ShapeDtypeStruct((nv,) + gain.shape, gain.dtype)),
        in_specs=[pl.BlockSpec(memory_space=pltpu.VMEM)] * 2,
        out_specs=(pl.BlockSpec(memory_space=pltpu.VMEM), pl.BlockSpec(memory_space=pltpu.VMEM)),
        scratch_shapes=sems,
        compiler_params=pltpu.CompilerParams(collective_id=cid, has_side_effects=True),
        cost_estimate=pl.CostEstimate(flops=0, transcendentals=0, bytes_accessed=2 * nv * size),
    )(rows, gain)


def scatter_kernel(npair, nb, src_ref, out_ref, send_sems, recv_sems):
    beta = lax.axis_index("pair")
    b = lax.axis_index("batch")
    v = lax.axis_index("vocab")
    groups = npair * nb
    me = beta * nb + b
    rows = out_ref.shape[3]
    depth = out_ref.shape[4]
    barrier = pltpu.get_barrier_semaphore()
    for k in STEPS(groups):
        t = (me + k) % groups
        pl.semaphore_signal(barrier, inc=1, device_id=(t // nb, t % nb, v), device_id_type=MESH)
    pl.semaphore_wait(barrier, groups - 1)

    def piece(t, h):
        return src_ref.at[pl.ds(h * rows, rows), pl.ds(pl.multiple_of(t * depth, depth), depth)]

    def remote(k, h):
        t = (me + k) % groups
        return pltpu.make_async_remote_copy(
            src_ref=piece(t, h),
            dst_ref=out_ref.at[b, h, beta],
            send_sem=send_sems.at[k * 2 + h],
            recv_sem=recv_sems.at[(b * 2 + h) * npair + beta],
            device_id=(t // nb, t % nb, v),
            device_id_type=MESH,
        )

    def local(h):
        return pltpu.make_async_copy(
            piece(me, h), out_ref.at[b, h, beta], recv_sems.at[(b * 2 + h) * npair + beta])

    for k in STEPS(groups):
        for h in range(2):
            remote(k, h).start()
    for h in range(2):
        local(h).start()
    for k in STEPS(groups):
        for h in range(2):
            remote(k, h).wait_send()
    for k in STEPS(groups):
        s = (me + k) % groups
        sp, sb = s // nb, s % nb
        for h in range(2):
            pltpu.make_async_remote_copy(
                src_ref=piece(me, h),
                dst_ref=out_ref.at[sb, h, sp],
                send_sem=send_sems.at[0],
                recv_sem=recv_sems.at[(sb * 2 + h) * npair + sp],
                device_id=(sp, sb, v),
                device_id_type=MESH,
            ).wait_recv()
    for h in range(2):
        local(h).wait()


def kblock_scatter(feats, npair, nb):
    groups = npair * nb
    rows = feats.shape[0] // 2
    depth = feats.shape[1] // groups
    size = feats.size * feats.dtype.itemsize
    return pl.pallas_call(
        functools.partial(scatter_kernel, npair, nb),
        out_shape=jax.ShapeDtypeStruct((nb, 2, npair, rows, depth), feats.dtype),
        in_specs=[pl.BlockSpec(memory_space=pltpu.VMEM)],
        out_specs=pl.BlockSpec(memory_space=pltpu.VMEM),
        scratch_shapes=[pltpu.SemaphoreType.DMA((2 * groups,)), pltpu.SemaphoreType.DMA((2 * groups,))],
        compiler_params=pltpu.CompilerParams(collective_id=0, has_side_effects=True),
        cost_estimate=pl.CostEstimate(flops=0, transcendentals=0, bytes_accessed=2 * size),
    )(feats)


def on_device(npair, nb, nv, hidden, norm_gain, head_weight):
    groups = npair * nb
    span = nv // groups
    local_rows, width = hidden.shape[1], hidden.shape[2]
    total_d = width * nv
    lanes = 128
    gain_rows = width // lanes
    gain_block = jnp.zeros((16, lanes), norm_gain.dtype).at[:gain_rows].set(norm_gain.reshape(gain_rows, lanes))
    got, got_gain = vocab_gather_pair(hidden[0], gain_block, nv, 1)
    wide = got.transpose(1, 0, 2).reshape(local_rows, total_d).astype(jnp.float32)
    gain = got_gain[:, :gain_rows, :].reshape(total_d)
    meansq = jnp.sum(wide * wide, axis=1) / total_d
    scaled = wide * lax.rsqrt(meansq + EPS)[:, None] * gain.astype(jnp.float32)[None, :]
    features = scaled.astype(jnp.bfloat16)
    ordered = kblock_scatter(features, npair, nb).reshape(groups * local_rows, total_d // groups)
    half = local_rows // 2
    out_rows = half
    lanes = 128
    me = lax.axis_index("pair")
    half_rows = ordered.shape[0] // 2
    mine = lax.dynamic_slice_in_dim(ordered, me * half_rows, half_rows, axis=0)
    theirs = lax.dynamic_slice_in_dim(ordered, (1 - me) * half_rows, half_rows, axis=0)
    cols = head_weight.shape[1]
    edges = [0, cols // 8, cols]
    pieces = []
    weight = head_weight
    for j in range(len(edges) - 1):
        w = weight[:, edges[j]:edges[j + 1]]
        sent = jnp.dot(theirs, w, preferred_element_type=jnp.float32)
        kept = jnp.dot(mine, w, preferred_element_type=jnp.float32)
        got_half = lax.ppermute(sent, "pair", [(0, 1), (1, 0)])
        summed = kept + got_half
        summed, weight, theirs, mine = lax.optimization_barrier((summed, weight, theirs, mine))
        pieces.append(lax.psum_scatter(summed, "batch", scatter_dimension=0, tiled=True))
    logits = jnp.concatenate(pieces, axis=1)
    cond = logits[:out_rows]
    uncond = logits[out_rows:]
    guided = GUIDE * cond + (1.0 - GUIDE) * uncond
    peak_c = jnp.max(cond, axis=1)
    peak_g = jnp.max(guided, axis=1)
    local_c = jnp.sum(jnp.exp(cond - peak_c[:, None]), axis=1)
    local_g = jnp.sum(jnp.exp(guided - peak_g[:, None]), axis=1)
    stats = jnp.zeros((8, lanes), jnp.float32).at[:4, :out_rows].set(
        jnp.stack([peak_c, local_c, peak_g, local_g]))
    every = vocab_gather(stats, nv, 2)[:, :4, :out_rows]
    top_c = jnp.max(every[:, 0], axis=0)
    top_g = jnp.max(every[:, 2], axis=0)
    total_c = jnp.sum(every[:, 1] * jnp.exp(every[:, 0] - top_c[None, :]), axis=0)
    total_g = jnp.sum(every[:, 3] * jnp.exp(every[:, 2] - top_g[None, :]), axis=0)
    cond_out = cond - (top_c + jnp.log(total_c))[:, None]
    guided_out = guided - (top_g + jnp.log(total_g))[:, None]
    return (guided_out, cond_out)


def solution(mesh):
    npair, nb, nv = mesh.shape["pair"], mesh.shape["batch"], mesh.shape["vocab"]
    in_specs = (P("pair", "batch", "vocab"), P("vocab"), P(("pair", "batch"), "vocab"))
    out_specs = (P(("pair", "batch"), "vocab"), P(("pair", "batch"), "vocab"))
    return jax.shard_map(
        functools.partial(on_device, npair, nb, nv),
        mesh=mesh, in_specs=in_specs, out_specs=out_specs, check_vma=False,
    )
```
